128 devices in a mesh: row: 16 (over z, y_hi, core), col: 8 (over y_lo, x).
Axes of the slice: x: 4, y: 4 (y_hi: 2, y_lo: 2; y = y_hi * 2 + y_lo), z: 4, core: 2. Of those that a mesh axis runs over, the one named last changes fastest.
Arguments:
- features: bfloat16 [65536, 256], P(('row', 'col')), may hold values from -6 to 6
- blocks: bfloat16 [16, 8, 192, 64, 64], P('row', 'col'), may hold values from -0.3125 to 0.3125
- block_rows: int32 [16, 8, 192], P('row', 'col'), may hold values from 0 to 63
- block_cols: int32 [16, 8, 192], P('row', 'col'), may hold values from 0 to 127
- block_count: int32 [16, 8], P('row', 'col'), may hold values from 1 to 192, as said below
- w_in: bfloat16 [512, 1024], replicated, may hold values from -0.25 to 0.25
- w_mid: bfloat16 [1024, 1024], replicated, may hold values from -0.1875 to 0.1875
- w_out: bfloat16 [1024, 256], replicated, may hold values from -0.1875 to 0.1875
- cotangent: bfloat16 [65536, 256], P(('row', 'col')), may hold values from -6 to 6
Outputs:
- updated: bfloat16 [65536, 256], P(('row', 'col'))
- grad_nodes: bfloat16 [65536, 256], P(('row', 'col'))
- grad_in: float32 [512, 1024], replicated
- grad_mid: float32 [1024, 1024], replicated
- grad_out: float32 [1024, 256], replicated
The draws below stay inside these ranges and needn't reach their ends.
Inputs may be any that keep to these rules, and one draw needn't show every extreme that they name: Only slots below a cell's block_count are used; the busiest cell uses all 192 slots.
All inputs are finite; a program needn't handle non-finite values.
Results may differ from the reference program's by a relative error of at most 0.015.
Values may be sent and summed in bfloat16 or wider, within the bound.
No kernel may reach another device: no remote copies, remote signals or barrier semaphores. Data moves between devices by JAX's collectives and lax.ppermute only.
A program may use at most 128 MiB of HBM per device.

```python
import math
import jax
import jax.numpy as jnp
from jax import lax

F = 256
HID = 1024
BLOCK = 64
NODE_DEV = 512
ROW_GROUPS = 16
COL_GROUPS = 8
NODES = 65536
GROUP_ROWS = 4096
GROUP_COLS = 8192
ROW_BLOCKS = 64
COL_BLOCKS = 128
SLOTS = 192


def draw_block_rows(key, part):
    return jax.random.randint(jax.random.fold_in(key, 11), (ROW_GROUPS, COL_GROUPS, SLOTS), 0, ROW_BLOCKS).astype(jnp.int32)


def draw_block_cols(key, part):
    return jax.random.randint(jax.random.fold_in(key, 23), (ROW_GROUPS, COL_GROUPS, SLOTS), 0, COL_BLOCKS).astype(jnp.int32)


def draw_block_count(key, part):
    first = jax.random.randint(jax.random.fold_in(key, 31), (ROW_GROUPS, COL_GROUPS), 1, SLOTS + 1)
    second = jax.random.randint(jax.random.fold_in(key, 37), (ROW_GROUPS, COL_GROUPS), 1, SLOTS + 1)
    base = jnp.maximum(first * second // SLOTS, 1)
    chosen = jax.random.randint(jax.random.fold_in(key, 41), (), 0, ROW_GROUPS * COL_GROUPS)
    cells = jnp.arange(ROW_GROUPS * COL_GROUPS, dtype=jnp.int32).reshape(ROW_GROUPS, COL_GROUPS)
    return jnp.where(cells == chosen, SLOTS, base).astype(jnp.int32)


def shard_levels(key, dims, split, smallest, high):
    gain, own = 1.0, jax.random.fold_in(key, 6)
    for dim, parts in split:
        draws = jnp.exp(jax.random.uniform(jax.random.fold_in(own, dim), (parts,), jnp.float32, smallest / len(split), high / len(split)))
        gain = gain * jnp.repeat(draws, dims[dim] // parts).reshape([-1 if axis == dim else 1 for axis in range(len(dims))])
    return gain


def noise(stream_key, shape, width, bound, split=(), kind=jnp.bfloat16):
    array = width * jax.random.normal(stream_key, shape, jnp.float32)
    if split:
        array = array * shard_levels(stream_key, shape, split, -0.22, 0.18)
    return jnp.clip(array, -bound, bound).astype(kind)


def setup_inputs(seed: int = 0) -> dict:
    splits = jax.random.split(jax.random.key(seed), 10)
    features = noise(splits[0], (NODES, F), 1.0, 6.0, ((0, 128),))
    blocks = noise(splits[1], (ROW_GROUPS, COL_GROUPS, SLOTS, BLOCK, BLOCK), (6 * BLOCK) ** -0.5, 0.3125, ((0, 16), (1, 8)))
    block_rows = draw_block_rows(jax.random.fold_in(splits[9], 71), 0)
    block_cols = draw_block_cols(jax.random.fold_in(splits[9], 71), 0)
    block_count = draw_block_count(jax.random.fold_in(splits[9], 71), 0)
    w_in = noise(splits[5], (2 * F, HID), (2 * F) ** -0.5, 0.25)
    w_mid = noise(splits[6], (HID, HID), HID ** -0.5, 0.1875)
    w_out = noise(splits[7], (HID, F), HID ** -0.5, 0.1875)
    cotangent = noise(splits[8], (NODES, F), 1.0, 6.0, ((0, 128),))
    return dict(features=features, blocks=blocks, block_rows=block_rows, block_cols=block_cols, block_count=block_count, w_in=w_in, w_mid=w_mid, w_out=w_out, cotangent=cotangent)


def silu_grad(value):
    sig = jax.nn.sigmoid(value)
    return sig * (1.0 + value * (1.0 - sig))

def cell_term(cell_blocks, gather_idx, add_idx, count, source, n_dst, transposed):
    picked = source[gather_idx]
    form = 'sba,sbf->saf' if transposed else 'sab,sbf->saf'
    prod = jnp.einsum(form, cell_blocks.astype(jnp.float32), picked.astype(jnp.float32))
    live = (jnp.arange(SLOTS, dtype=jnp.int32) < count).astype(jnp.float32)
    prod = prod * live[:, None, None]
    total = jnp.zeros((n_dst, BLOCK, F), jnp.float32).at[add_idx].add(prod)
    return total.reshape(n_dst * BLOCK, F)

def reference(features, blocks, block_rows, block_cols, block_count, w_in, w_mid, w_out, cotangent):
    grouped = features.reshape(ROW_GROUPS, COL_GROUPS, NODE_DEV, F)

    def row_group(g):

        def add_cell(total, c):
            source = lax.dynamic_index_in_dim(grouped, c, 1, keepdims=False).reshape(COL_BLOCKS, BLOCK, F)
            term = cell_term(blocks[g, c], block_cols[g, c], block_rows[g, c], block_count[g, c], source, ROW_BLOCKS, False)
            return (total + lax.optimization_barrier(term.astype(jnp.bfloat16)).astype(jnp.float32), None)
        total, _ = lax.scan(add_cell, jnp.zeros((GROUP_ROWS, F), jnp.float32), jnp.arange(COL_GROUPS, dtype=jnp.int32))
        return total.astype(jnp.bfloat16)
    aggregated = lax.map(row_group, jnp.arange(ROW_GROUPS, dtype=jnp.int32)).reshape(NODES, F)
    joined = jnp.concatenate([features, aggregated], axis=1)
    pre_one = jnp.dot(joined, w_in, preferred_element_type=jnp.float32)
    act_one = jax.nn.silu(pre_one).astype(jnp.bfloat16)
    pre_two = jnp.dot(act_one, w_mid, preferred_element_type=jnp.float32)
    act_two = jax.nn.silu(pre_two).astype(jnp.bfloat16)
    updated = (features.astype(jnp.float32) + jnp.dot(act_two, w_out, preferred_element_type=jnp.float32)).astype(jnp.bfloat16)
    ratio = 1.0 / math.sqrt(NODES)
    grad_out = jnp.dot(act_two.T, cotangent, preferred_element_type=jnp.float32) * ratio
    grad_pre_two = (jnp.dot(cotangent, w_out.T, preferred_element_type=jnp.float32) * silu_grad(pre_two)).astype(jnp.bfloat16)
    grad_mid = jnp.dot(act_one.T, grad_pre_two, preferred_element_type=jnp.float32) * ratio
    grad_pre_one = (jnp.dot(grad_pre_two, w_mid.T, preferred_element_type=jnp.float32) * silu_grad(pre_one)).astype(jnp.bfloat16)
    grad_in = jnp.dot(joined.T, grad_pre_one, preferred_element_type=jnp.float32) * ratio
    grad_joined = jnp.dot(grad_pre_one, w_in.T, preferred_element_type=jnp.float32)
    direct = cotangent.astype(jnp.float32) + grad_joined[:, :F]
    grad_agg = grad_joined[:, F:].astype(jnp.bfloat16)
    row_grads = grad_agg.reshape(ROW_GROUPS, ROW_BLOCKS, BLOCK, F)

    def col_group(c):

        def add_cell(total, g):
            source = lax.dynamic_index_in_dim(row_grads, g, 0, keepdims=False)
            term = cell_term(blocks[g, c], block_rows[g, c], block_cols[g, c], block_count[g, c], source, COL_BLOCKS, True)
            return (total + lax.optimization_barrier(term.astype(jnp.bfloat16)).astype(jnp.float32), None)
        total, _ = lax.scan(add_cell, jnp.zeros((GROUP_COLS, F), jnp.float32), jnp.arange(ROW_GROUPS, dtype=jnp.int32))
        return total
    sums = lax.map(col_group, jnp.arange(COL_GROUPS, dtype=jnp.int32))
    relaid = sums.reshape(COL_GROUPS, ROW_GROUPS, NODE_DEV, F).transpose(1, 0, 2, 3).reshape(NODES, F)
    grad_nodes = (direct + relaid).astype(jnp.bfloat16)
    return (updated, grad_nodes, grad_in, grad_mid, grad_out)
```

```python
import functools
import math

import jax
import jax.numpy as jnp
from jax import lax
from jax.experimental import pallas as pl
from jax.experimental.pallas import tpu as pltpu
from jax.sharding import Mesh, PartitionSpec as P

BF = jnp.bfloat16
F32 = jnp.float32
ROW = ("z", "yh", "core")
COL = ("yl", "x")
SLOTS = 192
SIDE = 64
CHUNK = 32
UNROLL = 8
VMEM_LIMIT = 60 * 1024 * 1024


def silu_grad(value):
    sig = jax.nn.sigmoid(value)
    return sig * (1.0 + value * (1.0 - sig))


def cells_kernel(transposed, off_ref, cnt_ref, blk0, blk1, *rest):
    pieces = rest[:8]
    out_ref, src, held, acc, blk_sem, src_sem = rest[8:]
    n_chunks = SLOTS // CHUNK
    blocks = (blk0, blk1)

    def copy_of(j, ch):
        at = pl.multiple_of(ch * CHUNK, CHUNK)
        return pltpu.make_async_copy(
            blocks[j].at[pl.ds(at, CHUNK)],
            held.at[j, pl.ds(at, CHUNK)],
            blk_sem.at[j * n_chunks + ch],
        )

    moves = [
        pltpu.make_async_copy(piece, src.at[pl.ds(p * 1024, 1024)], src_sem.at[p])
        for p, piece in enumerate(pieces)
    ]
    for move in moves:
        move.start()
    used = [lax.div(cnt_ref[j] + (CHUNK - 1), CHUNK) for j in range(2)]
    for j in range(2):

        @pl.loop(0, used[j])
        def _(ch):
            copy_of(j, ch).start()

    acc[...] = jnp.zeros_like(acc)
    for move in moves:
        move.wait()
    dims = (((0,), (0,)), ((), ())) if transposed else (((1,), (0,)), ((), ()))
    for j in range(2):
        count = cnt_ref[j]

        @pl.loop(0, used[j])
        def _(ch):
            copy_of(j, ch).wait()
            left = jnp.minimum(count - ch * CHUNK, CHUNK)

            @pl.loop(0, lax.div(left + (UNROLL - 1), UNROLL))
            def _(step):
                base = ch * CHUNK + step * UNROLL
                for u in range(UNROLL):
                    slot = base + u
                    take = pl.multiple_of(off_ref[j * SLOTS + slot], SIDE)
                    put = pl.multiple_of(off_ref[(2 + j) * SLOTS + slot], SIDE)
                    term = lax.dot_general(
                        held[j, slot],
                        src[pl.ds(take, SIDE), :],
                        dims,
                        preferred_element_type=F32,
                    )
                    acc[pl.ds(put, SIDE), :] += term

    out_ref[...] = acc[: 16 * 512, :].astype(BF).reshape(out_ref.shape)


def cell_products(transposed, offsets, counts, blk_own, blk_other, pieces):
    any_spec = pl.BlockSpec(memory_space=pl.ANY)
    smem = pl.BlockSpec(memory_space=pltpu.SMEM)
    n_chunks = SLOTS // CHUNK
    return pl.pallas_call(
        functools.partial(cells_kernel, transposed),
        out_shape=jax.ShapeDtypeStruct((16, 512, 128), BF),
        in_specs=[smem, smem] + [any_spec] * 10,
        out_specs=pl.BlockSpec(memory_space=pltpu.VMEM),
        scratch_shapes=[
            pltpu.VMEM((8192, 128), BF),
            pltpu.VMEM((2, SLOTS, SIDE, SIDE), BF),
            pltpu.VMEM((8192 + SIDE, 128), F32),
            pltpu.SemaphoreType.DMA((2 * n_chunks,)),
            pltpu.SemaphoreType.DMA((8,)),
        ],
        compiler_params=pltpu.CompilerParams(vmem_limit_bytes=VMEM_LIMIT),
        cost_estimate=pl.CostEstimate(
            flops=2 * 2 * SLOTS * SIDE * SIDE * 128, bytes_accessed=10 << 20, transcendentals=0
        ),
        name="cells_back" if transposed else "cells_forward",
    )(offsets, counts, blk_own, blk_other, *pieces)


def grads_kernel(core_ref, joined, act_one, cot, gp_one, gp_two, act_two, own_ref, other_ref):
    core = core_ref[0]
    sides = ((joined, gp_one, 0, 512), (act_one, gp_two, 512, 1024), (cot, act_two, 1536, 256))
    for ref, half in ((own_ref, core), (other_ref, 1 - core)):
        at = pl.multiple_of(half * 512, 512)
        for left, right, row, size in sides:
            for part in range(0, size, 256):
                ref[row + part : row + part + 256, :] = lax.dot_general(
                    left[:, part : part + 256],
                    right[:, pl.ds(at, 512)],
                    (((0,), (0,)), ((), ())),
                    preferred_element_type=F32,
                ).astype(BF)


def local_grads(core, joined, act_one, cot, gp_one, gp_two, act_two):
    vm = pl.BlockSpec(memory_space=pltpu.VMEM)
    return pl.pallas_call(
        grads_kernel,
        out_shape=(jax.ShapeDtypeStruct((1792, 512), BF),) * 2,
        in_specs=[pl.BlockSpec(memory_space=pltpu.SMEM)] + [vm] * 6,
        out_specs=(vm, vm),
        compiler_params=pltpu.CompilerParams(vmem_limit_bytes=VMEM_LIMIT),
        cost_estimate=pl.CostEstimate(
            flops=2 * 512 * 1792 * 1024, bytes_accessed=8 << 20, transcendentals=0
        ),
        name="local_grads",
    )(core.reshape(1), joined, act_one, cot, gp_one, gp_two, act_two)


def gather_steps(value, axes):
    pieces = []
    for p in range(8):
        big, small = p >> 1, p & 1
        if p == 0:
            pieces.append(value)
            continue
        perm = []
        for i in range(8):
            if axes == ("z", "yh"):
                to = (((i >> 1) + big) % 4) * 2 + ((i & 1) ^ small)
            else:
                to = ((i >> 2) ^ small) * 4 + ((i & 3) + big) % 4
            perm.append((i, to))
        pieces.append(lax.ppermute(value, axes, perm))
    return pieces


def halves(value, core):
    left, right = value[:, :128], value[:, 128:]
    first = core == 0
    mine = jnp.where(first, left, right)
    yours = jnp.where(first, right, left)
    got = lax.ppermute(yours, "core", [(0, 1), (1, 0)])
    return jnp.concatenate([mine, got], axis=0)


def finish_kernel(core_ref, pos_ref, *rest):
    own, other = rest[:4], rest[4:8]
    in_ref, mid_ref, out_ref = rest[8:]
    ratio = 1.0 / 256.0
    core, x = core_ref[0], pos_ref[0]
    for group, half in ((own, core), (other, 1 - core)):
        for k, piece in enumerate(group):
            src_x = lax.rem(x + (4 - k), 4)
            lane = pl.multiple_of(half * 512 + src_x * 128, 128)
            full = piece[...].astype(F32) * ratio
            in_ref[:, pl.ds(lane, 128)] = full[:512]
            mid_ref[:, pl.ds(lane, 128)] = full[512:1536]
            out_ref[pl.ds(lane, 128), :] = full[1536:].T


def finish_grads(core, x, own, other):
    vm = pl.BlockSpec(memory_space=pltpu.VMEM)
    sm = pl.BlockSpec(memory_space=pltpu.SMEM)
    return pl.pallas_call(
        finish_kernel,
        out_shape=(
            jax.ShapeDtypeStruct((512, 1024), F32),
            jax.ShapeDtypeStruct((1024, 1024), F32),
            jax.ShapeDtypeStruct((1024, 256), F32),
        ),
        in_specs=[sm, sm] + [vm] * 8,
        out_specs=(vm, vm, vm),
        compiler_params=pltpu.CompilerParams(vmem_limit_bytes=VMEM_LIMIT),
        cost_estimate=pl.CostEstimate(flops=1 << 20, bytes_accessed=11 << 20, transcendentals=0),
        name="finish_grads",
    )(core.reshape(1), x.reshape(1), *own, *other)


def sum_grads(core, own, other):
    x = lax.axis_index("x")
    got = lax.ppermute(other, "core", [(0, 1), (1, 0)])
    chip = (own.astype(F32) + got.astype(F32)).astype(BF)
    part = lax.all_to_all(chip.reshape(4, 448, 512), "z", 0, 0, tiled=True)
    part = jnp.sum(part.astype(F32), axis=0).astype(BF)
    part = part.reshape(4, 112, 4, 128).transpose(0, 2, 1, 3).reshape(16, 112, 128)
    part = lax.all_to_all(part, ("yh", "yl", "x"), 0, 0, tiled=True)
    part = jnp.sum(part.astype(F32), axis=0).astype(BF)
    lanes = jnp.broadcast_to(part[None], (16, 112, 128))
    lanes = lax.all_to_all(lanes, ("z", "yh", "yl"), 0, 0, tiled=True).reshape(1792, 128)
    mine = [lanes] + [
        lax.ppermute(lanes, "x", [(i, (i + k) % 4) for i in range(4)]) for k in range(1, 4)
    ]
    yours = [lax.ppermute(piece, "core", [(0, 1), (1, 0)]) for piece in mine]
    return finish_grads(core, x, mine, yours)


def shards(features, blocks, block_rows, block_cols, block_count, w_in, w_mid, w_out, cotangent):
    core = lax.axis_index("core")
    z, yh = lax.axis_index("z"), lax.axis_index("yh")
    yl, x = lax.axis_index("yl"), lax.axis_index("x")
    swap = [(0, 1), (1, 0)]
    blk_own = blocks[0, 0]
    meta = jnp.concatenate(
        [block_rows[0, 0], block_cols[0, 0], jnp.broadcast_to(block_count[0, 0], (128,))]
    )
    meta_other = lax.ppermute(meta, "core", swap)
    blk_other = lax.ppermute(blk_own, "core", swap)

    both = jnp.stack([meta, meta_other])
    rows, cols, count = both[:, :SLOTS], both[:, SLOTS : 2 * SLOTS], both[:, 2 * SLOTS]
    live = jnp.arange(SLOTS, dtype=jnp.int32)[None, :] < count[:, None]
    cell_core = jnp.stack([core, 1 - core])[:, None]
    spare = 16 * 512
    grp = cols >> 3
    step = (((z - (grp >> 2)) & 3) * 2) + (((grp >> 1) & 1) ^ yh)
    col_at = step * 1024 + ((grp & 1) ^ core) * 512 + (cols & 7) * SIDE
    row_to = jnp.where(live, cell_core * 4096 + rows * SIDE, spare)
    fwd_off = jnp.concatenate([col_at, row_to]).reshape(4 * SLOTS)
    own8 = rows >> 3
    step = (((x - own8) & 3) * 2) + ((own8 >> 2) ^ yl)
    row_at = step * 1024 + jnp.arange(2, dtype=jnp.int32)[:, None] * 512 + (rows & 7) * SIDE
    col_to = jnp.where(live, cols * SIDE, spare)
    bwd_off = jnp.concatenate([row_at, col_to]).reshape(4 * SLOTS)

    pieces = gather_steps(halves(features, core), ("z", "yh"))
    cells = cell_products(False, fwd_off, count, blk_own, blk_other, pieces)
    cells = lax.all_to_all(cells, ("core", "yl", "x"), 0, 0, tiled=True)
    sums = jnp.sum(cells.reshape(2, 8, 512, 128).astype(F32), axis=1).astype(BF)
    aggregated = jnp.concatenate([sums[0], sums[1]], axis=1)

    joined = jnp.concatenate([features, aggregated], axis=1)
    pre_one = jnp.dot(joined, w_in, preferred_element_type=F32)
    act_one = jax.nn.silu(pre_one).astype(BF)
    pre_two = jnp.dot(act_one, w_mid, preferred_element_type=F32)
    act_two = jax.nn.silu(pre_two).astype(BF)
    updated = (
        features.astype(F32) + jnp.dot(act_two, w_out, preferred_element_type=F32)
    ).astype(BF)
    grad_pre_two = (
        jnp.dot(cotangent, w_out.T, preferred_element_type=F32) * silu_grad(pre_two)
    ).astype(BF)
    grad_pre_one = (
        jnp.dot(grad_pre_two, w_mid.T, preferred_element_type=F32) * silu_grad(pre_one)
    ).astype(BF)
    grad_joined = jnp.dot(grad_pre_one, w_in.T, preferred_element_type=F32)
    direct = cotangent.astype(F32) + grad_joined[:, :256]
    grad_agg = grad_joined[:, 256:].astype(BF)

    pieces = gather_steps(halves(grad_agg, core), COL)
    own, other = local_grads(core, joined, act_one, cotangent, grad_pre_one, grad_pre_two, act_two)
    back = cell_products(True, bwd_off, count, blk_own, blk_other, pieces)
    back = lax.all_to_all(back, ROW, 0, 0, tiled=True)
    sums = jnp.sum(back.reshape(8, 2, 512, 128).astype(F32), axis=0)
    relaid = jnp.concatenate([sums[0], sums[1]], axis=1)
    grad_nodes = (direct + relaid).astype(BF)
    grad_in, grad_mid, grad_out = sum_grads(core, own, other)
    return updated, grad_nodes, grad_in, grad_mid, grad_out


def solution(mesh):
    fine = Mesh(mesh.devices.reshape(4, 2, 2, 2, 4), ROW + COL)
    nodes = P(ROW + COL, None)
    placed = (
        nodes,
        P(ROW, COL, None, None, None),
        P(ROW, COL, None),
        P(ROW, COL, None),
        P(ROW, COL),
        P(),
        P(),
        P(),
        nodes,
    )
    return jax.shard_map(
        shards,
        mesh=fine,
        in_specs=placed,
        out_specs=(nodes, nodes, P(), P(), P()),
        check_vma=False,
    )
```

```python
import functools

import jax
import jax.numpy as jnp
from jax import lax
from jax.experimental import pallas as pl
from jax.experimental.pallas import tpu as pltpu
from jax.sharding import Mesh, PartitionSpec as P


BF = jnp.bfloat16
F32 = jnp.float32
ROW = ("z", "yh", "core")
COL = ("yl", "x")
SLOTS = 192
SIDE = 64
CHUNK = 32
UNROLL = 8
VMEM_LIMIT = 60 * 1024 * 1024


def silu_grad(value):
    sig = jax.nn.sigmoid(value)
    return sig * (1.0 + value * (1.0 - sig))


def cells_kernel(transposed, off_ref, cnt_ref, place_ref, blk0, blk1, *rest):
    pieces = rest[:8]
    out_refs = rest[8:-5]
    src, held, acc, blk_sem, src_sem = rest[-5:]
    n_chunks = SLOTS // CHUNK
    blocks = (blk0, blk1)

    def copy_of(j, ch):
        at = pl.multiple_of(ch * CHUNK, CHUNK)
        return pltpu.make_async_copy(
            blocks[j].at[pl.ds(at, CHUNK)],
            held.at[j, pl.ds(at, CHUNK)],
            blk_sem.at[j * n_chunks + ch],
        )

    moves = [
        pltpu.make_async_copy(piece, src.at[pl.ds(p * 1024, 1024)], src_sem.at[p])
        for p, piece in enumerate(pieces)
    ]
    for move in moves:
        move.start()
    used = [lax.div(cnt_ref[j] + (CHUNK - 1), CHUNK) for j in range(2)]
    for j in range(2):

        @pl.loop(0, used[j])
        def _(ch):
            copy_of(j, ch).start()

    acc[...] = jnp.zeros_like(acc)
    for move in moves:
        move.wait()
    dims = (((0,), (0,)), ((), ())) if transposed else (((1,), (0,)), ((), ()))
    for j in range(2):
        count = cnt_ref[j]

        @pl.loop(0, used[j])
        def _(ch):
            copy_of(j, ch).wait()
            left = jnp.minimum(count - ch * CHUNK, CHUNK)

            @pl.loop(0, lax.div(left + (UNROLL - 1), UNROLL))
            def _(step):
                base = ch * CHUNK + step * UNROLL
                for u in range(UNROLL):
                    slot = base + u
                    take = pl.multiple_of(off_ref[j * SLOTS + slot], SIDE)
                    put = pl.multiple_of(off_ref[(2 + j) * SLOTS + slot], SIDE)
                    term = lax.dot_general(
                        held[j, slot],
                        src[pl.ds(take, SIDE), :],
                        dims,
                        preferred_element_type=F32,
                    )
                    acc[pl.ds(put, SIDE), :] += term

    if len(out_refs) == 1:
        out_refs[0][...] = acc[: 16 * 512, :].astype(BF).reshape(out_refs[0].shape)
    else:
        for p, out_ref in enumerate(out_refs):
            for h in range(2):
                at = pl.multiple_of(place_ref[2 * p + h], 512)
                out_ref[h * 512 : (h + 1) * 512, :] = acc[pl.ds(at, 512), :].astype(BF)


def cell_products(transposed, offsets, counts, place, blk_own, blk_other, pieces):
    any_spec = pl.BlockSpec(memory_space=pl.ANY)
    smem = pl.BlockSpec(memory_space=pltpu.SMEM)
    n_chunks = SLOTS // CHUNK
    return pl.pallas_call(
        functools.partial(cells_kernel, transposed),
        out_shape=(jax.ShapeDtypeStruct((1024, 128), BF),) * 8
        if transposed
        else jax.ShapeDtypeStruct((16, 512, 128), BF),
        in_specs=[smem] * 3 + [any_spec] * 10,
        out_specs=(pl.BlockSpec(memory_space=pltpu.VMEM),) * 8
        if transposed
        else pl.BlockSpec(memory_space=pltpu.VMEM),
        scratch_shapes=[
            pltpu.VMEM((8192, 128), BF),
            pltpu.VMEM((2, SLOTS, SIDE, SIDE), BF),
            pltpu.VMEM((8192 + SIDE, 128), F32),
            pltpu.SemaphoreType.DMA((2 * n_chunks,)),
            pltpu.SemaphoreType.DMA((8,)),
        ],
        compiler_params=pltpu.CompilerParams(vmem_limit_bytes=VMEM_LIMIT),
        cost_estimate=pl.CostEstimate(
            flops=2 * 2 * SLOTS * SIDE * SIDE * 128, bytes_accessed=10 << 20, transcendentals=0
        ),
        name="cells_back" if transposed else "cells_forward",
    )(offsets, counts, place, blk_own, blk_other, *pieces)


def grads_kernel(half_ref, joined, act_one, cot, gp_one, gp_two, act_two, sum_ref):
    at = pl.multiple_of(half_ref[0] * 512, 512)
    sides = ((joined, gp_one, 0, 512), (act_one, gp_two, 512, 1024), (cot, act_two, 1536, 256))
    for left, right, row, size in sides:
        for part in range(0, size, 256):
            sum_ref[row + part : row + part + 256, :] = lax.dot_general(
                left[:, part : part + 256],
                right[:, pl.ds(at, 512)],
                (((0,), (0,)), ((), ())),
                preferred_element_type=F32,
            ).astype(BF)


def local_grads(half, *operands):
    vm = pl.BlockSpec(memory_space=pltpu.VMEM)
    return pl.pallas_call(
        grads_kernel,
        out_shape=jax.ShapeDtypeStruct((1792, 512), BF),
        in_specs=[pl.BlockSpec(memory_space=pltpu.SMEM)] + [vm] * 6,
        out_specs=vm,
        compiler_params=pltpu.CompilerParams(vmem_limit_bytes=VMEM_LIMIT),
        cost_estimate=pl.CostEstimate(
            flops=512 * 1792 * 1024, bytes_accessed=8 << 20, transcendentals=0
        ),
    )(half.reshape(1), *operands)


def chip_kernel(z_ref, own, got, *out_refs):
    for k, out_ref in enumerate(out_refs):
        at = pl.multiple_of(lax.rem(z_ref[0] + k, 4) * 448, 64)
        rows = pl.ds(at, 448)
        out_ref[...] = (own[rows, :].astype(F32) + got[rows, :].astype(F32)).astype(BF)


def chip_sum(z, own, got):
    vm = pl.BlockSpec(memory_space=pltpu.VMEM)
    return pl.pallas_call(
        chip_kernel,
        out_shape=(jax.ShapeDtypeStruct((448, 512), BF),) * 4,
        in_specs=[pl.BlockSpec(memory_space=pltpu.SMEM), vm, vm],
        out_specs=(vm,) * 4,
        cost_estimate=pl.CostEstimate(flops=1 << 20, bytes_accessed=6 << 20, transcendentals=0),
        name="chip_sum",
    )(z.reshape(1), own, got)


def quarter_kernel(*refs):
    out_ref = refs[-1]
    total = refs[0][...].astype(F32)
    for ref in refs[1:-1]:
        total = total + ref[...].astype(F32)
    for row in range(4):
        for lane in range(4):
            out_ref[row * 4 + lane] = total[
                row * 112 : (row + 1) * 112, lane * 128 : (lane + 1) * 128
            ].astype(BF)


def quarter_sum(parts):
    vm = pl.BlockSpec(memory_space=pltpu.VMEM)
    return pl.pallas_call(
        quarter_kernel,
        out_shape=jax.ShapeDtypeStruct((16, 112, 128), BF),
        in_specs=[vm] * len(parts),
        out_specs=vm,
        cost_estimate=pl.CostEstimate(flops=1 << 20, bytes_accessed=3 << 20, transcendentals=0),
        name="quarter_sum",
    )(*parts)


def chunk_kernel(parts, out_ref):
    total = jnp.sum(parts[...].astype(F32), axis=0).astype(BF)
    for k in range(16):
        out_ref[k] = total


def chunk_sum(parts):
    vm = pl.BlockSpec(memory_space=pltpu.VMEM)
    return pl.pallas_call(
        chunk_kernel,
        out_shape=jax.ShapeDtypeStruct((16, 112, 128), BF),
        in_specs=[vm],
        out_specs=vm,
        cost_estimate=pl.CostEstimate(flops=1 << 20, bytes_accessed=1 << 20, transcendentals=0),
        name="chunk_sum",
    )(parts)


def step_perm(axes, p):
    big, small = p >> 1, p & 1
    perm = []
    for i in range(8):
        if axes == ("z", "yh"):
            to = (((i >> 1) + big) % 4) * 2 + ((i & 1) ^ small)
        else:
            to = ((i >> 2) ^ small) * 4 + ((i & 3) + big) % 4
        perm.append((i, to))
    return perm


def send_steps(pieces, axes):
    got = [pieces[0]]
    for p in range(1, 8):
        got.append(lax.ppermute(pieces[p], axes, step_perm(axes, p)))
    return got


def node_kernel(*refs):
    mine_ref, yours_ref = refs[-2:]
    for rows, out_ref in ((slice(0, 512), mine_ref), (slice(512, 1024), yours_ref)):
        total = refs[0][rows, :].astype(F32)
        for ref in refs[1:-2]:
            total = total + ref[rows, :].astype(F32)
        out_ref[...] = total.astype(out_ref.dtype)


def node_sum(parts):
    vm = pl.BlockSpec(memory_space=pltpu.VMEM)
    return pl.pallas_call(
        node_kernel,
        out_shape=(
            jax.ShapeDtypeStruct((512, 128), F32),
            jax.ShapeDtypeStruct((512, 128), BF),
        ),
        in_specs=[vm] * len(parts),
        out_specs=(vm, vm),
        cost_estimate=pl.CostEstimate(flops=1 << 20, bytes_accessed=3 << 20, transcendentals=0),
        name="node_sum",
    )(*parts)


def halves(value, core):
    left, right = value[:, :128], value[:, 128:]
    first = core == 0
    mine = jnp.where(first, left, right)
    yours = jnp.where(first, right, left)
    got = lax.ppermute(yours, "core", [(0, 1), (1, 0)])
    return jnp.concatenate([mine, got], axis=0)


def finish_kernel(lane_ref, own, other, *rest):
    outs = rest[-10:-7]
    scratch, sems = rest[-7:-1], rest[-1]
    moves = []
    for group, piece in enumerate((own, other)):
        full = piece[...].astype(F32) * (1.0 / 256.0)
        lane = pl.multiple_of(lane_ref[group], 128)
        held = scratch[group * 3 : group * 3 + 3]
        held[0][...] = full[:512]
        held[1][...] = full[512:1536]
        held[2][...] = full[1536:].T
        targets = (
            outs[0].at[:, pl.ds(lane, 128)],
            outs[1].at[:, pl.ds(lane, 128)],
            outs[2].at[pl.ds(lane, 128), :],
        )
        for k in range(3):
            move = pltpu.make_async_copy(held[k], targets[k], sems.at[group * 3 + k])
            move.start()
            moves.append(move)
    for move in moves:
        move.wait()


def finish_grads(lanes, own, other, outs):
    vm = pl.BlockSpec(memory_space=pltpu.VMEM)
    any_spec = pl.BlockSpec(memory_space=pl.ANY)
    held = [
        pltpu.VMEM((512, 128), F32),
        pltpu.VMEM((1024, 128), F32),
        pltpu.VMEM((128, 256), F32),
    ]
    return pl.pallas_call(
        finish_kernel,
        out_shape=(
            jax.ShapeDtypeStruct((512, 1024), F32),
            jax.ShapeDtypeStruct((1024, 1024), F32),
            jax.ShapeDtypeStruct((1024, 256), F32),
        ),
        in_specs=[pl.BlockSpec(memory_space=pltpu.SMEM), vm, vm] + [any_spec] * len(outs),
        out_specs=(any_spec,) * 3,
        scratch_shapes=held + held + [pltpu.SemaphoreType.DMA((6,))],
        input_output_aliases={3 + k: k for k in range(len(outs))},
        cost_estimate=pl.CostEstimate(flops=1 << 20, bytes_accessed=3 << 20, transcendentals=0),
        name="finish_grads",
    )(lanes, own, other, *outs)


def sum_grads(core, operands):
    x, z = lax.axis_index("x"), lax.axis_index("z")
    swap = [(0, 1), (1, 0)]
    other = local_grads(1 - core, *operands)
    got = lax.ppermute(other, "core", swap)
    own = local_grads(core, *operands)
    quarters = chip_sum(z, own, got)
    parts = [quarters[0]]
    for k in range(1, 4):
        parts.append(lax.ppermute(quarters[k], "z", [(i, (i + k) % 4) for i in range(4)]))
    part = quarter_sum(parts)
    part = lax.all_to_all(part, ("yh", "yl", "x"), 0, 0, tiled=True)
    lanes = lax.all_to_all(chunk_sum(part), ("z", "yh", "yl"), 0, 0, tiled=True)
    lanes = lanes.reshape(1792, 128)
    outs = ()
    for k in range(4):
        piece = lanes
        if k:
            piece = lax.ppermute(lanes, "x", [(i, (i + k) % 4) for i in range(4)])
        place = ((x - k) & 3) * 128
        at = jnp.stack([core * 512 + place, (1 - core) * 512 + place])
        outs = finish_grads(at, piece, lax.ppermute(piece, "core", swap), outs)
    return outs


def shards(features, blocks, block_rows, block_cols, block_count, w_in, w_mid, w_out, cotangent):
    core = lax.axis_index("core")
    z, yh = lax.axis_index("z"), lax.axis_index("yh")
    yl, x = lax.axis_index("yl"), lax.axis_index("x")
    swap = [(0, 1), (1, 0)]
    blk_own = blocks[0, 0]
    meta = jnp.concatenate(
        [block_rows[0, 0], block_cols[0, 0], jnp.broadcast_to(block_count[0, 0], (128,))]
    )
    meta_other = lax.ppermute(meta, "core", swap)
    blk_other = lax.ppermute(blk_own, "core", swap)

    both = jnp.stack([meta, meta_other])
    rows, cols, count = both[:, :SLOTS], both[:, SLOTS : 2 * SLOTS], both[:, 2 * SLOTS]
    live = jnp.arange(SLOTS, dtype=jnp.int32)[None, :] < count[:, None]
    cell_core = jnp.stack([core, 1 - core])[:, None]
    spare = 16 * 512
    grp = cols >> 3
    step = (((z - (grp >> 2)) & 3) * 2) + (((grp >> 1) & 1) ^ yh)
    col_at = step * 1024 + ((grp & 1) ^ core) * 512 + (cols & 7) * SIDE
    row_to = jnp.where(live, cell_core * 4096 + rows * SIDE, spare)
    fwd_off = jnp.concatenate([col_at, row_to]).reshape(4 * SLOTS)
    own8 = rows >> 3
    step = (((x - own8) & 3) * 2) + ((own8 >> 2) ^ yl)
    row_at = step * 1024 + jnp.arange(2, dtype=jnp.int32)[:, None] * 512 + (rows & 7) * SIDE
    col_to = jnp.where(live, cols * SIDE, spare)
    bwd_off = jnp.concatenate([row_at, col_to]).reshape(4 * SLOTS)

    p = jnp.arange(16, dtype=jnp.int32)
    place = (((z + (p >> 2)) & 3) * 4 + (yh ^ ((p >> 1) & 1)) * 2 + (core ^ (p & 1))) * 512
    shard = halves(features, core)
    pieces = send_steps([shard] * 8, ("z", "yh"))
    blk_own, _ = lax.optimization_barrier((blk_own, shard))
    cells = cell_products(False, fwd_off, count, place, blk_own, blk_other, pieces)
    cells = lax.all_to_all(cells, ("core", "yl", "x"), 0, 0, tiled=True)
    sums = jnp.sum(cells.reshape(2, 8, 512, 128).astype(F32), axis=1).astype(BF)
    aggregated = jnp.concatenate([sums[0], sums[1]], axis=1)

    joined = jnp.concatenate([features, aggregated], axis=1)
    pre_one = jnp.dot(joined, w_in, preferred_element_type=F32)
    act_one = jax.nn.silu(pre_one).astype(BF)
    pre_two = jnp.dot(act_one, w_mid, preferred_element_type=F32)
    act_two = jax.nn.silu(pre_two).astype(BF)
    updated = (
        features.astype(F32) + jnp.dot(act_two, w_out, preferred_element_type=F32)
    ).astype(BF)
    grad_pre_two = (
        jnp.dot(cotangent, w_out.T, preferred_element_type=F32) * silu_grad(pre_two)
    ).astype(BF)
    grad_pre_one = (
        jnp.dot(grad_pre_two, w_mid.T, preferred_element_type=F32) * silu_grad(pre_one)
    ).astype(BF)
    grad_joined = jnp.dot(grad_pre_one, w_in.T, preferred_element_type=F32)
    direct = cotangent.astype(F32) + grad_joined[:, :256]
    grad_agg = grad_joined[:, 256:].astype(BF)

    pieces = send_steps([halves(grad_agg, core)] * 8, COL)
    operands = (joined, act_one, cotangent, grad_pre_one, grad_pre_two, act_two)
    grad_in, grad_mid, grad_out = sum_grads(core, operands)
    back = cell_products(True, bwd_off, count, place, blk_own, blk_other, pieces)
    mine, yours = node_sum(send_steps(back, ("z", "yh")))
    got = lax.ppermute(yours, "core", swap).astype(F32)
    first = core == 0
    relaid = jnp.concatenate([jnp.where(first, mine, got), jnp.where(first, got, mine)], axis=1)
    grad_nodes = (direct + relaid).astype(BF)
    return updated, grad_nodes, grad_in, grad_mid, grad_out


def solution(mesh):
    fine = Mesh(mesh.devices.reshape(4, 2, 2, 2, 4), ROW + COL)
    nodes = P(ROW + COL, None)
    placed = (
        nodes,
        P(ROW, COL, None, None, None),
        P(ROW, COL, None),
        P(ROW, COL, None),
        P(ROW, COL),
        P(),
        P(),
        P(),
        nodes,
    )

    return jax.shard_map(
        shards,
        mesh=fine,
        in_specs=placed,
        out_specs=(nodes, nodes, P(), P(), P()),
        check_vma=False,
    )
```

```python
import functools

import jax
import jax.numpy as jnp
from jax import lax
from jax.experimental import pallas as pl
from jax.experimental.pallas import tpu as pltpu
from jax.experimental.layout import Layout, with_layout_constraint
from jax.sharding import Mesh, PartitionSpec as P


BF = jnp.bfloat16
F32 = jnp.float32
ROW = ("z", "yh", "core")
COL = ("yl", "x")
SLOTS = 192
SIDE = 64
CHUNK = 32
UNROLL = 8
FINISH = (
    ("m", 0),
    ("y", 0),
    ("m", 1),
    ("m", 3),
    ("y", 1),
    ("y", 3),
    ("m", 2),
    ("y", 2),
)
VMEM_LIMIT = 60 * 1024 * 1024


def silu_grad(value):
    sig = jax.nn.sigmoid(value)
    return sig * (1.0 + value * (1.0 - sig))


def cells_kernel(transposed, off_ref, cnt_ref, place_ref, blk0, blk1, *rest):
    pieces = rest[:8]
    out_refs = rest[8:-5]
    src, held, acc, blk_sem, src_sem = rest[-5:]
    n_chunks = SLOTS // CHUNK
    blocks = (blk0, blk1)

    def copy_of(j, ch):
        at = pl.multiple_of(ch * CHUNK, CHUNK)
        return pltpu.make_async_copy(
            blocks[j].at[pl.ds(at, CHUNK)],
            held.at[j, pl.ds(at, CHUNK)],
            blk_sem.at[j * n_chunks + ch],
        )

    moves = [
        pltpu.make_async_copy(piece, src.at[pl.ds(p * 1024, 1024)], src_sem.at[p])
        for p, piece in enumerate(pieces)
    ]
    for move in moves:
        move.start()
    used = [lax.div(cnt_ref[j] + (CHUNK - 1), CHUNK) for j in range(2)]
    for j in range(2):

        @pl.loop(0, used[j])
        def _(ch):
            copy_of(j, ch).start()

    acc[...] = jnp.zeros_like(acc)
    for move in moves:
        move.wait()
    dims = (((0,), (0,)), ((), ())) if transposed else (((1,), (0,)), ((), ()))
    for j in range(2):
        count = cnt_ref[j]

        @pl.loop(0, used[j])
        def _(ch):
            copy_of(j, ch).wait()
            left = jnp.minimum(count - ch * CHUNK, CHUNK)

            @pl.loop(0, lax.div(left + (UNROLL - 1), UNROLL))
            def _(step):
                base = ch * CHUNK + step * UNROLL
                for u in range(UNROLL):
                    slot = base + u
                    take = pl.multiple_of(off_ref[j * SLOTS + slot], SIDE)
                    put = pl.multiple_of(off_ref[(2 + j) * SLOTS + slot], SIDE)
                    term = lax.dot_general(
                        held[j, slot],
                        src[pl.ds(take, SIDE), :],
                        dims,
                        preferred_element_type=F32,
                    )
                    acc[pl.ds(put, SIDE), :] += term

    if len(out_refs) == 1:
        out_refs[0][...] = acc[: 16 * 512, :].astype(BF).reshape(out_refs[0].shape)
    else:
        for p, out_ref in enumerate(out_refs):
            for h in range(2):
                at = pl.multiple_of(place_ref[2 * p + h], 512)
                out_ref[h * 512 : (h + 1) * 512, :] = acc[pl.ds(at, 512), :].astype(BF)


def cell_products(transposed, offsets, counts, place, blk_own, blk_other, pieces):
    any_spec = pl.BlockSpec(memory_space=pl.ANY)
    smem = pl.BlockSpec(memory_space=pltpu.SMEM)
    n_chunks = SLOTS // CHUNK
    return pl.pallas_call(
        functools.partial(cells_kernel, transposed),
        out_shape=(jax.ShapeDtypeStruct((1024, 128), BF),) * 8
        if transposed
        else jax.ShapeDtypeStruct((16, 512, 128), BF),
        in_specs=[smem] * 3 + [any_spec] * 10,
        out_specs=(pl.BlockSpec(memory_space=pltpu.VMEM),) * 8
        if transposed
        else pl.BlockSpec(memory_space=pltpu.VMEM),
        scratch_shapes=[
            pltpu.VMEM((8192, 128), BF),
            pltpu.VMEM((2, SLOTS, SIDE, SIDE), BF),
            pltpu.VMEM((8192 + SIDE, 128), F32),
            pltpu.SemaphoreType.DMA((2 * n_chunks,)),
            pltpu.SemaphoreType.DMA((8,)),
        ],
        compiler_params=pltpu.CompilerParams(vmem_limit_bytes=VMEM_LIMIT),
        cost_estimate=pl.CostEstimate(
            flops=2 * 2 * SLOTS * SIDE * SIDE * 128, bytes_accessed=10 << 20, transcendentals=0
        ),
        name="cells_back" if transposed else "cells_forward",
    )(offsets, counts, place, blk_own, blk_other, *pieces)


def grads_kernel(half_ref, joined, act_one, cot, gp_one, gp_two, act_two, sum_ref):
    at = pl.multiple_of(half_ref[0] * 512, 512)
    sides = ((joined, gp_one, 0, 512), (act_one, gp_two, 512, 1024), (cot, act_two, 1536, 256))
    for left, right, row, size in sides:
        for part in range(0, size, 256):
            sum_ref[row + part : row + part + 256, :] = lax.dot_general(
                left[:, part : part + 256],
                right[:, pl.ds(at, 512)],
                (((0,), (0,)), ((), ())),
                preferred_element_type=F32,
            ).astype(BF)


def local_grads(half, *operands):
    vm = pl.BlockSpec(memory_space=pltpu.VMEM)
    return pl.pallas_call(
        grads_kernel,
        out_shape=jax.ShapeDtypeStruct((1792, 512), BF),
        in_specs=[pl.BlockSpec(memory_space=pltpu.SMEM)] + [vm] * 6,
        out_specs=vm,
        compiler_params=pltpu.CompilerParams(vmem_limit_bytes=VMEM_LIMIT),
        cost_estimate=pl.CostEstimate(
            flops=512 * 1792 * 1024, bytes_accessed=8 << 20, transcendentals=0
        ),
    )(half.reshape(1), *operands)


def chip_kernel(own, got, out_ref):
    for row in range(16):
        rows = slice(row * 112, (row + 1) * 112)
        for lane in range(4):
            lanes = slice(lane * 128, (lane + 1) * 128)
            out_ref[row * 4 + lane] = (
                own[rows, lanes].astype(F32) + got[rows, lanes].astype(F32)
            ).astype(BF)


def chip_sum(own, got):
    vm = pl.BlockSpec(memory_space=pltpu.VMEM)
    return pl.pallas_call(
        chip_kernel,
        out_shape=jax.ShapeDtypeStruct((64, 112, 128), BF),
        in_specs=[vm, vm],
        out_specs=vm,
        cost_estimate=pl.CostEstimate(flops=1 << 20, bytes_accessed=6 << 20, transcendentals=0),
        name="chip_sum",
    )(own, got)


def chunk_kernel(parts, out_ref):
    total = jnp.sum(parts[...].astype(F32), axis=0).astype(BF)
    for k in range(16):
        out_ref[k] = total


def chunk_sum(parts):
    vm = pl.BlockSpec(memory_space=pltpu.VMEM)
    return pl.pallas_call(
        chunk_kernel,
        out_shape=jax.ShapeDtypeStruct((16, 112, 128), BF),
        in_specs=[vm],
        out_specs=vm,
        cost_estimate=pl.CostEstimate(flops=1 << 20, bytes_accessed=1 << 20, transcendentals=0),
        name="chunk_sum",
    )(parts)


def step_perm(axes, p):
    big, small = p >> 1, p & 1
    perm = []
    for i in range(8):
        if axes == ("z", "yh"):
            to = (((i >> 1) + big) % 4) * 2 + ((i & 1) ^ small)
        else:
            to = ((i >> 2) ^ small) * 4 + ((i & 3) + big) % 4
        perm.append((i, to))
    return perm


def send_steps(pieces, axes):
    got = [pieces[0]]
    for p in range(1, 8):
        got.append(lax.ppermute(pieces[p], axes, step_perm(axes, p)))
    return got


def node_kernel(*refs):
    mine_ref, yours_ref = refs[-2:]
    for rows, out_ref in ((slice(0, 512), mine_ref), (slice(512, 1024), yours_ref)):
        total = refs[0][rows, :].astype(F32)
        for ref in refs[1:-2]:
            total = total + ref[rows, :].astype(F32)
        out_ref[...] = total.astype(out_ref.dtype)


def node_sum(parts):
    vm = pl.BlockSpec(memory_space=pltpu.VMEM)
    return pl.pallas_call(
        node_kernel,
        out_shape=(
            jax.ShapeDtypeStruct((512, 128), F32),
            jax.ShapeDtypeStruct((512, 128), BF),
        ),
        in_specs=[vm] * len(parts),
        out_specs=(vm, vm),
        cost_estimate=pl.CostEstimate(flops=1 << 20, bytes_accessed=3 << 20, transcendentals=0),
        name="node_sum",
    )(*parts)


def halves(value, core):
    left, right = value[:, :128], value[:, 128:]
    first = core == 0
    mine = jnp.where(first, left, right)
    yours = jnp.where(first, right, left)
    got = lax.ppermute(yours, "core", [(0, 1), (1, 0)])
    return jnp.concatenate([mine, got], axis=0)


def finish_kernel(lane_ref, piece, *rest):
    outs, held, sems = rest[-7:-4], rest[-4:-1], rest[-1]
    lane = pl.multiple_of(lane_ref[0], 128)
    targets = (
        outs[0].at[:, pl.ds(lane, 128)],
        outs[1].at[:, pl.ds(lane, 128)],
        outs[2].at[pl.ds(lane, 128), :],
    )
    moves = [pltpu.make_async_copy(held[k], targets[k], sems.at[k]) for k in range(3)]
    held[0][...] = piece[:512, :].astype(F32) * (1.0 / 256.0)
    moves[0].start()
    held[1][...] = piece[512:1536, :].astype(F32) * (1.0 / 256.0)
    moves[1].start()
    held[2][...] = (piece[1536:, :].astype(F32) * (1.0 / 256.0)).T
    moves[2].start()
    for move in moves:
        move.wait()


def finish_grads(lane, piece, outs):
    vm = pl.BlockSpec(memory_space=pltpu.VMEM)
    any_spec = pl.BlockSpec(memory_space=pl.ANY)
    return pl.pallas_call(
        finish_kernel,
        out_shape=(
            jax.ShapeDtypeStruct((512, 1024), F32),
            jax.ShapeDtypeStruct((1024, 1024), F32),
            jax.ShapeDtypeStruct((1024, 256), F32),
        ),
        in_specs=[pl.BlockSpec(memory_space=pltpu.SMEM), vm] + [any_spec] * len(outs),
        out_specs=(any_spec,) * 3,
        scratch_shapes=[
            pltpu.VMEM((512, 128), F32),
            pltpu.VMEM((1024, 128), F32),
            pltpu.VMEM((128, 256), F32),
            pltpu.SemaphoreType.DMA((3,)),
        ],
        input_output_aliases={2 + k: k for k in range(len(outs))},
        cost_estimate=pl.CostEstimate(flops=1 << 20, bytes_accessed=2 << 20, transcendentals=0),
        name="finish_grads",
    )(lane, piece, *outs)


def sum_grads(core, operands):
    x = lax.axis_index("x")
    swap = [(0, 1), (1, 0)]
    other = local_grads(1 - core, *operands)
    got = lax.ppermute(other, "core", swap)
    own = local_grads(core, *operands)
    parts = lax.all_to_all(chip_sum(own, got), ("z", "yh", "yl", "x"), 0, 0, tiled=True)
    chunk = chunk_sum(parts)
    lanes = lax.all_to_all(chunk, ("z", "yh", "yl"), 0, 0, tiled=True)
    lanes = lanes.reshape(1792, 128)
    mine, yours = [lanes], []
    for k in range(1, 4):
        mine.append(lax.ppermute(lanes, "x", [(i, (i + k) % 4) for i in range(4)]))
    for k in range(4):
        yours.append(lax.ppermute(mine[k], "core", swap))
    place = ((x - jnp.arange(4, dtype=jnp.int32)) & 3) * 128
    at_mine, at_yours = core * 512 + place, (1 - core) * 512 + place
    outs = ()
    for side, k in FINISH:
        if side == "m":
            outs = finish_grads(at_mine[k : k + 1], mine[k], outs)
        else:
            outs = finish_grads(at_yours[k : k + 1], yours[k], outs)
    return outs


def shards(features, blocks, block_rows, block_cols, block_count, w_in, w_mid, w_out, cotangent):
    core = lax.axis_index("core")
    z, yh = lax.axis_index("z"), lax.axis_index("yh")
    yl, x = lax.axis_index("yl"), lax.axis_index("x")
    swap = [(0, 1), (1, 0)]
    blk_own = blocks[0, 0].transpose(1, 2, 0)
    meta = jnp.concatenate(
        [block_rows[0, 0], block_cols[0, 0], jnp.broadcast_to(block_count[0, 0], (128,))]
    )
    meta_other = lax.ppermute(meta, "core", swap)
    blk_other = lax.ppermute(blk_own, "core", swap)

    both = jnp.stack([meta, meta_other])
    rows, cols, count = both[:, :SLOTS], both[:, SLOTS : 2 * SLOTS], both[:, 2 * SLOTS]
    live = jnp.arange(SLOTS, dtype=jnp.int32)[None, :] < count[:, None]
    cell_core = jnp.stack([core, 1 - core])[:, None]
    spare = 16 * 512
    grp = cols >> 3
    step = (((z - (grp >> 2)) & 3) * 2) + (((grp >> 1) & 1) ^ yh)
    col_at = step * 1024 + ((grp & 1) ^ core) * 512 + (cols & 7) * SIDE
    row_to = jnp.where(live, cell_core * 4096 + rows * SIDE, spare)
    fwd_off = jnp.concatenate([col_at, row_to]).reshape(4 * SLOTS)
    own8 = rows >> 3
    step = (((x - own8) & 3) * 2) + ((own8 >> 2) ^ yl)
    row_at = step * 1024 + jnp.arange(2, dtype=jnp.int32)[:, None] * 512 + (rows & 7) * SIDE
    col_to = jnp.where(live, cols * SIDE, spare)
    bwd_off = jnp.concatenate([row_at, col_to]).reshape(4 * SLOTS)

    p = jnp.arange(16, dtype=jnp.int32)
    place = (((z + (p >> 2)) & 3) * 4 + (yh ^ ((p >> 1) & 1)) * 2 + (core ^ (p & 1))) * 512
    shard = halves(features, core)
    pieces = send_steps([shard] * 8, ("z", "yh"))
    blk_own, _ = lax.optimization_barrier((blk_own, shard))
    blk_own = with_layout_constraint(blk_own, Layout((0, 1, 2))).transpose(2, 0, 1)
    blk_other = blk_other.transpose(2, 0, 1)
    cells = cell_products(False, fwd_off, count, place, blk_own, blk_other, pieces)
    cells = lax.all_to_all(cells, ("core", "yl", "x"), 0, 0, tiled=True)
    sums = jnp.sum(cells.reshape(2, 8, 512, 128).astype(F32), axis=1).astype(BF)
    aggregated = jnp.concatenate([sums[0], sums[1]], axis=1)

    joined = jnp.concatenate([features, aggregated], axis=1)
    pre_one = jnp.dot(joined, w_in, preferred_element_type=F32)
    act_one = jax.nn.silu(pre_one).astype(BF)
    pre_two = jnp.dot(act_one, w_mid, preferred_element_type=F32)
    act_two = jax.nn.silu(pre_two).astype(BF)
    updated = (
        features.astype(F32) + jnp.dot(act_two, w_out, preferred_element_type=F32)
    ).astype(BF)
    grad_pre_two = (
        jnp.dot(cotangent, w_out.T, preferred_element_type=F32) * silu_grad(pre_two)
    ).astype(BF)
    grad_pre_one = (
        jnp.dot(grad_pre_two, w_mid.T, preferred_element_type=F32) * silu_grad(pre_one)
    ).astype(BF)
    grad_joined = jnp.dot(grad_pre_one, w_in.T, preferred_element_type=F32)
    direct = cotangent.astype(F32) + grad_joined[:, :256]
    grad_agg = grad_joined[:, 256:].astype(BF)

    pieces = send_steps([halves(grad_agg, core)] * 8, COL)
    operands = (joined, act_one, cotangent, grad_pre_one, grad_pre_two, act_two)
    grad_in, grad_mid, grad_out = sum_grads(core, operands)
    back = cell_products(True, bwd_off, count, place, blk_own, blk_other, pieces)
    mine, yours = node_sum(send_steps(back, ("z", "yh")))
    got = lax.ppermute(yours, "core", swap).astype(F32)
    first = core == 0
    relaid = jnp.concatenate([jnp.where(first, mine, got), jnp.where(first, got, mine)], axis=1)
    grad_nodes = (direct + relaid).astype(BF)
    return updated, grad_nodes, grad_in, grad_mid, grad_out


def solution(mesh):
    fine = Mesh(mesh.devices.reshape(4, 2, 2, 2, 4), ROW + COL)
    nodes = P(ROW + COL, None)
    placed = (
        nodes,
        P(ROW, COL, None, None, None),
        P(ROW, COL, None),
        P(ROW, COL, None),
        P(ROW, COL),
        P(),
        P(),
        P(),
        nodes,
    )

    return jax.shard_map(
        shards,
        mesh=fine,
        in_specs=placed,
        out_specs=(nodes, nodes, P(), P(), P()),
        check_vma=False,
    )
```

```python
import functools

import jax
import jax.numpy as jnp
from jax import lax
from jax.experimental import pallas as pl
from jax.experimental.pallas import tpu as pltpu
from jax.experimental.layout import Layout, with_layout_constraint
from jax.sharding import Mesh, PartitionSpec as P


BF = jnp.bfloat16
F32 = jnp.float32
ROW = ("z", "yh", "core")
COL = ("yl", "x")
SLOTS = 192
SIDE = 64
CHUNK = 32
UNROLL = 8
FINISH = (
    (("m", 0), ("y", 0), ("m", 1), ("m", 3), ("y", 1), ("y", 3)),
    (("m", 2), ("y", 2)),
)
VMEM_LIMIT = 60 * 1024 * 1024


def silu_grad(value):
    sig = jax.nn.sigmoid(value)
    return sig * (1.0 + value * (1.0 - sig))


def cells_kernel(transposed, off_ref, cnt_ref, place_ref, blk0, blk1, *rest):
    pieces = rest[:8]
    out_refs = rest[8:-5]
    src, held, acc, blk_sem, src_sem = rest[-5:]
    n_chunks = SLOTS // CHUNK
    blocks = (blk0, blk1)

    def copy_of(j, ch):
        at = pl.multiple_of(ch * CHUNK, CHUNK)
        return pltpu.make_async_copy(
            blocks[j].at[pl.ds(at, CHUNK)],
            held.at[j, pl.ds(at, CHUNK)],
            blk_sem.at[j * n_chunks + ch],
        )

    moves = [
        pltpu.make_async_copy(piece, src.at[pl.ds(p * 1024, 1024)], src_sem.at[p])
        for p, piece in enumerate(pieces)
    ]
    for move in moves:
        move.start()
    used = [lax.div(cnt_ref[j] + (CHUNK - 1), CHUNK) for j in range(2)]
    for j in range(2):

        @pl.loop(0, used[j])
        def _(ch):
            copy_of(j, ch).start()

    acc[...] = jnp.zeros_like(acc)
    for move in moves:
        move.wait()
    dims = (((0,), (0,)), ((), ())) if transposed else (((1,), (0,)), ((), ()))
    for j in range(2):
        count = cnt_ref[j]

        @pl.loop(0, used[j])
        def _(ch):
            copy_of(j, ch).wait()
            left = jnp.minimum(count - ch * CHUNK, CHUNK)

            @pl.loop(0, lax.div(left + (UNROLL - 1), UNROLL))
            def _(step):
                base = ch * CHUNK + step * UNROLL
                for u in range(UNROLL):
                    slot = base + u
                    take = pl.multiple_of(off_ref[j * SLOTS + slot], SIDE)
                    put = pl.multiple_of(off_ref[(2 + j) * SLOTS + slot], SIDE)
                    term = lax.dot_general(
                        held[j, slot],
                        src[pl.ds(take, SIDE), :],
                        dims,
                        preferred_element_type=F32,
                    )
                    acc[pl.ds(put, SIDE), :] += term

    if len(out_refs) == 1:
        out_refs[0][...] = acc[: 16 * 512, :].astype(BF).reshape(out_refs[0].shape)
    else:
        for p, out_ref in enumerate(out_refs):
            for h in range(2):
                at = pl.multiple_of(place_ref[2 * p + h], 512)
                out_ref[h * 512 : (h + 1) * 512, :] = acc[pl.ds(at, 512), :].astype(BF)


def cell_products(transposed, offsets, counts, place, blk_own, blk_other, pieces):
    any_spec = pl.BlockSpec(memory_space=pl.ANY)
    smem = pl.BlockSpec(memory_space=pltpu.SMEM)
    n_chunks = SLOTS // CHUNK
    return pl.pallas_call(
        functools.partial(cells_kernel, transposed),
        out_shape=(jax.ShapeDtypeStruct((1024, 128), BF),) * 8
        if transposed
        else jax.ShapeDtypeStruct((16, 512, 128), BF),
        in_specs=[smem] * 3 + [any_spec] * 10,
        out_specs=(pl.BlockSpec(memory_space=pltpu.VMEM),) * 8
        if transposed
        else pl.BlockSpec(memory_space=pltpu.VMEM),
        scratch_shapes=[
            pltpu.VMEM((8192, 128), BF),
            pltpu.VMEM((2, SLOTS, SIDE, SIDE), BF),
            pltpu.VMEM((8192 + SIDE, 128), F32),
            pltpu.SemaphoreType.DMA((2 * n_chunks,)),
            pltpu.SemaphoreType.DMA((8,)),
        ],
        compiler_params=pltpu.CompilerParams(vmem_limit_bytes=VMEM_LIMIT),
        cost_estimate=pl.CostEstimate(
            flops=2 * 2 * SLOTS * SIDE * SIDE * 128, bytes_accessed=10 << 20, transcendentals=0
        ),
        name="cells_back" if transposed else "cells_forward",
    )(offsets, counts, place, blk_own, blk_other, *pieces)


def grads_kernel(half_ref, joined, act_one, cot, gp_one, gp_two, act_two, sum_ref):
    at = pl.multiple_of(half_ref[0] * 512, 512)
    sides = ((joined, gp_one, 0, 512), (act_one, gp_two, 512, 1024), (cot, act_two, 1536, 256))
    for left, right, row, size in sides:
        for part in range(0, size, 256):
            sum_ref[row + part : row + part + 256, :] = lax.dot_general(
                left[:, part : part + 256],
                right[:, pl.ds(at, 512)],
                (((0,), (0,)), ((), ())),
                preferred_element_type=F32,
            ).astype(BF)


def local_grads(half, *operands):
    vm = pl.BlockSpec(memory_space=pltpu.VMEM)
    return pl.pallas_call(
        grads_kernel,
        out_shape=jax.ShapeDtypeStruct((1792, 512), BF),
        in_specs=[pl.BlockSpec(memory_space=pltpu.SMEM)] + [vm] * 6,
        out_specs=vm,
        compiler_params=pltpu.CompilerParams(vmem_limit_bytes=VMEM_LIMIT),
        cost_estimate=pl.CostEstimate(
            flops=512 * 1792 * 1024, bytes_accessed=8 << 20, transcendentals=0
        ),
    )(half.reshape(1), *operands)


def chip_kernel(own, got, out_ref):
    for row in range(16):
        rows = slice(row * 112, (row + 1) * 112)
        for lane in range(4):
            lanes = slice(lane * 128, (lane + 1) * 128)
            out_ref[row * 4 + lane] = (
                own[rows, lanes].astype(F32) + got[rows, lanes].astype(F32)
            ).astype(BF)


def chip_sum(own, got):
    vm = pl.BlockSpec(memory_space=pltpu.VMEM)
    return pl.pallas_call(
        chip_kernel,
        out_shape=jax.ShapeDtypeStruct((64, 112, 128), BF),
        in_specs=[vm, vm],
        out_specs=vm,
        cost_estimate=pl.CostEstimate(flops=1 << 20, bytes_accessed=6 << 20, transcendentals=0),
        name="chip_sum",
    )(own, got)


def chunk_kernel(parts, out_ref):
    total = jnp.sum(parts[...].astype(F32), axis=0).astype(BF)
    for k in range(16):
        out_ref[k] = total


def chunk_sum(parts):
    vm = pl.BlockSpec(memory_space=pltpu.VMEM)
    return pl.pallas_call(
        chunk_kernel,
        out_shape=jax.ShapeDtypeStruct((16, 112, 128), BF),
        in_specs=[vm],
        out_specs=vm,
        cost_estimate=pl.CostEstimate(flops=1 << 20, bytes_accessed=1 << 20, transcendentals=0),
        name="chunk_sum",
    )(parts)


def ring_shift(value, axis, k):
    return lax.ppermute(value, axis, [(i, (i + k) % 4) for i in range(4)])


def flip(value, axis):
    return lax.ppermute(value, axis, [(0, 1), (1, 0)])


def gather_steps(value, ring, pair):
    got = [value] * 8
    got[1] = flip(value, pair)
    for small in range(2):
        for big in (2, 1, 3):
            p = 2 * big + small
            got[p] = ring_shift(got[small], ring, big)
    return got


def pair_kernel(*refs):
    total = refs[0][...].astype(F32)
    for ref in refs[1:-1]:
        total = total + ref[...].astype(F32)
    refs[-1][...] = total.astype(BF)


def pair_sum(parts):
    vm = pl.BlockSpec(memory_space=pltpu.VMEM)
    return pl.pallas_call(
        pair_kernel,
        out_shape=jax.ShapeDtypeStruct((1024, 128), BF),
        in_specs=[vm] * len(parts),
        out_specs=vm,
        cost_estimate=pl.CostEstimate(flops=1 << 19, bytes_accessed=5 << 18, transcendentals=0),
        name="pair_sum",
    )(*parts)


def scatter_steps(pieces, ring, pair):
    far, near = [pieces[1]], [pieces[0]]
    for small, got in ((1, far), (0, near)):
        for big in (2, 1, 3):
            p = 2 * big + small
            got.append(ring_shift(pieces[p], ring, big))
    far = pair_sum(far)
    return near + [flip(far, pair)]


def node_kernel(*refs):
    mine_ref, yours_ref = refs[-2:]
    for rows, out_ref in ((slice(0, 512), mine_ref), (slice(512, 1024), yours_ref)):
        total = refs[0][rows, :].astype(F32)
        for ref in refs[1:-2]:
            total = total + ref[rows, :].astype(F32)
        out_ref[...] = total.astype(out_ref.dtype)


def node_sum(parts):
    vm = pl.BlockSpec(memory_space=pltpu.VMEM)
    return pl.pallas_call(
        node_kernel,
        out_shape=(
            jax.ShapeDtypeStruct((512, 128), F32),
            jax.ShapeDtypeStruct((512, 128), BF),
        ),
        in_specs=[vm] * len(parts),
        out_specs=(vm, vm),
        cost_estimate=pl.CostEstimate(flops=1 << 20, bytes_accessed=3 << 20, transcendentals=0),
        name="node_sum",
    )(*parts)


def halves(value, core):
    left, right = value[:, :128], value[:, 128:]
    first = core == 0
    mine = jnp.where(first, left, right)
    yours = jnp.where(first, right, left)
    got = lax.ppermute(yours, "core", [(0, 1), (1, 0)])
    return jnp.concatenate([mine, got], axis=0)


def finish_kernel(n, lane_ref, *rest):
    pieces, rest = rest[:n], rest[-9:]
    outs = rest[:3]
    taken, first, second, third, in_sem, out_sem = rest[3:9]
    reads = [
        pltpu.make_async_copy(piece, taken.at[k], in_sem.at[k]) for k, piece in enumerate(pieces)
    ]
    for read in reads:
        read.start()
    writes = []
    for k in range(n):
        lane = pl.multiple_of(lane_ref[k], 128)
        held = (first.at[k], second.at[k], third.at[k])
        targets = (
            outs[0].at[:, pl.ds(lane, 128)],
            outs[1].at[:, pl.ds(lane, 128)],
            outs[2].at[pl.ds(lane, 128), :],
        )
        moves = [
            pltpu.make_async_copy(held[i], targets[i], out_sem.at[3 * k + i]) for i in range(3)
        ]
        reads[k].wait()
        first[k] = taken[k, :512, :].astype(F32) * (1.0 / 256.0)
        moves[0].start()
        second[k] = taken[k, 512:1536, :].astype(F32) * (1.0 / 256.0)
        moves[1].start()
        third[k] = (taken[k, 1536:, :].astype(F32) * (1.0 / 256.0)).T
        moves[2].start()
        writes += moves
    for write in writes:
        write.wait()


def finish_grads(lanes, pieces, outs):
    any_spec = pl.BlockSpec(memory_space=pl.ANY)
    n = len(pieces)
    return pl.pallas_call(
        functools.partial(finish_kernel, n),
        out_shape=(
            jax.ShapeDtypeStruct((512, 1024), F32),
            jax.ShapeDtypeStruct((1024, 1024), F32),
            jax.ShapeDtypeStruct((1024, 256), F32),
        ),
        in_specs=[pl.BlockSpec(memory_space=pltpu.SMEM)] + [any_spec] * (n + len(outs)),
        out_specs=(any_spec,) * 3,
        scratch_shapes=[
            pltpu.VMEM((n, 1792, 128), BF),
            pltpu.VMEM((n, 512, 128), F32),
            pltpu.VMEM((n, 1024, 128), F32),
            pltpu.VMEM((n, 128, 256), F32),
            pltpu.SemaphoreType.DMA((n,)),
            pltpu.SemaphoreType.DMA((3 * n,)),
        ],
        input_output_aliases={1 + n + k: k for k in range(len(outs))},
        cost_estimate=pl.CostEstimate(flops=n << 20, bytes_accessed=n << 20, transcendentals=0),
        name="finish_grads",
    )(lanes, *pieces, *outs)


def sum_grads(core, operands):
    x = lax.axis_index("x")
    swap = [(0, 1), (1, 0)]
    other = local_grads(1 - core, *operands)
    got = lax.ppermute(other, "core", swap)
    own = local_grads(core, *operands)
    parts = lax.all_to_all(chip_sum(own, got), ("z", "yh", "yl", "x"), 0, 0, tiled=True)
    chunk = chunk_sum(parts)
    lanes = lax.all_to_all(chunk, ("z", "yh", "yl"), 0, 0, tiled=True)
    lanes = lanes.reshape(1792, 128)
    mine, yours = [lanes], []
    for k in range(1, 4):
        mine.append(lax.ppermute(lanes, "x", [(i, (i + k) % 4) for i in range(4)]))
    for k in range(4):
        yours.append(lax.ppermute(mine[k], "core", swap))
    place = ((x - jnp.arange(4, dtype=jnp.int32)) & 3) * 128
    at_mine, at_yours = core * 512 + place, (1 - core) * 512 + place
    outs = ()
    for order in FINISH:
        lanes = jnp.stack([(at_mine if side == "m" else at_yours)[k] for side, k in order])
        pieces = [(mine if side == "m" else yours)[k] for side, k in order]
        outs = finish_grads(lanes, pieces, outs)
    return outs


def shards(features, blocks, block_rows, block_cols, block_count, w_in, w_mid, w_out, cotangent):
    core = lax.axis_index("core")
    z, yh = lax.axis_index("z"), lax.axis_index("yh")
    yl, x = lax.axis_index("yl"), lax.axis_index("x")
    swap = [(0, 1), (1, 0)]
    blk_own = blocks[0, 0].transpose(1, 2, 0)
    meta = jnp.concatenate(
        [block_rows[0, 0], block_cols[0, 0], jnp.broadcast_to(block_count[0, 0], (128,))]
    )
    meta_other = lax.ppermute(meta, "core", swap)
    blk_other = lax.ppermute(blk_own, "core", swap)

    both = jnp.stack([meta, meta_other])
    rows, cols, count = both[:, :SLOTS], both[:, SLOTS : 2 * SLOTS], both[:, 2 * SLOTS]
    live = jnp.arange(SLOTS, dtype=jnp.int32)[None, :] < count[:, None]
    cell_core = jnp.stack([core, 1 - core])[:, None]
    spare = 16 * 512
    grp = cols >> 3
    step = (((z - (grp >> 2)) & 3) * 2) + (((grp >> 1) & 1) ^ yh)
    col_at = step * 1024 + ((grp & 1) ^ core) * 512 + (cols & 7) * SIDE
    row_to = jnp.where(live, cell_core * 4096 + rows * SIDE, spare)
    fwd_off = jnp.concatenate([col_at, row_to]).reshape(4 * SLOTS)
    own8 = rows >> 3
    step = (((x - own8) & 3) * 2) + ((own8 >> 2) ^ yl)
    row_at = step * 1024 + jnp.arange(2, dtype=jnp.int32)[:, None] * 512 + (rows & 7) * SIDE
    col_to = jnp.where(live, cols * SIDE, spare)
    bwd_off = jnp.concatenate([row_at, col_to]).reshape(4 * SLOTS)

    p = jnp.arange(16, dtype=jnp.int32)
    place = (((z + (p >> 2)) & 3) * 4 + (yh ^ ((p >> 1) & 1)) * 2 + (core ^ (p & 1))) * 512
    shard = halves(features, core)
    pieces = gather_steps(shard, "z", "yh")
    blk_own, _ = lax.optimization_barrier((blk_own, shard))
    blk_own = with_layout_constraint(blk_own, Layout((0, 1, 2))).transpose(2, 0, 1)
    blk_other = blk_other.transpose(2, 0, 1)
    cells = cell_products(False, fwd_off, count, place, blk_own, blk_other, pieces)
    cells = lax.all_to_all(cells, ("core", "yl", "x"), 0, 0, tiled=True)
    sums = jnp.sum(cells.reshape(2, 8, 512, 128).astype(F32), axis=1).astype(BF)
    aggregated = jnp.concatenate([sums[0], sums[1]], axis=1)

    joined = jnp.concatenate([features, aggregated], axis=1)
    pre_one = jnp.dot(joined, w_in, preferred_element_type=F32)
    act_one = jax.nn.silu(pre_one).astype(BF)
    pre_two = jnp.dot(act_one, w_mid, preferred_element_type=F32)
    act_two = jax.nn.silu(pre_two).astype(BF)
    updated = (
        features.astype(F32) + jnp.dot(act_two, w_out, preferred_element_type=F32)
    ).astype(BF)
    grad_pre_two = (
        jnp.dot(cotangent, w_out.T, preferred_element_type=F32) * silu_grad(pre_two)
    ).astype(BF)
    grad_pre_one = (
        jnp.dot(grad_pre_two, w_mid.T, preferred_element_type=F32) * silu_grad(pre_one)
    ).astype(BF)
    grad_joined = jnp.dot(grad_pre_one, w_in.T, preferred_element_type=F32)
    direct = cotangent.astype(F32) + grad_joined[:, :256]
    grad_agg = grad_joined[:, 256:].astype(BF)

    pieces = gather_steps(halves(grad_agg, core), "x", "yl")
    operands = (joined, act_one, cotangent, grad_pre_one, grad_pre_two, act_two)
    grad_in, grad_mid, grad_out = sum_grads(core, operands)
    back = cell_products(True, bwd_off, count, place, blk_own, blk_other, pieces)
    mine, yours = node_sum(scatter_steps(back, "z", "yh"))
    got = lax.ppermute(yours, "core", swap).astype(F32)
    first = core == 0
    relaid = jnp.concatenate([jnp.where(first, mine, got), jnp.where(first, got, mine)], axis=1)
    grad_nodes = (direct + relaid).astype(BF)
    return updated, grad_nodes, grad_in, grad_mid, grad_out


def solution(mesh):
    fine = Mesh(mesh.devices.reshape(4, 2, 2, 2, 4), ROW + COL)
    nodes = P(ROW + COL, None)
    placed = (
        nodes,
        P(ROW, COL, None, None, None),
        P(ROW, COL, None),
        P(ROW, COL, None),
        P(ROW, COL),
        P(),
        P(),
        P(),
        nodes,
    )

    return jax.shard_map(
        shards,
        mesh=fine,
        in_specs=placed,
        out_specs=(nodes, nodes, P(), P(), P()),
        check_vma=False,
    )
```

```python
import functools

import jax
import jax.numpy as jnp
from jax import lax
from jax.experimental import pallas as pl
from jax.experimental.pallas import tpu as pltpu
from jax.experimental.layout import Layout, with_layout_constraint
from jax.sharding import Mesh, PartitionSpec as P


BF = jnp.bfloat16
F32 = jnp.float32
ROW = ("z", "yh", "core")
COL = ("yl", "x")
SLOTS = 192
SIDE = 64
CHUNK = 32
UNROLL = 32
FINISH = (
    (("m", 0), ("y", 0), ("m", 1), ("m", 3)),
    (("y", 1), ("y", 3), ("m", 2), ("y", 2)),
)
VMEM_LIMIT = 60 * 1024 * 1024


def silu_grad(value):
    sig = jax.nn.sigmoid(value)
    return sig * (1.0 + value * (1.0 - sig))


def cells_kernel(transposed, off_ref, cnt_ref, place_ref, blk0, blk1, *rest):
    pieces = rest[:8]
    out_refs = rest[8:-5]
    src, held, acc, blk_sem, src_sem = rest[-5:]
    n_chunks = SLOTS // CHUNK
    blocks = (blk0, blk1)

    def copy_of(j, ch):
        at = pl.multiple_of(ch * CHUNK, CHUNK)
        return pltpu.make_async_copy(
            blocks[j].at[pl.ds(at, CHUNK)],
            held.at[j, pl.ds(at, CHUNK)],
            blk_sem.at[j * n_chunks + ch],
        )

    moves = [
        pltpu.make_async_copy(piece, src.at[pl.ds(p * 1024, 1024)], src_sem.at[p])
        for p, piece in enumerate(pieces)
    ]
    for move in moves:
        move.start()
    used = [lax.div(cnt_ref[j] + (CHUNK - 1), CHUNK) for j in range(2)]
    for j in range(2):

        @pl.loop(0, used[j])
        def _(ch):
            copy_of(j, ch).start()

    acc[...] = jnp.zeros_like(acc)
    for move in moves:
        move.wait()
    dims = (((0,), (0,)), ((), ())) if transposed else (((1,), (0,)), ((), ()))
    for j in range(2):
        count = cnt_ref[j]

        @pl.loop(0, used[j])
        def _(ch):
            copy_of(j, ch).wait()
            left = jnp.minimum(count - ch * CHUNK, CHUNK)

            @pl.loop(0, lax.div(left + (UNROLL - 1), UNROLL))
            def _(step):
                base = ch * CHUNK + step * UNROLL
                for u in range(UNROLL):
                    slot = base + u
                    take = pl.multiple_of(off_ref[j * SLOTS + slot], SIDE)
                    put = pl.multiple_of(off_ref[(2 + j) * SLOTS + slot], SIDE)
                    term = lax.dot_general(
                        held[j, slot],
                        src[pl.ds(take, SIDE), :],
                        dims,
                        preferred_element_type=F32,
                    )
                    acc[pl.ds(put, SIDE), :] += term

    if len(out_refs) == 1:
        out_refs[0][...] = acc[: 16 * 512, :].astype(BF).reshape(out_refs[0].shape)
    else:
        for p, out_ref in enumerate(out_refs):
            for h in range(2):
                at = pl.multiple_of(place_ref[2 * p + h], 512)
                out_ref[h * 512 : (h + 1) * 512, :] = acc[pl.ds(at, 512), :].astype(BF)


def cell_products(transposed, offsets, counts, place, blk_own, blk_other, pieces):
    any_spec = pl.BlockSpec(memory_space=pl.ANY)
    smem = pl.BlockSpec(memory_space=pltpu.SMEM)
    n_chunks = SLOTS // CHUNK
    return pl.pallas_call(
        functools.partial(cells_kernel, transposed),
        out_shape=(jax.ShapeDtypeStruct((1024, 128), BF),) * 8
        if transposed
        else jax.ShapeDtypeStruct((16, 512, 128), BF),
        in_specs=[smem] * 3 + [any_spec] * 10,
        out_specs=(pl.BlockSpec(memory_space=pltpu.VMEM),) * 8
        if transposed
        else pl.BlockSpec(memory_space=pltpu.VMEM),
        scratch_shapes=[
            pltpu.VMEM((8192, 128), BF),
            pltpu.VMEM((2, SLOTS, SIDE, SIDE), BF),
            pltpu.VMEM((8192 + SIDE, 128), F32),
            pltpu.SemaphoreType.DMA((2 * n_chunks,)),
            pltpu.SemaphoreType.DMA((8,)),
        ],
        compiler_params=pltpu.CompilerParams(vmem_limit_bytes=VMEM_LIMIT),
        cost_estimate=pl.CostEstimate(
            flops=2 * 2 * SLOTS * SIDE * SIDE * 128, bytes_accessed=10 << 20, transcendentals=0
        ),
        name="cells_back" if transposed else "cells_forward",
    )(offsets, counts, place, blk_own, blk_other, *pieces)


def grads_kernel(half_ref, joined, act_one, cot, gp_one, gp_two, act_two, sum_ref):
    at = pl.multiple_of(half_ref[0] * 512, 512)
    sides = ((joined, gp_one, 0, 512), (act_one, gp_two, 512, 1024), (cot, act_two, 1536, 256))
    for left, right, row, size in sides:
        for part in range(0, size, 256):
            sum_ref[row + part : row + part + 256, :] = lax.dot_general(
                left[:, part : part + 256],
                right[:, pl.ds(at, 512)],
                (((0,), (0,)), ((), ())),
                preferred_element_type=F32,
            ).astype(BF)


def local_grads(half, *operands):
    vm = pl.BlockSpec(memory_space=pltpu.VMEM)
    return pl.pallas_call(
        grads_kernel,
        out_shape=jax.ShapeDtypeStruct((1792, 512), BF),
        in_specs=[pl.BlockSpec(memory_space=pltpu.SMEM)] + [vm] * 6,
        out_specs=vm,
        compiler_params=pltpu.CompilerParams(vmem_limit_bytes=VMEM_LIMIT),
        cost_estimate=pl.CostEstimate(
            flops=512 * 1792 * 1024, bytes_accessed=8 << 20, transcendentals=0
        ),
    )(half.reshape(1), *operands)


def chip_kernel(own, got, out_ref):
    for row in range(4):
        rows = slice(row * 112, (row + 1) * 112)
        for lane in range(4):
            lanes = slice(lane * 128, (lane + 1) * 128)
            out_ref[row * 4 + lane] = (
                own[rows, lanes].astype(F32) + got[rows, lanes].astype(F32)
            ).astype(BF)


def chip_sum(own, got):
    rows = pl.BlockSpec((448, 512), lambda i: (i, 0))
    return pl.pallas_call(
        chip_kernel,
        grid=(4,),
        out_shape=jax.ShapeDtypeStruct((64, 112, 128), BF),
        in_specs=[rows, rows],
        out_specs=pl.BlockSpec((16, 112, 128), lambda i: (i, 0, 0)),
        cost_estimate=pl.CostEstimate(flops=1 << 20, bytes_accessed=6 << 20, transcendentals=0),
        name="chip_sum",
    )(own, got)


def chunk_kernel(parts, out_ref):
    total = jnp.sum(parts[...].astype(F32), axis=0).astype(BF)
    for k in range(16):
        out_ref[k] = total


def chunk_sum(parts):
    vm = pl.BlockSpec(memory_space=pltpu.VMEM)
    return pl.pallas_call(
        chunk_kernel,
        out_shape=jax.ShapeDtypeStruct((16, 112, 128), BF),
        in_specs=[vm],
        out_specs=vm,
        cost_estimate=pl.CostEstimate(flops=1 << 20, bytes_accessed=1 << 20, transcendentals=0),
        name="chunk_sum",
    )(parts)


def ring_shift(value, axis, k):
    return lax.ppermute(value, axis, [(i, (i + k) % 4) for i in range(4)])


def flip(value, axis):
    return lax.ppermute(value, axis, [(0, 1), (1, 0)])


def gather_steps(value, ring, pair):
    got = [value] * 8
    got[1] = flip(value, pair)
    for small in range(2):
        for big in (2, 1, 3):
            p = 2 * big + small
            got[p] = ring_shift(got[small], ring, big)
    return got


def pair_kernel(*refs):
    total = refs[0][...].astype(F32)
    for ref in refs[1:-1]:
        total = total + ref[...].astype(F32)
    refs[-1][...] = total.astype(BF)


def pair_sum(parts):
    vm = pl.BlockSpec(memory_space=pltpu.VMEM)
    return pl.pallas_call(
        pair_kernel,
        out_shape=jax.ShapeDtypeStruct((1024, 128), BF),
        in_specs=[vm] * len(parts),
        out_specs=vm,
        cost_estimate=pl.CostEstimate(flops=1 << 19, bytes_accessed=5 << 18, transcendentals=0),
        name="pair_sum",
    )(*parts)


def scatter_steps(pieces, ring, pair):
    far, near = [pieces[1]], [pieces[0]]
    for small, got in ((1, far), (0, near)):
        for big in (2, 1, 3):
            p = 2 * big + small
            got.append(ring_shift(pieces[p], ring, big))
    far = pair_sum(far)
    return near + [flip(far, pair)]


def node_kernel(*refs):
    mine_ref, yours_ref = refs[-2:]
    for rows, out_ref in ((slice(0, 512), mine_ref), (slice(512, 1024), yours_ref)):
        total = refs[0][rows, :].astype(F32)
        for ref in refs[1:-2]:
            total = total + ref[rows, :].astype(F32)
        out_ref[...] = total.astype(out_ref.dtype)


def node_sum(parts):
    vm = pl.BlockSpec(memory_space=pltpu.VMEM)
    return pl.pallas_call(
        node_kernel,
        out_shape=(
            jax.ShapeDtypeStruct((512, 128), F32),
            jax.ShapeDtypeStruct((512, 128), BF),
        ),
        in_specs=[vm] * len(parts),
        out_specs=(vm, vm),
        cost_estimate=pl.CostEstimate(flops=1 << 20, bytes_accessed=3 << 20, transcendentals=0),
        name="node_sum",
    )(*parts)


def halves(value, core):
    left, right = value[:, :128], value[:, 128:]
    first = core == 0
    mine = jnp.where(first, left, right)
    yours = jnp.where(first, right, left)
    got = lax.ppermute(yours, "core", [(0, 1), (1, 0)])
    return jnp.concatenate([mine, got], axis=0)


def finish_kernel(n, lane_ref, *rest):
    pieces, rest = rest[:n], rest[-9:]
    outs = rest[:3]
    taken, first, second, third, in_sem, out_sem = rest[3:9]
    reads = [
        pltpu.make_async_copy(piece, taken.at[k], in_sem.at[k]) for k, piece in enumerate(pieces)
    ]
    for read in reads:
        read.start()
    writes = []
    for k in range(n):
        lane = pl.multiple_of(lane_ref[k], 128)
        held = (first.at[k], second.at[k], third.at[k])
        targets = (
            outs[0].at[:, pl.ds(lane, 128)],
            outs[1].at[:, pl.ds(lane, 128)],
            outs[2].at[pl.ds(lane, 128), :],
        )
        moves = [
            pltpu.make_async_copy(held[i], targets[i], out_sem.at[3 * k + i]) for i in range(3)
        ]
        reads[k].wait()
        first[k] = taken[k, :512, :].astype(F32) * (1.0 / 256.0)
        moves[0].start()
        second[k] = taken[k, 512:1536, :].astype(F32) * (1.0 / 256.0)
        moves[1].start()
        third[k] = (taken[k, 1536:, :].astype(F32) * (1.0 / 256.0)).T
        moves[2].start()
        writes += moves
    for write in writes:
        write.wait()


def finish_grads(lanes, pieces, outs):
    any_spec = pl.BlockSpec(memory_space=pl.ANY)
    n = len(pieces)
    return pl.pallas_call(
        functools.partial(finish_kernel, n),
        out_shape=(
            jax.ShapeDtypeStruct((512, 1024), F32),
            jax.ShapeDtypeStruct((1024, 1024), F32),
            jax.ShapeDtypeStruct((1024, 256), F32),
        ),
        in_specs=[pl.BlockSpec(memory_space=pltpu.SMEM)] + [any_spec] * (n + len(outs)),
        out_specs=(any_spec,) * 3,
        scratch_shapes=[
            pltpu.VMEM((n, 1792, 128), BF),
            pltpu.VMEM((n, 512, 128), F32),
            pltpu.VMEM((n, 1024, 128), F32),
            pltpu.VMEM((n, 128, 256), F32),
            pltpu.SemaphoreType.DMA((n,)),
            pltpu.SemaphoreType.DMA((3 * n,)),
        ],
        input_output_aliases={1 + n + k: k for k in range(len(outs))},
        cost_estimate=pl.CostEstimate(flops=n << 20, bytes_accessed=n << 20, transcendentals=0),
        name="finish_grads",
    )(lanes, *pieces, *outs)


def sum_grads(core, operands):
    x = lax.axis_index("x")
    swap = [(0, 1), (1, 0)]
    other = local_grads(1 - core, *operands)
    got = lax.ppermute(other, "core", swap)
    own = local_grads(core, *operands)
    parts = lax.all_to_all(chip_sum(own, got), ("z", "yh", "yl", "x"), 0, 0, tiled=True)
    chunk = chunk_sum(parts)
    lanes = lax.all_to_all(chunk, ("z", "yh", "yl"), 0, 0, tiled=True)
    lanes = lanes.reshape(1792, 128)
    mine, yours = [lanes], []
    for k in range(1, 4):
        mine.append(lax.ppermute(lanes, "x", [(i, (i + k) % 4) for i in range(4)]))
    for k in range(4):
        yours.append(lax.ppermute(mine[k], "core", swap))
    outs = ()
    for order in FINISH:
        steps = jnp.array([k for _, k in order], jnp.int32)
        other_core = jnp.array([side == "y" for side, _ in order], jnp.int32)
        lanes = (core ^ other_core) * 512 + ((x - steps) & 3) * 128
        pieces = [(mine if side == "m" else yours)[k] for side, k in order]
        outs = finish_grads(lanes, pieces, outs)
    return outs


def shards(features, blocks, block_rows, block_cols, block_count, w_in, w_mid, w_out, cotangent):
    core = lax.axis_index("core")
    z, yh = lax.axis_index("z"), lax.axis_index("yh")
    yl, x = lax.axis_index("yl"), lax.axis_index("x")
    swap = [(0, 1), (1, 0)]
    blk_own = blocks[0, 0].transpose(1, 2, 0)
    shard = halves(features, core)
    slots, _ = lax.optimization_barrier(((block_rows, block_cols, block_count), shard))
    meta = jnp.concatenate(
        [slots[0][0, 0], slots[1][0, 0], jnp.broadcast_to(slots[2][0, 0], (128,))]
    )
    meta_other = lax.ppermute(meta, "core", swap)
    blk_other = lax.ppermute(blk_own, "core", swap)

    both = jnp.stack([meta, meta_other])
    rows, cols, count = both[:, :SLOTS], both[:, SLOTS : 2 * SLOTS], both[:, 2 * SLOTS]
    live = jnp.arange(SLOTS, dtype=jnp.int32)[None, :] < count[:, None]
    cell_core = jnp.stack([core, 1 - core])[:, None]
    spare = 16 * 512
    grp = cols >> 3
    step = (((z - (grp >> 2)) & 3) * 2) + (((grp >> 1) & 1) ^ yh)
    col_at = step * 1024 + ((grp & 1) ^ core) * 512 + (cols & 7) * SIDE
    row_to = jnp.where(live, cell_core * 4096 + rows * SIDE, spare)
    fwd_off = jnp.concatenate([col_at, row_to]).reshape(4 * SLOTS)
    own8 = rows >> 3
    step = (((x - own8) & 3) * 2) + ((own8 >> 2) ^ yl)
    row_at = step * 1024 + jnp.arange(2, dtype=jnp.int32)[:, None] * 512 + (rows & 7) * SIDE
    col_to = jnp.where(live, cols * SIDE, spare)
    bwd_off = jnp.concatenate([row_at, col_to]).reshape(4 * SLOTS)

    p = jnp.arange(16, dtype=jnp.int32)
    place = (((z + (p >> 2)) & 3) * 4 + (yh ^ ((p >> 1) & 1)) * 2 + (core ^ (p & 1))) * 512
    pieces = gather_steps(shard, "z", "yh")
    blk_own, _ = lax.optimization_barrier((blk_own, shard))
    blk_own = with_layout_constraint(blk_own, Layout((0, 1, 2))).transpose(2, 0, 1)
    blk_other = blk_other.transpose(2, 0, 1)
    cells = cell_products(False, fwd_off, count, place, blk_own, blk_other, pieces)
    cells = lax.all_to_all(cells, ("core", "yl", "x"), 0, 0, tiled=True)
    sums = jnp.sum(cells.reshape(2, 8, 512, 128).astype(F32), axis=1).astype(BF)
    aggregated = jnp.concatenate([sums[0], sums[1]], axis=1)

    joined = jnp.concatenate([features, aggregated], axis=1)
    pre_one = jnp.dot(joined, w_in, preferred_element_type=F32)
    act_one = jax.nn.silu(pre_one).astype(BF)
    pre_two = jnp.dot(act_one, w_mid, preferred_element_type=F32)
    act_two = jax.nn.silu(pre_two).astype(BF)
    updated = (
        features.astype(F32) + jnp.dot(act_two, w_out, preferred_element_type=F32)
    ).astype(BF)
    grad_pre_two = (
        jnp.dot(cotangent, w_out.T, preferred_element_type=F32) * silu_grad(pre_two)
    ).astype(BF)
    grad_pre_one = (
        jnp.dot(grad_pre_two, w_mid.T, preferred_element_type=F32) * silu_grad(pre_one)
    ).astype(BF)
    grad_joined = jnp.dot(grad_pre_one, w_in.T, preferred_element_type=F32)
    direct = cotangent.astype(F32) + grad_joined[:, :256]
    grad_agg = grad_joined[:, 256:].astype(BF)

    pieces = gather_steps(halves(grad_agg, core), "x", "yl")
    operands = (joined, act_one, cotangent, grad_pre_one, grad_pre_two, act_two)
    grad_in, grad_mid, grad_out = sum_grads(core, operands)
    back = cell_products(True, bwd_off, count, place, blk_own, blk_other, pieces)
    mine, yours = node_sum(scatter_steps(back, "z", "yh"))
    got = lax.ppermute(yours, "core", swap).astype(F32)
    first = core == 0
    relaid = jnp.concatenate([jnp.where(first, mine, got), jnp.where(first, got, mine)], axis=1)
    grad_nodes = (direct + relaid).astype(BF)
    return updated, grad_nodes, grad_in, grad_mid, grad_out


def solution(mesh):
    fine = Mesh(mesh.devices.reshape(4, 2, 2, 2, 4), ROW + COL)
    nodes = P(ROW + COL, None)
    placed = (
        nodes,
        P(ROW, COL, None, None, None),
        P(ROW, COL, None),
        P(ROW, COL, None),
        P(ROW, COL),
        P(),
        P(),
        P(),
        nodes,
    )

    return jax.shard_map(
        shards,
        mesh=fine,
        in_specs=placed,
        out_specs=(nodes, nodes, P(), P(), P()),
        check_vma=False,
    )
```

```python
import functools

import jax
import jax.numpy as jnp
from jax import lax
from jax.experimental import pallas as pl
from jax.experimental.pallas import tpu as pltpu
from jax.experimental.layout import Layout, with_layout_constraint
from jax.sharding import Mesh, PartitionSpec as P


BF = jnp.bfloat16
F32 = jnp.float32
ROW = ("z", "yh", "core")
COL = ("yl", "x")
SLOTS = 192
SIDE = 64
CHUNK = 32
UNROLL = 32
CELL_VMEM = 28 << 20


def silu_grad(value):
    sig = jax.nn.sigmoid(value)
    return sig * (1.0 + value * (1.0 - sig))


def cells_kernel(transposed, off_ref, cnt_ref, place_ref, blk0, blk1, *rest):
    pieces = rest[:8]
    out_refs = rest[8:-5]
    src, held, acc, blk_sem, src_sem = rest[-5:]
    n_chunks = SLOTS // CHUNK
    blocks = (blk0, blk1)

    def copy_of(j, ch):
        at = pl.multiple_of(ch * CHUNK, CHUNK)
        return pltpu.make_async_copy(
            blocks[j].at[pl.ds(at, CHUNK)],
            held.at[j, pl.ds(at, CHUNK)],
            blk_sem.at[j * n_chunks + ch],
        )

    moves = [
        pltpu.make_async_copy(piece, src.at[pl.ds(p * 1024, 1024)], src_sem.at[p])
        for p, piece in enumerate(pieces)
    ]
    for move in moves:
        move.start()
    used = [lax.div(cnt_ref[j] + (CHUNK - 1), CHUNK) for j in range(2)]
    for j in range(2):

        @pl.loop(0, used[j])
        def _(ch):
            copy_of(j, ch).start()

    acc[...] = jnp.zeros_like(acc)
    for move in moves:
        move.wait()
    dims = (((0,), (0,)), ((), ())) if transposed else (((1,), (0,)), ((), ()))
    for j in range(2):
        count = cnt_ref[j]

        @pl.loop(0, used[j])
        def _(ch):
            copy_of(j, ch).wait()
            left = jnp.minimum(count - ch * CHUNK, CHUNK)

            @pl.loop(0, lax.div(left + (UNROLL - 1), UNROLL))
            def _(step):
                base = ch * CHUNK + step * UNROLL
                for u in range(UNROLL):
                    slot = base + u
                    take = pl.multiple_of(off_ref[j * SLOTS + slot], SIDE)
                    put = pl.multiple_of(off_ref[(2 + j) * SLOTS + slot], SIDE)
                    term = lax.dot_general(
                        held[j, slot],
                        src[pl.ds(take, SIDE), :],
                        dims,
                        preferred_element_type=F32,
                    )
                    acc[pl.ds(put, SIDE), :] += term

    if len(out_refs) == 1:
        out_refs[0][...] = acc[: 16 * 512, :].astype(BF).reshape(out_refs[0].shape)
    else:
        for p, out_ref in enumerate(out_refs):
            for h in range(2):
                at = pl.multiple_of(place_ref[2 * p + h], 512)
                out_ref[h * 512 : (h + 1) * 512, :] = acc[pl.ds(at, 512), :].astype(BF)


def cell_products(transposed, offsets, counts, place, blk_own, blk_other, pieces):
    any_spec = pl.BlockSpec(memory_space=pl.ANY)
    smem = pl.BlockSpec(memory_space=pltpu.SMEM)
    n_chunks = SLOTS // CHUNK
    return pl.pallas_call(
        functools.partial(cells_kernel, transposed),
        out_shape=(jax.ShapeDtypeStruct((1024, 128), BF),) * 8
        if transposed
        else jax.ShapeDtypeStruct((16, 512, 128), BF),
        in_specs=[smem] * 3 + [any_spec] * 10,
        out_specs=(pl.BlockSpec(memory_space=pltpu.VMEM),) * 8
        if transposed
        else pl.BlockSpec(memory_space=pltpu.VMEM),
        scratch_shapes=[
            pltpu.VMEM((8192, 128), BF),
            pltpu.VMEM((2, SLOTS, SIDE, SIDE), BF),
            pltpu.VMEM((8192 + SIDE, 128), F32),
            pltpu.SemaphoreType.DMA((2 * n_chunks,)),
            pltpu.SemaphoreType.DMA((8,)),
        ],
        compiler_params=pltpu.CompilerParams(vmem_limit_bytes=CELL_VMEM),
        cost_estimate=pl.CostEstimate(
            flops=2 * 2 * SLOTS * SIDE * SIDE * 128, bytes_accessed=10 << 20, transcendentals=0
        ),
        name="cells_back" if transposed else "cells_forward",
    )(offsets, counts, place, blk_own, blk_other, *pieces)


def grads_kernel(half_ref, joined, act_one, cot, gp_one, gp_two, act_two, sum_ref):
    at = pl.multiple_of(half_ref[0] * 512, 512)
    sides = ((joined, gp_one, 0, 512), (act_one, gp_two, 512, 1024), (cot, act_two, 1536, 256))
    for left, right, row, size in sides:
        for part in range(0, size, 256):
            sum_ref[row + part : row + part + 256, :] = lax.dot_general(
                left[:, part : part + 256],
                right[:, pl.ds(at, 512)],
                (((0,), (0,)), ((), ())),
                preferred_element_type=F32,
            ).astype(BF)


def local_grads(half, *operands):
    vm = pl.BlockSpec(memory_space=pltpu.VMEM)
    return pl.pallas_call(
        grads_kernel,
        out_shape=jax.ShapeDtypeStruct((1792, 512), BF),
        in_specs=[pl.BlockSpec(memory_space=pltpu.SMEM)] + [vm] * 6,
        out_specs=vm,
        compiler_params=pltpu.CompilerParams(vmem_limit_bytes=16 << 20),
        cost_estimate=pl.CostEstimate(
            flops=512 * 1792 * 1024, bytes_accessed=8 << 20, transcendentals=0
        ),
    )(half.reshape(1), *operands)


def chip_kernel(own, got, out_ref):
    for row in range(16):
        rows = slice(row * 112, (row + 1) * 112)
        for lane in range(4):
            lanes = slice(lane * 128, (lane + 1) * 128)
            out_ref[row * 4 + lane] = (
                own[rows, lanes].astype(F32) + got[rows, lanes].astype(F32)
            ).astype(BF)


def chip_sum(own, got):
    vm = pl.BlockSpec(memory_space=pltpu.VMEM)
    return pl.pallas_call(
        chip_kernel,
        out_shape=jax.ShapeDtypeStruct((64, 112, 128), BF),
        in_specs=[vm, vm],
        out_specs=vm,
        cost_estimate=pl.CostEstimate(flops=1 << 20, bytes_accessed=6 << 20, transcendentals=0),
        compiler_params=pltpu.CompilerParams(vmem_limit_bytes=12 << 20),
        name="chip_sum",
    )(own, got)


def chunk_kernel(parts, out_ref):
    total = jnp.sum(parts[...].astype(F32), axis=0).astype(BF)
    for k in range(64):
        out_ref[k] = total


def chunk_sum(parts):
    vm = pl.BlockSpec(memory_space=pltpu.VMEM)
    return pl.pallas_call(
        chunk_kernel,
        out_shape=jax.ShapeDtypeStruct((64, 112, 128), BF),
        in_specs=[vm],
        out_specs=vm,
        cost_estimate=pl.CostEstimate(flops=1 << 20, bytes_accessed=1 << 20, transcendentals=0),
        compiler_params=pltpu.CompilerParams(vmem_limit_bytes=12 << 20),
        name="chunk_sum",
    )(parts)


def ring_shift(value, axis, k):
    return lax.ppermute(value, axis, [(i, (i + k) % 4) for i in range(4)])


def flip(value, axis):
    return lax.ppermute(value, axis, [(0, 1), (1, 0)])


def gather_steps(value, ring, pair):
    got = [value] * 8
    got[1] = flip(value, pair)
    for small in range(2):
        for big in (2, 1, 3):
            p = 2 * big + small
            got[p] = ring_shift(got[small], ring, big)
    return got


def pair_kernel(*refs):
    total = refs[0][...].astype(F32)
    for ref in refs[1:-1]:
        total = total + ref[...].astype(F32)
    refs[-1][...] = total.astype(BF)


def pair_sum(parts):
    vm = pl.BlockSpec(memory_space=pltpu.VMEM)
    return pl.pallas_call(
        pair_kernel,
        out_shape=jax.ShapeDtypeStruct((1024, 128), BF),
        in_specs=[vm] * len(parts),
        out_specs=vm,
        cost_estimate=pl.CostEstimate(flops=1 << 19, bytes_accessed=5 << 18, transcendentals=0),
        compiler_params=pltpu.CompilerParams(vmem_limit_bytes=6 << 20),
        name="pair_sum",
    )(*parts)


def scatter_steps(pieces, ring, pair):
    far, near = [pieces[1]], [pieces[0]]
    for small, got in ((1, far), (0, near)):
        for big in (2, 1, 3):
            p = 2 * big + small
            got.append(ring_shift(pieces[p], ring, big))
    far = pair_sum(far)
    return near + [flip(far, pair)]


def node_kernel(*refs):
    mine_ref, yours_ref = refs[-2:]
    for rows, out_ref in ((slice(0, 512), mine_ref), (slice(512, 1024), yours_ref)):
        total = refs[0][rows, :].astype(F32)
        for ref in refs[1:-2]:
            total = total + ref[rows, :].astype(F32)
        out_ref[...] = total.astype(out_ref.dtype)


def node_sum(parts):
    vm = pl.BlockSpec(memory_space=pltpu.VMEM)
    return pl.pallas_call(
        node_kernel,
        out_shape=(
            jax.ShapeDtypeStruct((512, 128), F32),
            jax.ShapeDtypeStruct((512, 128), BF),
        ),
        in_specs=[vm] * len(parts),
        out_specs=(vm, vm),
        cost_estimate=pl.CostEstimate(flops=1 << 20, bytes_accessed=3 << 20, transcendentals=0),
        compiler_params=pltpu.CompilerParams(vmem_limit_bytes=8 << 20),
        name="node_sum",
    )(*parts)


def halves(value, core):
    left, right = value[:, :128], value[:, 128:]
    first = core == 0
    mine = jnp.where(first, left, right)
    yours = jnp.where(first, right, left)
    got = lax.ppermute(yours, "core", [(0, 1), (1, 0)])
    return jnp.concatenate([mine, got], axis=0)


def finish_kernel(half_ref, blocks_ref, *rest):
    outs, total, turned, sems = rest[-6:-3], rest[-3], rest[-2], rest[-1]
    lane = pl.multiple_of(half_ref[0] * 512, 512)
    lanes = pl.ds(lane, 512)
    moves = (
        pltpu.make_async_copy(total.at[:512], outs[0].at[:, lanes], sems.at[0]),
        pltpu.make_async_copy(total.at[512:1536], outs[1].at[:, lanes], sems.at[1]),
        pltpu.make_async_copy(turned, outs[2].at[lanes, :], sems.at[2]),
    )
    for row in range(16):
        for col in range(4):
            total[row * 112 : (row + 1) * 112, col * 128 : (col + 1) * 128] = blocks_ref[
                row * 4 + col
            ].astype(F32) * (1.0 / 256.0)
        if row == 4:
            moves[0].start()
        if row == 13:
            moves[1].start()
    turned[...] = total[1536:, :].T
    moves[2].start()
    for move in moves:
        move.wait()


def finish_grads(half, blocks, outs):
    vm = pl.BlockSpec(memory_space=pltpu.VMEM)
    any_spec = pl.BlockSpec(memory_space=pl.ANY)
    return pl.pallas_call(
        finish_kernel,
        out_shape=(
            jax.ShapeDtypeStruct((512, 1024), F32),
            jax.ShapeDtypeStruct((1024, 1024), F32),
            jax.ShapeDtypeStruct((1024, 256), F32),
        ),
        in_specs=[pl.BlockSpec(memory_space=pltpu.SMEM), vm] + [any_spec] * len(outs),
        out_specs=(any_spec,) * 3,
        scratch_shapes=[
            pltpu.VMEM((1792, 512), F32),
            pltpu.VMEM((512, 256), F32),
            pltpu.SemaphoreType.DMA((3,)),
        ],
        input_output_aliases={2 + k: k for k in range(len(outs))},
        compiler_params=pltpu.CompilerParams(vmem_limit_bytes=16 << 20),
        cost_estimate=pl.CostEstimate(flops=4 << 20, bytes_accessed=6 << 20, transcendentals=0),
        name="finish_grads",
    )(half.reshape(1), blocks, *outs)


def sum_grads(core, operands):
    swap = [(0, 1), (1, 0)]
    other = local_grads(1 - core, *operands)
    got = lax.ppermute(other, "core", swap)
    own = local_grads(core, *operands)
    parts = lax.all_to_all(chip_sum(own, got), ("z", "yh", "yl", "x"), 0, 0, tiled=True)
    chunk = chunk_sum(parts)
    mine = lax.all_to_all(chunk, ("z", "yh", "yl", "x"), 0, 0, tiled=True)
    yours = lax.ppermute(mine, "core", swap)
    outs = finish_grads(core, mine, ())
    return finish_grads(1 - core, yours, outs)


def shards(features, blocks, block_rows, block_cols, block_count, w_in, w_mid, w_out, cotangent):
    core = lax.axis_index("core")
    z, yh = lax.axis_index("z"), lax.axis_index("yh")
    yl, x = lax.axis_index("yl"), lax.axis_index("x")
    swap = [(0, 1), (1, 0)]
    blk_own = blocks[0, 0].transpose(1, 2, 0)
    shard = halves(features, core)
    slots, _ = lax.optimization_barrier(((block_rows, block_cols, block_count), shard))
    meta = jnp.concatenate(
        [slots[0][0, 0], slots[1][0, 0], jnp.broadcast_to(slots[2][0, 0], (128,))]
    )
    meta_other = lax.ppermute(meta, "core", swap)
    blk_other = lax.ppermute(blk_own, "core", swap)

    both = jnp.stack([meta, meta_other])
    rows, cols, count = both[:, :SLOTS], both[:, SLOTS : 2 * SLOTS], both[:, 2 * SLOTS]
    live = jnp.arange(SLOTS, dtype=jnp.int32)[None, :] < count[:, None]
    cell_core = jnp.stack([core, 1 - core])[:, None]
    spare = 16 * 512
    grp = cols >> 3
    step = (((z - (grp >> 2)) & 3) * 2) + (((grp >> 1) & 1) ^ yh)
    col_at = step * 1024 + ((grp & 1) ^ core) * 512 + (cols & 7) * SIDE
    row_to = jnp.where(live, cell_core * 4096 + rows * SIDE, spare)
    fwd_off = jnp.concatenate([col_at, row_to]).reshape(4 * SLOTS)
    own8 = rows >> 3
    step = (((x - own8) & 3) * 2) + ((own8 >> 2) ^ yl)
    row_at = step * 1024 + jnp.arange(2, dtype=jnp.int32)[:, None] * 512 + (rows & 7) * SIDE
    col_to = jnp.where(live, cols * SIDE, spare)
    bwd_off = jnp.concatenate([row_at, col_to]).reshape(4 * SLOTS)

    p = jnp.arange(16, dtype=jnp.int32)
    place = (((z + (p >> 2)) & 3) * 4 + (yh ^ ((p >> 1) & 1)) * 2 + (core ^ (p & 1))) * 512
    pieces = gather_steps(shard, "z", "yh")
    blk_own, _ = lax.optimization_barrier((blk_own, shard))
    blk_own = with_layout_constraint(blk_own, Layout((0, 1, 2))).transpose(2, 0, 1)
    blk_other = blk_other.transpose(2, 0, 1)
    cells = cell_products(False, fwd_off, count, place, blk_own, blk_other, pieces)
    cells = lax.all_to_all(cells, ("core", "yl", "x"), 0, 0, tiled=True)
    sums = jnp.sum(cells.reshape(2, 8, 512, 128).astype(F32), axis=1).astype(BF)
    aggregated = jnp.concatenate([sums[0], sums[1]], axis=1)

    joined = jnp.concatenate([features, aggregated], axis=1)
    pre_one = jnp.dot(joined, w_in, preferred_element_type=F32)
    act_one = jax.nn.silu(pre_one).astype(BF)
    pre_two = jnp.dot(act_one, w_mid, preferred_element_type=F32)
    act_two = jax.nn.silu(pre_two).astype(BF)
    updated = (
        features.astype(F32) + jnp.dot(act_two, w_out, preferred_element_type=F32)
    ).astype(BF)
    grad_pre_two = (
        jnp.dot(cotangent, w_out.T, preferred_element_type=F32) * silu_grad(pre_two)
    ).astype(BF)
    grad_pre_one = (
        jnp.dot(grad_pre_two, w_mid.T, preferred_element_type=F32) * silu_grad(pre_one)
    ).astype(BF)
    grad_joined = jnp.dot(grad_pre_one, w_in.T, preferred_element_type=F32)
    direct = cotangent.astype(F32) + grad_joined[:, :256]
    grad_agg = grad_joined[:, 256:].astype(BF)

    pieces = gather_steps(halves(grad_agg, core), "x", "yl")
    operands = (joined, act_one, cotangent, grad_pre_one, grad_pre_two, act_two)
    grad_in, grad_mid, grad_out = sum_grads(core, operands)
    back = cell_products(True, bwd_off, count, place, blk_own, blk_other, pieces)
    mine, yours = node_sum(scatter_steps(back, "z", "yh"))
    got = lax.ppermute(yours, "core", swap).astype(F32)
    first = core == 0
    relaid = jnp.concatenate(
        [jnp.where(first, mine, got), jnp.where(first, got, mine)], axis=1
    )
    grad_nodes = (direct + relaid).astype(BF)
    return updated, grad_nodes, grad_in, grad_mid, grad_out


def solution(mesh):
    fine = Mesh(mesh.devices.reshape(4, 2, 2, 2, 4), ROW + COL)
    nodes = P(ROW + COL, None)
    placed = (
        nodes,
        P(ROW, COL, None, None, None),
        P(ROW, COL, None),
        P(ROW, COL, None),
        P(ROW, COL),
        P(),
        P(),
        P(),
        nodes,
    )

    return jax.shard_map(
        shards,
        mesh=fine,
        in_specs=placed,
        out_specs=(nodes, nodes, P(), P(), P()),
        check_vma=False,
    )
```

```python
import functools

import jax
import jax.numpy as jnp
from jax import lax
from jax.experimental import pallas as pl
from jax.experimental.pallas import tpu as pltpu
from jax.experimental.layout import Layout, with_layout_constraint
from jax.sharding import Mesh, PartitionSpec as P


BF = jnp.bfloat16
F32 = jnp.float32
ROW = ("z", "yh", "core")
COL = ("yl", "x")
SLOTS = 192
SIDE = 64
CHUNK = 32
UNROLL = 32
CELL_VMEM = 28 << 20


def silu_grad(value):
    sig = jax.nn.sigmoid(value)
    return sig * (1.0 + value * (1.0 - sig))


def cells_kernel(transposed, spots, off_ref, cnt_ref, place_ref, blk0, blk1, *rest):
    pieces = rest[: len(spots)]
    out_refs = rest[len(spots) : -7]
    src, held, acc, sent, blk_sem, src_sem, out_sem = rest[-7:]
    n_chunks = SLOTS // CHUNK
    blocks = (blk0, blk1)

    def copy_of(j, ch):
        at = pl.multiple_of(ch * CHUNK, CHUNK)
        return pltpu.make_async_copy(
            blocks[j].at[pl.ds(at, CHUNK)],
            held.at[j, pl.ds(at, CHUNK)],
            blk_sem.at[j * n_chunks + ch],
        )

    moves = [
        pltpu.make_async_copy(piece, src.at[pl.ds(spot, piece.shape[0])], src_sem.at[p])
        for p, (spot, piece) in enumerate(zip(spots, pieces))
    ]
    for move in moves:
        move.start()
    used = [lax.div(cnt_ref[j] + (CHUNK - 1), CHUNK) for j in range(2)]
    for j in range(2):

        @pl.loop(0, used[j])
        def _(ch):
            copy_of(j, ch).start()

    acc[...] = jnp.zeros_like(acc)
    for move in moves:
        move.wait()
    dims = (((0,), (0,)), ((), ())) if transposed else (((1,), (0,)), ((), ()))
    for j in range(2):
        count = cnt_ref[j]

        @pl.loop(0, used[j])
        def _(ch):
            copy_of(j, ch).wait()
            left = jnp.minimum(count - ch * CHUNK, CHUNK)

            @pl.loop(0, lax.div(left + (UNROLL - 1), UNROLL))
            def _(step):
                base = ch * CHUNK + step * UNROLL
                for u in range(UNROLL):
                    slot = base + u
                    take = pl.multiple_of(off_ref[j * SLOTS + slot], SIDE)
                    put = pl.multiple_of(off_ref[(2 + j) * SLOTS + slot], SIDE)
                    term = lax.dot_general(
                        held[j, slot],
                        src[pl.ds(take, SIDE), :],
                        dims,
                        preferred_element_type=F32,
                    )
                    acc[pl.ds(put, SIDE), :] += term

    if len(out_refs) == 1:
        out_refs[0][...] = acc[: 16 * 512, :].astype(BF).reshape(out_refs[0].shape)
    else:
        moves = []
        for p, out_ref in enumerate(out_refs):
            for h in range(2):
                at = pl.multiple_of(place_ref[2 * p + h], 512)
                sent[p, h * 512 : (h + 1) * 512, :] = acc[pl.ds(at, 512), :].astype(BF)
            moves.append(pltpu.make_async_copy(sent.at[p], out_ref, out_sem.at[p]))
            moves[-1].start()
        for move in moves:
            move.wait()


def in_hbm(value):
    return pltpu.with_memory_space_constraint(value, pltpu.HBM)


def cell_products(transposed, offsets, counts, place, blk_own, blk_other, pieces):
    spots = [spot for spot, _ in pieces]
    any_spec = pl.BlockSpec(memory_space=pl.ANY)
    hbm = pl.BlockSpec(memory_space=pltpu.HBM)
    smem = pl.BlockSpec(memory_space=pltpu.SMEM)
    n_chunks = SLOTS // CHUNK
    return pl.pallas_call(
        functools.partial(cells_kernel, transposed, spots),
        out_shape=(pltpu.HBM((1024, 128), BF),) * 8
        if transposed
        else jax.ShapeDtypeStruct((16, 512, 128), BF),
        in_specs=[smem] * 3 + [hbm] * 2 + [any_spec] * len(pieces),
        out_specs=(hbm,) * 8
        if transposed
        else pl.BlockSpec(memory_space=pltpu.VMEM),
        scratch_shapes=[
            pltpu.VMEM((8192, 128), BF),
            pltpu.VMEM((2, SLOTS, SIDE, SIDE), BF),
            pltpu.VMEM((8192 + SIDE, 128), F32),
            pltpu.VMEM((8, 1024, 128) if transposed else (8, 16, 128), BF),
            pltpu.SemaphoreType.DMA((2 * n_chunks,)),
            pltpu.SemaphoreType.DMA((len(pieces),)),
            pltpu.SemaphoreType.DMA((8,)),
        ],
        compiler_params=pltpu.CompilerParams(vmem_limit_bytes=CELL_VMEM),
        cost_estimate=pl.CostEstimate(
            flops=2 * 2 * SLOTS * SIDE * SIDE * 128, bytes_accessed=10 << 20, transcendentals=0
        ),
        name="cells_back" if transposed else "cells_forward",
    )(offsets, counts, place, in_hbm(blk_own), in_hbm(blk_other), *(piece for _, piece in pieces))


def grads_kernel(half_ref, joined, act_one, cot, gp_one, gp_two, act_two, sum_ref):
    at = pl.multiple_of(half_ref[0] * 512, 512)
    sides = ((joined, gp_one, 0, 512), (act_one, gp_two, 512, 1024), (cot, act_two, 1536, 256))
    for left, right, row, size in sides:
        for part in range(0, size, 256):
            sum_ref[row + part : row + part + 256, :] = lax.dot_general(
                left[:, part : part + 256],
                right[:, pl.ds(at, 512)],
                (((0,), (0,)), ((), ())),
                preferred_element_type=F32,
            ).astype(BF)


def local_grads(half, *operands):
    vm = pl.BlockSpec(memory_space=pltpu.VMEM)
    return pl.pallas_call(
        grads_kernel,
        out_shape=jax.ShapeDtypeStruct((1792, 512), BF),
        in_specs=[pl.BlockSpec(memory_space=pltpu.SMEM)] + [vm] * 6,
        out_specs=vm,
        compiler_params=pltpu.CompilerParams(vmem_limit_bytes=16 << 20),
        cost_estimate=pl.CostEstimate(
            flops=512 * 1792 * 1024, bytes_accessed=8 << 20, transcendentals=0
        ),
    )(half.reshape(1), *operands)


def chip_kernel(own, got, out_ref, held, sems):
    moves = []
    for row in range(16):
        rows = slice(row * 112, (row + 1) * 112)
        for lane in range(4):
            lanes = slice(lane * 128, (lane + 1) * 128)
            held[row * 4 + lane] = (own[rows, lanes].astype(F32) + got[rows, lanes].astype(F32)).astype(
                BF
            )
        if row % 4 == 3:
            part = slice((row - 3) * 4, (row + 1) * 4)
            moves.append(pltpu.make_async_copy(held.at[part], out_ref.at[part], sems.at[row // 4]))
            moves[-1].start()
    for move in moves:
        move.wait()


def chip_sum(own, got):
    vm = pl.BlockSpec(memory_space=pltpu.VMEM)
    return pl.pallas_call(
        chip_kernel,
        out_shape=pltpu.HBM((64, 112, 128), BF),
        in_specs=[vm, vm],
        out_specs=pl.BlockSpec(memory_space=pltpu.HBM),
        scratch_shapes=[pltpu.VMEM((64, 112, 128), BF), pltpu.SemaphoreType.DMA((4,))],
        cost_estimate=pl.CostEstimate(flops=1 << 20, bytes_accessed=6 << 20, transcendentals=0),
        compiler_params=pltpu.CompilerParams(vmem_limit_bytes=12 << 20),
        name="chip_sum",
    )(own, got)


def chunk_kernel(parts, out_ref, held, sems):
    total = jnp.sum(parts[...].astype(F32), axis=0).astype(BF)
    for k in range(8):
        held[k] = total
    moves = [
        pltpu.make_async_copy(held, out_ref.at[8 * k : 8 * k + 8], sems.at[k]) for k in range(8)
    ]
    for move in moves:
        move.start()
    for move in moves:
        move.wait()


def chunk_sum(parts):
    return pl.pallas_call(
        chunk_kernel,
        out_shape=pltpu.HBM((64, 112, 128), BF),
        in_specs=[pl.BlockSpec(memory_space=pltpu.VMEM)],
        out_specs=pl.BlockSpec(memory_space=pltpu.HBM),
        scratch_shapes=[pltpu.VMEM((8, 112, 128), BF), pltpu.SemaphoreType.DMA((8,))],
        cost_estimate=pl.CostEstimate(flops=1 << 20, bytes_accessed=3 << 20, transcendentals=0),
        compiler_params=pltpu.CompilerParams(vmem_limit_bytes=12 << 20),
        name="chunk_sum",
    )(parts)


def ring_shift(value, axis, k):
    return lax.ppermute(value, axis, [(i, (i + k) % 4) for i in range(4)])


def flip(value, axis):
    return lax.ppermute(value, axis, [(0, 1), (1, 0)])


def gather_steps(value, ring, pair):
    over = flip(value, pair)
    below = ring_shift(value, ring, 1)
    above = ring_shift(value, ring, 3)
    low = ring_shift(above[:512], ring, 3)
    high = ring_shift(below[512:], ring, 1)
    over_below = ring_shift(over, ring, 1)
    over_above = ring_shift(over, ring, 3)
    over_low = flip(low, pair)
    over_high = flip(high, pair)
    return [
        (0, value),
        (1024, over),
        (2048, below),
        (3072, over_below),
        (4096, low),
        (4608, high),
        (5120, over_low),
        (5632, over_high),
        (6144, above),
        (7168, over_above),
    ]


def gather_direct(value, ring, pair):
    got = [value] * 8
    got[1] = flip(value, pair)
    for small in range(2):
        for big in (2, 1, 3):
            p = 2 * big + small
            got[p] = ring_shift(got[small], ring, big)
    return [(1024 * p, block) for p, block in enumerate(got)]


def pair_kernel(*refs):
    total = refs[0][...].astype(F32)
    for ref in refs[1:-1]:
        total = total + ref[...].astype(F32)
    refs[-1][...] = total.astype(BF)


def pair_sum(parts):
    vm = pl.BlockSpec(memory_space=pltpu.VMEM)
    return pl.pallas_call(
        pair_kernel,
        out_shape=jax.ShapeDtypeStruct((1024, 128), BF),
        in_specs=[vm] * len(parts),
        out_specs=vm,
        cost_estimate=pl.CostEstimate(flops=1 << 19, bytes_accessed=5 << 18, transcendentals=0),
        compiler_params=pltpu.CompilerParams(vmem_limit_bytes=6 << 20),
        name="pair_sum",
    )(*parts)


def scatter_steps(pieces, ring, pair):
    far, near = [pieces[1]], [pieces[0]]
    for small, got in ((1, far), (0, near)):
        for big in (2, 1, 3):
            p = 2 * big + small
            got.append(ring_shift(pieces[p], ring, big))
    far = pair_sum(far)
    return near + [flip(far, pair)]


def node_kernel(*refs):
    mine_ref, yours_ref = refs[-2:]
    for rows, out_ref in ((slice(0, 512), mine_ref), (slice(512, 1024), yours_ref)):
        total = refs[0][rows, :].astype(F32)
        for ref in refs[1:-2]:
            total = total + ref[rows, :].astype(F32)
        out_ref[...] = total.astype(out_ref.dtype)


def node_sum(parts):
    vm = pl.BlockSpec(memory_space=pltpu.VMEM)
    return pl.pallas_call(
        node_kernel,
        out_shape=(
            jax.ShapeDtypeStruct((512, 128), F32),
            jax.ShapeDtypeStruct((512, 128), BF),
        ),
        in_specs=[vm] * len(parts),
        out_specs=(vm, vm),
        cost_estimate=pl.CostEstimate(flops=1 << 20, bytes_accessed=3 << 20, transcendentals=0),
        compiler_params=pltpu.CompilerParams(vmem_limit_bytes=8 << 20),
        name="node_sum",
    )(*parts)


def halves(value, core):
    left, right = value[:, :128], value[:, 128:]
    first = core == 0
    mine = jnp.where(first, left, right)
    yours = jnp.where(first, right, left)
    got = lax.ppermute(yours, "core", [(0, 1), (1, 0)])
    return jnp.concatenate([mine, got], axis=0)


def finish_kernel(half_ref, blocks_ref, *rest):
    outs, total, turned, sems = rest[-6:-3], rest[-3], rest[-2], rest[-1]
    lane = pl.multiple_of(half_ref[0] * 512, 512)
    lanes = pl.ds(lane, 512)
    moves = (
        pltpu.make_async_copy(total.at[:512], outs[0].at[:, lanes], sems.at[0]),
        pltpu.make_async_copy(total.at[512:1536], outs[1].at[:, lanes], sems.at[1]),
        pltpu.make_async_copy(turned, outs[2].at[lanes, :], sems.at[2]),
    )
    for row in range(16):
        for col in range(4):
            total[row * 112 : (row + 1) * 112, col * 128 : (col + 1) * 128] = blocks_ref[
                row * 4 + col
            ].astype(F32) * (1.0 / 256.0)
        if row == 4:
            moves[0].start()
        if row == 13:
            moves[1].start()
    turned[...] = total[1536:, :].T
    moves[2].start()
    for move in moves:
        move.wait()


def finish_grads(half, blocks, outs):
    vm = pl.BlockSpec(memory_space=pltpu.VMEM)
    any_spec = pl.BlockSpec(memory_space=pl.ANY)
    return pl.pallas_call(
        finish_kernel,
        out_shape=(
            jax.ShapeDtypeStruct((512, 1024), F32),
            jax.ShapeDtypeStruct((1024, 1024), F32),
            jax.ShapeDtypeStruct((1024, 256), F32),
        ),
        in_specs=[pl.BlockSpec(memory_space=pltpu.SMEM), vm] + [any_spec] * len(outs),
        out_specs=(any_spec,) * 3,
        scratch_shapes=[
            pltpu.VMEM((1792, 512), F32),
            pltpu.VMEM((512, 256), F32),
            pltpu.SemaphoreType.DMA((3,)),
        ],
        input_output_aliases={2 + k: k for k in range(len(outs))},
        compiler_params=pltpu.CompilerParams(vmem_limit_bytes=16 << 20),
        cost_estimate=pl.CostEstimate(flops=4 << 20, bytes_accessed=6 << 20, transcendentals=0),
        name="finish_grads",
    )(half.reshape(1), blocks, *outs)


def sum_grads(core, operands):
    swap = [(0, 1), (1, 0)]
    other = local_grads(1 - core, *operands)
    got = lax.ppermute(other, "core", swap)
    own = local_grads(core, *operands)
    parts = lax.all_to_all(chip_sum(own, got), ("z", "yh", "yl", "x"), 0, 0, tiled=True)
    chunk = chunk_sum(parts)
    mine = lax.all_to_all(chunk, ("z", "yh", "yl", "x"), 0, 0, tiled=True)
    yours = lax.ppermute(mine, "core", swap)
    outs = finish_grads(core, mine, ())
    return finish_grads(1 - core, yours, outs)


def shards(features, blocks, block_rows, block_cols, block_count, w_in, w_mid, w_out, cotangent):
    core = lax.axis_index("core")
    z, yh = lax.axis_index("z"), lax.axis_index("yh")
    yl, x = lax.axis_index("yl"), lax.axis_index("x")
    swap = [(0, 1), (1, 0)]
    blk_own = blocks[0, 0].transpose(1, 2, 0)
    shard = halves(features, core)
    slots, _ = lax.optimization_barrier(((block_rows, block_cols, block_count), shard))
    meta = jnp.concatenate(
        [slots[0][0, 0], slots[1][0, 0], jnp.broadcast_to(slots[2][0, 0], (128,))]
    )
    meta_other = lax.ppermute(meta, "core", swap)
    blk_other = lax.ppermute(blk_own, "core", swap)

    both = jnp.stack([meta, meta_other])
    rows, cols, count = both[:, :SLOTS], both[:, SLOTS : 2 * SLOTS], both[:, 2 * SLOTS]
    live = jnp.arange(SLOTS, dtype=jnp.int32)[None, :] < count[:, None]
    cell_core = jnp.stack([core, 1 - core])[:, None]
    spare = 16 * 512
    grp = cols >> 3
    step = (((z - (grp >> 2)) & 3) * 2) + (((grp >> 1) & 1) ^ yh)
    col_at = step * 1024 + ((grp & 1) ^ core) * 512 + (cols & 7) * SIDE
    row_to = jnp.where(live, cell_core * 4096 + rows * SIDE, spare)
    fwd_off = jnp.concatenate([col_at, row_to]).reshape(4 * SLOTS)
    own8 = rows >> 3
    step = (((x - own8) & 3) * 2) + ((own8 >> 2) ^ yl)
    row_at = step * 1024 + jnp.arange(2, dtype=jnp.int32)[:, None] * 512 + (rows & 7) * SIDE
    col_to = jnp.where(live, cols * SIDE, spare)
    bwd_off = jnp.concatenate([row_at, col_to]).reshape(4 * SLOTS)

    p = jnp.arange(16, dtype=jnp.int32)
    place = (((z + (p >> 2)) & 3) * 4 + (yh ^ ((p >> 1) & 1)) * 2 + (core ^ (p & 1))) * 512
    pieces = gather_steps(shard, "z", "yh")
    blk_own, _ = lax.optimization_barrier((blk_own, shard))
    blk_own = with_layout_constraint(blk_own, Layout((0, 1, 2))).transpose(2, 0, 1)
    blk_other = blk_other.transpose(2, 0, 1)
    cells = cell_products(False, fwd_off, count, place, blk_own, blk_other, pieces)
    cells = lax.all_to_all(cells, ("core", "yl", "x"), 0, 0, tiled=True)
    sums = jnp.sum(cells.reshape(2, 8, 512, 128).astype(F32), axis=1).astype(BF)
    aggregated = jnp.concatenate([sums[0], sums[1]], axis=1)

    joined = jnp.concatenate([features, aggregated], axis=1)
    pre_one = jnp.dot(joined, w_in, preferred_element_type=F32)
    act_one = jax.nn.silu(pre_one).astype(BF)
    pre_two = jnp.dot(act_one, w_mid, preferred_element_type=F32)
    act_two = jax.nn.silu(pre_two).astype(BF)
    updated = (
        features.astype(F32) + jnp.dot(act_two, w_out, preferred_element_type=F32)
    ).astype(BF)
    grad_pre_two = (
        jnp.dot(cotangent, w_out.T, preferred_element_type=F32) * silu_grad(pre_two)
    ).astype(BF)
    grad_pre_one = (
        jnp.dot(grad_pre_two, w_mid.T, preferred_element_type=F32) * silu_grad(pre_one)
    ).astype(BF)
    grad_joined = jnp.dot(grad_pre_one, w_in.T, preferred_element_type=F32)
    direct = cotangent.astype(F32) + grad_joined[:, :256]
    grad_agg = grad_joined[:, 256:].astype(BF)

    pieces = gather_direct(halves(grad_agg, core), "x", "yl")
    operands = (joined, act_one, cotangent, grad_pre_one, grad_pre_two, act_two)
    grad_in, grad_mid, grad_out = sum_grads(core, operands)
    back = cell_products(True, bwd_off, count, place, blk_own, blk_other, pieces)
    mine, yours = node_sum(scatter_steps(back, "z", "yh"))
    got = lax.ppermute(yours, "core", swap).astype(F32)
    first = core == 0
    relaid = jnp.concatenate(
        [jnp.where(first, mine, got), jnp.where(first, got, mine)], axis=1
    )
    grad_nodes = (direct + relaid).astype(BF)
    return updated, grad_nodes, grad_in, grad_mid, grad_out


def solution(mesh):
    fine = Mesh(mesh.devices.reshape(4, 2, 2, 2, 4), ROW + COL)
    nodes = P(ROW + COL, None)
    placed = (
        nodes,
        P(ROW, COL, None, None, None),
        P(ROW, COL, None),
        P(ROW, COL, None),
        P(ROW, COL),
        P(),
        P(),
        P(),
        nodes,
    )

    return jax.shard_map(
        shards,
        mesh=fine,
        in_specs=placed,
        out_specs=(nodes, nodes, P(), P(), P()),
        check_vma=False,
    )
```

```python
import functools

import jax
import jax.numpy as jnp
from jax import lax
from jax.experimental import pallas as pl
from jax.experimental.pallas import tpu as pltpu
from jax.sharding import Mesh, PartitionSpec as P


BF = jnp.bfloat16
F32 = jnp.float32
ROW = ("z", "yh", "core")
COL = ("yl", "x")
SLOTS = 192
SIDE = 64
CHUNK = 32
UNROLL = 32
CELL_VMEM = 28 << 20


def silu_grad(value):
    sig = jax.nn.sigmoid(value)
    return sig * (1.0 + value * (1.0 - sig))


def cells_kernel(transposed, spots, off_ref, cnt_ref, place_ref, blk0, blk1, *rest):
    pieces = rest[: len(spots)]
    out_refs = rest[len(spots) : -7]
    src, held, acc, sent, blk_sem, src_sem, out_sem = rest[-7:]
    n_chunks = SLOTS // CHUNK
    blocks = (blk0, blk1)

    def copy_of(j, ch):
        at = pl.multiple_of(ch * CHUNK, CHUNK)
        return pltpu.make_async_copy(
            blocks[j].at[pl.ds(at, CHUNK)],
            held.at[j, pl.ds(at, CHUNK)],
            blk_sem.at[j * n_chunks + ch],
        )

    moves = [
        pltpu.make_async_copy(piece, src.at[pl.ds(spot, piece.shape[0])], src_sem.at[p])
        for p, (spot, piece) in enumerate(zip(spots, pieces))
    ]
    for move in moves:
        move.start()
    used = [lax.div(cnt_ref[j] + (CHUNK - 1), CHUNK) for j in range(2)]
    for j in range(2):

        @pl.loop(0, used[j])
        def _(ch):
            copy_of(j, ch).start()

    acc[...] = jnp.zeros_like(acc)
    for move in moves:
        move.wait()
    dims = (((0,), (0,)), ((), ())) if transposed else (((1,), (0,)), ((), ()))
    for j in range(2):
        count = cnt_ref[j]

        @pl.loop(0, used[j])
        def _(ch):
            copy_of(j, ch).wait()
            left = jnp.minimum(count - ch * CHUNK, CHUNK)

            @pl.loop(0, lax.div(left + (UNROLL - 1), UNROLL))
            def _(step):
                base = ch * CHUNK + step * UNROLL
                for u in range(UNROLL):
                    slot = base + u
                    take = pl.multiple_of(off_ref[j * SLOTS + slot], SIDE)
                    put = pl.multiple_of(off_ref[(2 + j) * SLOTS + slot], SIDE)
                    term = lax.dot_general(
                        held[j, slot],
                        src[pl.ds(take, SIDE), :],
                        dims,
                        preferred_element_type=F32,
                    )
                    acc[pl.ds(put, SIDE), :] += term

    if len(out_refs) == 1:
        out_refs[0][...] = acc[: 16 * 512, :].astype(BF).reshape(out_refs[0].shape)
    else:
        moves = []
        for p, out_ref in enumerate(out_refs):
            for h in range(2):
                at = pl.multiple_of(place_ref[2 * p + h], 512)
                sent[p, h * 512 : (h + 1) * 512, :] = acc[pl.ds(at, 512), :].astype(BF)
            moves.append(pltpu.make_async_copy(sent.at[p], out_ref, out_sem.at[p]))
            moves[-1].start()
        for move in moves:
            move.wait()


def in_hbm(value):
    return pltpu.with_memory_space_constraint(value, pltpu.HBM)


def cell_products(transposed, offsets, counts, place, blk_own, blk_other, pieces):
    spots = [spot for spot, _ in pieces]
    any_spec = pl.BlockSpec(memory_space=pl.ANY)
    hbm = pl.BlockSpec(memory_space=pltpu.HBM)
    smem = pl.BlockSpec(memory_space=pltpu.SMEM)
    n_chunks = SLOTS // CHUNK
    return pl.pallas_call(
        functools.partial(cells_kernel, transposed, spots),
        out_shape=(pltpu.HBM((1024, 128), BF),) * 8
        if transposed
        else jax.ShapeDtypeStruct((16, 512, 128), BF),
        in_specs=[smem] * 3 + [hbm] * 2 + [any_spec] * len(pieces),
        out_specs=(hbm,) * 8
        if transposed
        else pl.BlockSpec(memory_space=pltpu.VMEM),
        scratch_shapes=[
            pltpu.VMEM((8192, 128), BF),
            pltpu.VMEM((2, SLOTS, SIDE, SIDE), BF),
            pltpu.VMEM((8192 + SIDE, 128), F32),
            pltpu.VMEM((8, 1024, 128) if transposed else (8, 16, 128), BF),
            pltpu.SemaphoreType.DMA((2 * n_chunks,)),
            pltpu.SemaphoreType.DMA((len(pieces),)),
            pltpu.SemaphoreType.DMA((8,)),
        ],
        compiler_params=pltpu.CompilerParams(vmem_limit_bytes=CELL_VMEM),
        cost_estimate=pl.CostEstimate(
            flops=2 * 2 * SLOTS * SIDE * SIDE * 128, bytes_accessed=10 << 20, transcendentals=0
        ),
        name="cells_back" if transposed else "cells_forward",
    )(offsets, counts, place, in_hbm(blk_own), in_hbm(blk_other), *(piece for _, piece in pieces))


def grads_kernel(half_ref, joined, act_one, cot, gp_one, gp_two, act_two, sum_ref):
    at = pl.multiple_of(half_ref[0] * 512, 512)
    sides = ((joined, gp_one, 0, 512), (act_one, gp_two, 512, 1024), (cot, act_two, 1536, 256))
    for left, right, row, size in sides:
        for part in range(0, size, 256):
            sum_ref[row + part : row + part + 256, :] = lax.dot_general(
                left[:, part : part + 256],
                right[:, pl.ds(at, 512)],
                (((0,), (0,)), ((), ())),
                preferred_element_type=F32,
            ).astype(BF)


def local_grads(half, *operands):
    vm = pl.BlockSpec(memory_space=pltpu.VMEM)
    return pl.pallas_call(
        grads_kernel,
        out_shape=jax.ShapeDtypeStruct((1792, 512), BF),
        in_specs=[pl.BlockSpec(memory_space=pltpu.SMEM)] + [vm] * 6,
        out_specs=vm,
        compiler_params=pltpu.CompilerParams(vmem_limit_bytes=16 << 20),
        cost_estimate=pl.CostEstimate(
            flops=512 * 1792 * 1024, bytes_accessed=8 << 20, transcendentals=0
        ),
    )(half.reshape(1), *operands)


def chip_kernel(own, got, out_ref, held, sems):
    moves = []
    for row in range(16):
        rows = slice(row * 112, (row + 1) * 112)
        for lane in range(4):
            lanes = slice(lane * 128, (lane + 1) * 128)
            held[row * 4 + lane] = (own[rows, lanes].astype(F32) + got[rows, lanes].astype(F32)).astype(
                BF
            )
        if row % 4 == 3:
            part = slice((row - 3) * 4, (row + 1) * 4)
            moves.append(pltpu.make_async_copy(held.at[part], out_ref.at[part], sems.at[row // 4]))
            moves[-1].start()
    for move in moves:
        move.wait()


def chip_sum(own, got):
    vm = pl.BlockSpec(memory_space=pltpu.VMEM)
    return pl.pallas_call(
        chip_kernel,
        out_shape=pltpu.HBM((64, 112, 128), BF),
        in_specs=[vm, vm],
        out_specs=pl.BlockSpec(memory_space=pltpu.HBM),
        scratch_shapes=[pltpu.VMEM((64, 112, 128), BF), pltpu.SemaphoreType.DMA((4,))],
        cost_estimate=pl.CostEstimate(flops=1 << 20, bytes_accessed=6 << 20, transcendentals=0),
        compiler_params=pltpu.CompilerParams(vmem_limit_bytes=12 << 20),
        name="chip_sum",
    )(own, got)


def chunk_kernel(parts, out_ref, held, sems):
    total = jnp.sum(parts[...].astype(F32), axis=0).astype(BF)
    for k in range(8):
        held[k] = total
    moves = [
        pltpu.make_async_copy(held, out_ref.at[8 * k : 8 * k + 8], sems.at[k]) for k in range(8)
    ]
    for move in moves:
        move.start()
    for move in moves:
        move.wait()


def chunk_sum(parts):
    return pl.pallas_call(
        chunk_kernel,
        out_shape=pltpu.HBM((64, 112, 128), BF),
        in_specs=[pl.BlockSpec(memory_space=pltpu.VMEM)],
        out_specs=pl.BlockSpec(memory_space=pltpu.HBM),
        scratch_shapes=[pltpu.VMEM((8, 112, 128), BF), pltpu.SemaphoreType.DMA((8,))],
        cost_estimate=pl.CostEstimate(flops=1 << 20, bytes_accessed=3 << 20, transcendentals=0),
        compiler_params=pltpu.CompilerParams(vmem_limit_bytes=12 << 20),
        name="chunk_sum",
    )(parts)


def ring_shift(value, axis, k):
    return lax.ppermute(value, axis, [(i, (i + k) % 4) for i in range(4)])


def flip(value, axis):
    return lax.ppermute(value, axis, [(0, 1), (1, 0)])


def gather_steps(value, ring, pair):
    over = flip(value, pair)
    below = ring_shift(value, ring, 1)
    above = ring_shift(value, ring, 3)
    low = ring_shift(above[:512], ring, 3)
    high = ring_shift(below[512:], ring, 1)
    over_below = ring_shift(over, ring, 1)
    over_above = ring_shift(over, ring, 3)
    over_low = flip(low, pair)
    over_high = flip(high, pair)
    return [
        (0, value),
        (1024, over),
        (2048, below),
        (3072, over_below),
        (4096, low),
        (4608, high),
        (5120, over_low),
        (5632, over_high),
        (6144, above),
        (7168, over_above),
    ]


def gather_direct(value, ring, pair):
    got = [value] * 8
    got[1] = flip(value, pair)
    for small in range(2):
        for big in (2, 1, 3):
            p = 2 * big + small
            got[p] = ring_shift(got[small], ring, big)
    return [(1024 * p, block) for p, block in enumerate(got)]


def pair_kernel(*refs):
    total = refs[0][...].astype(F32)
    for ref in refs[1:-1]:
        total = total + ref[...].astype(F32)
    refs[-1][...] = total.astype(BF)


def pair_sum(parts):
    vm = pl.BlockSpec(memory_space=pltpu.VMEM)
    return pl.pallas_call(
        pair_kernel,
        out_shape=jax.ShapeDtypeStruct((1024, 128), BF),
        in_specs=[vm] * len(parts),
        out_specs=vm,
        cost_estimate=pl.CostEstimate(flops=1 << 19, bytes_accessed=5 << 18, transcendentals=0),
        compiler_params=pltpu.CompilerParams(vmem_limit_bytes=6 << 20),
    )(*parts)


def scatter_steps(pieces, ring, pair):
    cross = flip(pieces[5], pair)
    far, near = [pieces[1]], [pieces[0]]
    for small, got in ((1, far), (0, near)):
        for big in (1, 3):
            p = 2 * big + small
            got.append(ring_shift(pieces[p], ring, big))
    cross = pair_sum([pieces[4], cross])
    near.append(ring_shift(cross, ring, 2))
    far = pair_sum(far)
    return near + [flip(far, pair)]


def node_kernel(*refs):
    mine_ref, yours_ref = refs[-2:]
    for rows, out_ref in ((slice(0, 512), mine_ref), (slice(512, 1024), yours_ref)):
        total = refs[0][rows, :].astype(F32)
        for ref in refs[1:-2]:
            total = total + ref[rows, :].astype(F32)
        out_ref[...] = total.astype(out_ref.dtype)


def node_sum(parts):
    vm = pl.BlockSpec(memory_space=pltpu.VMEM)
    return pl.pallas_call(
        node_kernel,
        out_shape=(
            jax.ShapeDtypeStruct((512, 128), F32),
            jax.ShapeDtypeStruct((512, 128), BF),
        ),
        in_specs=[vm] * len(parts),
        out_specs=(vm, vm),
        cost_estimate=pl.CostEstimate(flops=1 << 20, bytes_accessed=3 << 20, transcendentals=0),
        compiler_params=pltpu.CompilerParams(vmem_limit_bytes=8 << 20),
        name="node_sum",
    )(*parts)


def halves(value, core):
    left, right = value[:, :128], value[:, 128:]
    first = core == 0
    mine = jnp.where(first, left, right)
    yours = jnp.where(first, right, left)
    got = flip(yours, "core")
    return jnp.concatenate([mine, got], axis=0)


def finish_kernel(half_ref, blocks_ref, *rest):
    outs, total, turned, sems = rest[-6:-3], rest[-3], rest[-2], rest[-1]
    lane = pl.multiple_of(half_ref[0] * 512, 512)
    lanes = pl.ds(lane, 512)
    moves = (
        pltpu.make_async_copy(total.at[:512], outs[0].at[:, lanes], sems.at[0]),
        pltpu.make_async_copy(total.at[512:1536], outs[1].at[:, lanes], sems.at[1]),
        pltpu.make_async_copy(turned, outs[2].at[lanes, :], sems.at[2]),
    )
    for row in range(16):
        for col in range(4):
            total[row * 112 : (row + 1) * 112, col * 128 : (col + 1) * 128] = blocks_ref[
                row * 4 + col
            ].astype(F32) * (1.0 / 256.0)
        if row == 4:
            moves[0].start()
        if row == 13:
            moves[1].start()
    turned[...] = total[1536:, :].T
    moves[2].start()
    for move in moves:
        move.wait()


def finish_grads(half, blocks, outs):
    vm = pl.BlockSpec(memory_space=pltpu.VMEM)
    any_spec = pl.BlockSpec(memory_space=pl.ANY)
    return pl.pallas_call(
        finish_kernel,
        out_shape=(
            jax.ShapeDtypeStruct((512, 1024), F32),
            jax.ShapeDtypeStruct((1024, 1024), F32),
            jax.ShapeDtypeStruct((1024, 256), F32),
        ),
        in_specs=[pl.BlockSpec(memory_space=pltpu.SMEM), vm] + [any_spec] * len(outs),
        out_specs=(any_spec,) * 3,
        scratch_shapes=[
            pltpu.VMEM((1792, 512), F32),
            pltpu.VMEM((512, 256), F32),
            pltpu.SemaphoreType.DMA((3,)),
        ],
        input_output_aliases={2 + k: k for k in range(len(outs))},
        compiler_params=pltpu.CompilerParams(vmem_limit_bytes=16 << 20),
        cost_estimate=pl.CostEstimate(flops=4 << 20, bytes_accessed=6 << 20, transcendentals=0),
        name="finish_grads",
    )(half.reshape(1), blocks, *outs)


def sum_grads(core, operands):
    swap = [(0, 1), (1, 0)]
    other = local_grads(1 - core, *operands)
    got = lax.ppermute(other, "core", swap)
    own = local_grads(core, *operands)
    parts = lax.all_to_all(chip_sum(own, got), ("z", "yh", "yl", "x"), 0, 0, tiled=True)
    chunk = chunk_sum(parts)
    mine = lax.all_to_all(chunk, ("z", "yh", "yl", "x"), 0, 0, tiled=True)
    yours = lax.ppermute(mine, "core", swap)
    outs = finish_grads(core, mine, ())
    return finish_grads(1 - core, yours, outs)


def shards(features, blocks, block_rows, block_cols, block_count, w_in, w_mid, w_out, cotangent):
    core = lax.axis_index("core")
    z, yh = lax.axis_index("z"), lax.axis_index("yh")
    yl, x = lax.axis_index("yl"), lax.axis_index("x")
    swap = [(0, 1), (1, 0)]
    shard = halves(features, core)
    blk_own = blocks[0, 0]
    slots, _ = lax.optimization_barrier(((block_rows, block_cols, block_count), shard))
    meta = jnp.concatenate(
        [slots[0][0, 0], slots[1][0, 0], jnp.broadcast_to(slots[2][0, 0], (128,))]
    )
    meta_other = lax.ppermute(meta, "core", swap)
    blk_other = flip(blk_own, "core")

    both = jnp.stack([meta, meta_other])
    rows, cols, count = both[:, :SLOTS], both[:, SLOTS : 2 * SLOTS], both[:, 2 * SLOTS]
    live = jnp.arange(SLOTS, dtype=jnp.int32)[None, :] < count[:, None]
    cell_core = jnp.stack([core, 1 - core])[:, None]
    spare = 16 * 512
    grp = cols >> 3
    step = (((z - (grp >> 2)) & 3) * 2) + (((grp >> 1) & 1) ^ yh)
    col_at = step * 1024 + ((grp & 1) ^ core) * 512 + (cols & 7) * SIDE
    row_to = jnp.where(live, cell_core * 4096 + rows * SIDE, spare)
    fwd_off = jnp.concatenate([col_at, row_to]).reshape(4 * SLOTS)
    own8 = rows >> 3
    step = (((x - own8) & 3) * 2) + ((own8 >> 2) ^ yl)
    row_at = step * 1024 + jnp.arange(2, dtype=jnp.int32)[:, None] * 512 + (rows & 7) * SIDE
    col_to = jnp.where(live, cols * SIDE, spare)
    bwd_off = jnp.concatenate([row_at, col_to]).reshape(4 * SLOTS)

    p = jnp.arange(16, dtype=jnp.int32)
    place = (((z + (p >> 2)) & 3) * 4 + (yh ^ ((p >> 1) & 1)) * 2 + (core ^ (p & 1))) * 512
    pieces = gather_steps(shard, "z", "yh")
    cells = cell_products(False, fwd_off, count, place, blk_own, blk_other, pieces)
    cells = lax.all_to_all(cells, ("core", "yl", "x"), 0, 0, tiled=True)
    sums = jnp.sum(cells.reshape(2, 8, 512, 128).astype(F32), axis=1).astype(BF)
    aggregated = jnp.concatenate([sums[0], sums[1]], axis=1)

    joined = jnp.concatenate([features, aggregated], axis=1)
    pre_one = jnp.dot(joined, w_in, preferred_element_type=F32)
    act_one = jax.nn.silu(pre_one).astype(BF)
    pre_two = jnp.dot(act_one, w_mid, preferred_element_type=F32)
    act_two = jax.nn.silu(pre_two).astype(BF)
    updated = (
        features.astype(F32) + jnp.dot(act_two, w_out, preferred_element_type=F32)
    ).astype(BF)
    grad_pre_two = (
        jnp.dot(cotangent, w_out.T, preferred_element_type=F32) * silu_grad(pre_two)
    ).astype(BF)
    grad_pre_one = (
        jnp.dot(grad_pre_two, w_mid.T, preferred_element_type=F32) * silu_grad(pre_one)
    ).astype(BF)
    grad_joined = jnp.dot(grad_pre_one, w_in.T, preferred_element_type=F32)
    direct = cotangent.astype(F32) + grad_joined[:, :256]
    grad_agg = grad_joined[:, 256:].astype(BF)

    pieces = gather_direct(halves(grad_agg, core), "x", "yl")
    operands = (joined, act_one, cotangent, grad_pre_one, grad_pre_two, act_two)
    grad_in, grad_mid, grad_out = sum_grads(core, operands)
    back = cell_products(True, bwd_off, count, place, blk_own, blk_other, pieces)
    mine, yours = node_sum(scatter_steps(back, "z", "yh"))
    got = lax.ppermute(yours, "core", swap).astype(F32)
    first = core == 0
    relaid = jnp.concatenate(
        [jnp.where(first, mine, got), jnp.where(first, got, mine)], axis=1
    )
    grad_nodes = (direct + relaid).astype(BF)
    return updated, grad_nodes, grad_in, grad_mid, grad_out


def solution(mesh):
    fine = Mesh(mesh.devices.reshape(4, 2, 2, 2, 4), ROW + COL)
    nodes = P(ROW + COL, None)
    placed = (
        nodes,
        P(ROW, COL, None, None, None),
        P(ROW, COL, None),
        P(ROW, COL, None),
        P(ROW, COL),
        P(),
        P(),
        P(),
        nodes,
    )

    return jax.shard_map(
        shards,
        mesh=fine,
        in_specs=placed,
        out_specs=(nodes, nodes, P(), P(), P()),
        check_vma=False,
    )
```

```python
import functools

import jax
import jax.numpy as jnp
from jax import lax
from jax.experimental import pallas as pl
from jax.experimental.pallas import tpu as pltpu
from jax.sharding import Mesh, PartitionSpec as P


BF = jnp.bfloat16
F32 = jnp.float32
ROW = ("z", "yh", "core")
COL = ("yl", "x")
SLOTS = 192
SIDE = 64
CHUNK = 32
UNROLL = 32
CELL_VMEM = 28 << 20


def silu_grad(value):
    sig = jax.nn.sigmoid(value)
    return sig * (1.0 + value * (1.0 - sig))


def cells_kernel(transposed, spots, off_ref, cnt_ref, place_ref, blk0, blk1, *rest):
    pieces = rest[: len(spots)]
    out_refs = rest[len(spots) : -7]
    src, held, acc, sent, blk_sem, src_sem, out_sem = rest[-7:]
    n_chunks = SLOTS // CHUNK
    blocks = (blk0, blk1)

    def copy_of(j, ch):
        at = pl.multiple_of(ch * CHUNK, CHUNK)
        return pltpu.make_async_copy(
            blocks[j].at[pl.ds(at, CHUNK)],
            held.at[j, pl.ds(at, CHUNK)],
            blk_sem.at[j * n_chunks + ch],
        )

    moves = [
        pltpu.make_async_copy(piece, src.at[pl.ds(spot, piece.shape[0])], src_sem.at[p])
        for p, (spot, piece) in enumerate(zip(spots, pieces))
    ]
    for move in moves:
        move.start()
    used = [lax.div(cnt_ref[j] + (CHUNK - 1), CHUNK) for j in range(2)]
    for j in range(2):

        @pl.loop(0, used[j])
        def _(ch):
            copy_of(j, ch).start()

    acc[...] = jnp.zeros_like(acc)
    for move in moves:
        move.wait()
    dims = (((0,), (0,)), ((), ())) if transposed else (((1,), (0,)), ((), ()))
    for j in range(2):
        count = cnt_ref[j]

        @pl.loop(0, used[j])
        def _(ch):
            copy_of(j, ch).wait()
            left = jnp.minimum(count - ch * CHUNK, CHUNK)

            @pl.loop(0, lax.div(left + (UNROLL - 1), UNROLL))
            def _(step):
                base = ch * CHUNK + step * UNROLL
                for u in range(UNROLL):
                    slot = base + u
                    take = pl.multiple_of(off_ref[j * SLOTS + slot], SIDE)
                    put = pl.multiple_of(off_ref[(2 + j) * SLOTS + slot], SIDE)
                    term = lax.dot_general(
                        held[j, slot],
                        src[pl.ds(take, SIDE), :],
                        dims,
                        preferred_element_type=F32,
                    )
                    acc[pl.ds(put, SIDE), :] += term

    if len(out_refs) == 1:
        out_refs[0][...] = acc[: 16 * 512, :].astype(BF).reshape(out_refs[0].shape)
    else:
        moves = []
        for p, out_ref in enumerate(out_refs):
            for h in range(2):
                at = pl.multiple_of(place_ref[2 * p + h], 512)
                sent[p, h * 512 : (h + 1) * 512, :] = acc[pl.ds(at, 512), :].astype(BF)
            moves.append(pltpu.make_async_copy(sent.at[p], out_ref, out_sem.at[p]))
            moves[-1].start()
        for move in moves:
            move.wait()


def in_hbm(value):
    return pltpu.with_memory_space_constraint(value, pltpu.HBM)


def cell_products(transposed, offsets, counts, place, blk_own, blk_other, pieces):
    spots = [spot for spot, _ in pieces]
    any_spec = pl.BlockSpec(memory_space=pl.ANY)
    hbm = pl.BlockSpec(memory_space=pltpu.HBM)
    smem = pl.BlockSpec(memory_space=pltpu.SMEM)
    n_chunks = SLOTS // CHUNK
    return pl.pallas_call(
        functools.partial(cells_kernel, transposed, spots),
        out_shape=(pltpu.HBM((1024, 128), BF),) * 8
        if transposed
        else jax.ShapeDtypeStruct((16, 512, 128), BF),
        in_specs=[smem] * 3 + [hbm] * 2 + [any_spec] * len(pieces),
        out_specs=(hbm,) * 8
        if transposed
        else pl.BlockSpec(memory_space=pltpu.VMEM),
        scratch_shapes=[
            pltpu.VMEM((8192, 128), BF),
            pltpu.VMEM((2, SLOTS, SIDE, SIDE), BF),
            pltpu.VMEM((8192 + SIDE, 128), F32),
            pltpu.VMEM((8, 1024, 128) if transposed else (8, 16, 128), BF),
            pltpu.SemaphoreType.DMA((2 * n_chunks,)),
            pltpu.SemaphoreType.DMA((len(pieces),)),
            pltpu.SemaphoreType.DMA((8,)),
        ],
        compiler_params=pltpu.CompilerParams(vmem_limit_bytes=CELL_VMEM),
        cost_estimate=pl.CostEstimate(
            flops=2 * 2 * SLOTS * SIDE * SIDE * 128, bytes_accessed=10 << 20, transcendentals=0
        ),
        name="cells_back" if transposed else "cells_forward",
    )(offsets, counts, place, in_hbm(blk_own), in_hbm(blk_other), *(piece for _, piece in pieces))


def grads_kernel(half_ref, joined, act_one, cot, gp_one, gp_two, act_two, sum_ref):
    at = pl.multiple_of(half_ref[0] * 512, 512)
    sides = ((joined, gp_one, 0, 512), (act_one, gp_two, 512, 1024), (cot, act_two, 1536, 256))
    for left, right, row, size in sides:
        for part in range(0, size, 256):
            sum_ref[row + part : row + part + 256, :] = lax.dot_general(
                left[:, part : part + 256],
                right[:, pl.ds(at, 512)],
                (((0,), (0,)), ((), ())),
                preferred_element_type=F32,
            ).astype(BF)


def local_grads(half, *operands):
    vm = pl.BlockSpec(memory_space=pltpu.VMEM)
    return pl.pallas_call(
        grads_kernel,
        out_shape=jax.ShapeDtypeStruct((1792, 512), BF),
        in_specs=[pl.BlockSpec(memory_space=pltpu.SMEM)] + [vm] * 6,
        out_specs=vm,
        compiler_params=pltpu.CompilerParams(vmem_limit_bytes=16 << 20),
        cost_estimate=pl.CostEstimate(
            flops=512 * 1792 * 1024, bytes_accessed=8 << 20, transcendentals=0
        ),
    )(half.reshape(1), *operands)


def chip_kernel(own, got, out_ref, held, sems):
    moves = []
    for row in range(16):
        rows = slice(row * 112, (row + 1) * 112)
        for lane in range(4):
            lanes = slice(lane * 128, (lane + 1) * 128)
            held[row * 4 + lane] = (own[rows, lanes].astype(F32) + got[rows, lanes].astype(F32)).astype(
                BF
            )
        if row % 4 == 3:
            part = slice((row - 3) * 4, (row + 1) * 4)
            moves.append(pltpu.make_async_copy(held.at[part], out_ref.at[part], sems.at[row // 4]))
            moves[-1].start()
    for move in moves:
        move.wait()


def chip_sum(own, got):
    vm = pl.BlockSpec(memory_space=pltpu.VMEM)
    return pl.pallas_call(
        chip_kernel,
        out_shape=pltpu.HBM((64, 112, 128), BF),
        in_specs=[vm, vm],
        out_specs=pl.BlockSpec(memory_space=pltpu.HBM),
        scratch_shapes=[pltpu.VMEM((64, 112, 128), BF), pltpu.SemaphoreType.DMA((4,))],
        cost_estimate=pl.CostEstimate(flops=1 << 20, bytes_accessed=6 << 20, transcendentals=0),
        compiler_params=pltpu.CompilerParams(vmem_limit_bytes=12 << 20),
        name="chip_sum",
    )(own, got)


def chunk_kernel(parts, out_ref, taken, held, in_sem, out_sem):
    reads = [
        pltpu.make_async_copy(parts.at[8 * k : 8 * k + 8], taken.at[k], in_sem.at[k])
        for k in range(8)
    ]
    for read in reads:
        read.start()
    total = None
    for k, read in enumerate(reads):
        read.wait()
        part = jnp.sum(taken[k].astype(F32), axis=0)
        total = part if total is None else total + part
    total = total.astype(BF)
    for k in range(8):
        held[k] = total
    writes = [
        pltpu.make_async_copy(held, out_ref.at[8 * k : 8 * k + 8], out_sem.at[k])
        for k in range(8)
    ]
    for write in writes:
        write.start()
    for write in writes:
        write.wait()


def chunk_sum(parts):
    return pl.pallas_call(
        chunk_kernel,
        out_shape=pltpu.HBM((64, 112, 128), BF),
        in_specs=[pl.BlockSpec(memory_space=pl.ANY)],
        out_specs=pl.BlockSpec(memory_space=pltpu.HBM),
        scratch_shapes=[
            pltpu.VMEM((8, 8, 112, 128), BF),
            pltpu.VMEM((8, 112, 128), BF),
            pltpu.SemaphoreType.DMA((8,)),
            pltpu.SemaphoreType.DMA((8,)),
        ],
        cost_estimate=pl.CostEstimate(flops=1 << 20, bytes_accessed=3 << 20, transcendentals=0),
        compiler_params=pltpu.CompilerParams(vmem_limit_bytes=12 << 20),
        name="chunk_sum",
    )(parts)


def ring_shift(value, axis, k):
    return lax.ppermute(value, axis, [(i, (i + k) % 4) for i in range(4)])


def flip(value, axis):
    return lax.ppermute(value, axis, [(0, 1), (1, 0)])


def gather_steps(value, ring, pair):
    over = flip(value, pair)
    below = ring_shift(value, ring, 1)
    above = ring_shift(value, ring, 3)
    low = ring_shift(above[:512], ring, 3)
    high = ring_shift(below[512:], ring, 1)
    over_below = ring_shift(over, ring, 1)
    over_above = ring_shift(over, ring, 3)
    over_low = flip(low, pair)
    over_high = flip(high, pair)
    return [
        (0, value),
        (1024, over),
        (2048, below),
        (3072, over_below),
        (4096, low),
        (4608, high),
        (5120, over_low),
        (5632, over_high),
        (6144, above),
        (7168, over_above),
    ]


def gather_direct(value, ring, pair):
    got = [value] * 8
    got[1] = flip(value, pair)
    for small in range(2):
        for big in (2, 1, 3):
            p = 2 * big + small
            got[p] = ring_shift(got[small], ring, big)
    return [(1024 * p, block) for p, block in enumerate(got)]


def pair_kernel(*refs):
    total = refs[0][...].astype(F32)
    for ref in refs[1:-1]:
        total = total + ref[...].astype(F32)
    refs[-1][...] = total.astype(BF)


def pair_sum(parts):
    vm = pl.BlockSpec(memory_space=pltpu.VMEM)
    return pl.pallas_call(
        pair_kernel,
        out_shape=jax.ShapeDtypeStruct((1024, 128), BF),
        in_specs=[vm] * len(parts),
        out_specs=vm,
        cost_estimate=pl.CostEstimate(flops=1 << 19, bytes_accessed=5 << 18, transcendentals=0),
        compiler_params=pltpu.CompilerParams(vmem_limit_bytes=6 << 20),
    )(*parts)


def scatter_steps(pieces, ring, pair):
    cross = flip(pieces[5], pair)
    far, near = [pieces[1]], [pieces[0]]
    for small, got in ((1, far), (0, near)):
        for big in (1, 3):
            p = 2 * big + small
            got.append(ring_shift(pieces[p], ring, big))
    cross = pair_sum([pieces[4], cross])
    near.append(ring_shift(cross, ring, 2))
    far = pair_sum(far)
    return near + [flip(far, pair)]


def node_kernel(*refs):
    mine_ref, yours_ref = refs[-2:]
    for rows, out_ref in ((slice(0, 512), mine_ref), (slice(512, 1024), yours_ref)):
        total = refs[0][rows, :].astype(F32)
        for ref in refs[1:-2]:
            total = total + ref[rows, :].astype(F32)
        out_ref[...] = total.astype(out_ref.dtype)


def node_sum(parts):
    vm = pl.BlockSpec(memory_space=pltpu.VMEM)
    return pl.pallas_call(
        node_kernel,
        out_shape=(
            jax.ShapeDtypeStruct((512, 128), F32),
            jax.ShapeDtypeStruct((512, 128), BF),
        ),
        in_specs=[vm] * len(parts),
        out_specs=(vm, vm),
        cost_estimate=pl.CostEstimate(flops=1 << 20, bytes_accessed=3 << 20, transcendentals=0),
        compiler_params=pltpu.CompilerParams(vmem_limit_bytes=8 << 20),
        name="node_sum",
    )(*parts)


def halves(value, core):
    left, right = value[:, :128], value[:, 128:]
    first = core == 0
    mine = jnp.where(first, left, right)
    yours = jnp.where(first, right, left)
    got = flip(yours, "core")
    return jnp.concatenate([mine, got], axis=0)


def finish_kernel(half_ref, blocks_ref, *rest):
    outs, taken, total, turned, sems, in_sem = rest[-8:-5], *rest[-5:]
    reads = [
        pltpu.make_async_copy(blocks_ref.at[16 * k : 16 * k + 16], taken.at[k], in_sem.at[k])
        for k in range(4)
    ]
    for read in reads:
        read.start()
    lane = pl.multiple_of(half_ref[0] * 512, 512)
    lanes = pl.ds(lane, 512)
    moves = (
        pltpu.make_async_copy(total.at[:512], outs[0].at[:, lanes], sems.at[0]),
        pltpu.make_async_copy(total.at[512:1536], outs[1].at[:, lanes], sems.at[1]),
        pltpu.make_async_copy(turned, outs[2].at[lanes, :], sems.at[2]),
    )
    for row in range(16):
        if row % 4 == 0:
            reads[row // 4].wait()
        for col in range(4):
            total[row * 112 : (row + 1) * 112, col * 128 : (col + 1) * 128] = taken[
                row // 4, (row % 4) * 4 + col
            ].astype(F32) * (1.0 / 256.0)
        if row == 4:
            moves[0].start()
        if row == 13:
            moves[1].start()
    turned[...] = total[1536:, :].T
    moves[2].start()
    for move in moves:
        move.wait()


def finish_grads(half, blocks, outs):
    any_spec = pl.BlockSpec(memory_space=pl.ANY)
    return pl.pallas_call(
        finish_kernel,
        out_shape=(
            jax.ShapeDtypeStruct((512, 1024), F32),
            jax.ShapeDtypeStruct((1024, 1024), F32),
            jax.ShapeDtypeStruct((1024, 256), F32),
        ),
        in_specs=[pl.BlockSpec(memory_space=pltpu.SMEM)] + [any_spec] * (1 + len(outs)),
        out_specs=(any_spec,) * 3,
        scratch_shapes=[
            pltpu.VMEM((4, 16, 112, 128), BF),
            pltpu.VMEM((1792, 512), F32),
            pltpu.VMEM((512, 256), F32),
            pltpu.SemaphoreType.DMA((3,)),
            pltpu.SemaphoreType.DMA((4,)),
        ],
        input_output_aliases={2 + k: k for k in range(len(outs))},
        compiler_params=pltpu.CompilerParams(vmem_limit_bytes=16 << 20),
        cost_estimate=pl.CostEstimate(flops=4 << 20, bytes_accessed=6 << 20, transcendentals=0),
        name="finish_grads",
    )(half.reshape(1), blocks, *outs)


def sum_grads(core, operands):
    swap = [(0, 1), (1, 0)]
    other = local_grads(1 - core, *operands)
    got = lax.ppermute(other, "core", swap)
    own = local_grads(core, *operands)
    parts = lax.all_to_all(chip_sum(own, got), ("z", "yh", "yl", "x"), 0, 0, tiled=True)
    chunk = chunk_sum(parts)
    mine = lax.all_to_all(chunk, ("z", "yh", "yl", "x"), 0, 0, tiled=True)
    yours = lax.ppermute(mine, "core", swap)
    outs = finish_grads(core, mine, ())
    return finish_grads(1 - core, yours, outs)


def shards(features, blocks, block_rows, block_cols, block_count, w_in, w_mid, w_out, cotangent):
    core = lax.axis_index("core")
    z, yh = lax.axis_index("z"), lax.axis_index("yh")
    yl, x = lax.axis_index("yl"), lax.axis_index("x")
    swap = [(0, 1), (1, 0)]
    shard = halves(features, core)
    blk_own = blocks[0, 0]
    slots, _ = lax.optimization_barrier(((block_rows, block_cols, block_count), shard))
    meta = jnp.concatenate(
        [slots[0][0, 0], slots[1][0, 0], jnp.broadcast_to(slots[2][0, 0], (128,))]
    )
    meta_other = lax.ppermute(meta, "core", swap)
    blk_other = flip(blk_own, "core")

    both = jnp.stack([meta, meta_other])
    rows, cols, count = both[:, :SLOTS], both[:, SLOTS : 2 * SLOTS], both[:, 2 * SLOTS]
    live = jnp.arange(SLOTS, dtype=jnp.int32)[None, :] < count[:, None]
    cell_core = jnp.stack([core, 1 - core])[:, None]
    spare = 16 * 512
    grp = cols >> 3
    step = (((z - (grp >> 2)) & 3) * 2) + (((grp >> 1) & 1) ^ yh)
    col_at = step * 1024 + ((grp & 1) ^ core) * 512 + (cols & 7) * SIDE
    row_to = jnp.where(live, cell_core * 4096 + rows * SIDE, spare)
    fwd_off = jnp.concatenate([col_at, row_to]).reshape(4 * SLOTS)
    own8 = rows >> 3
    step = (((x - own8) & 3) * 2) + ((own8 >> 2) ^ yl)
    row_at = step * 1024 + jnp.arange(2, dtype=jnp.int32)[:, None] * 512 + (rows & 7) * SIDE
    col_to = jnp.where(live, cols * SIDE, spare)
    bwd_off = jnp.concatenate([row_at, col_to]).reshape(4 * SLOTS)

    p = jnp.arange(16, dtype=jnp.int32)
    place = (((z + (p >> 2)) & 3) * 4 + (yh ^ ((p >> 1) & 1)) * 2 + (core ^ (p & 1))) * 512
    pieces = gather_steps(shard, "z", "yh")
    cells = cell_products(False, fwd_off, count, place, blk_own, blk_other, pieces)
    cells = lax.all_to_all(cells, ("core", "yl", "x"), 0, 0, tiled=True)
    sums = jnp.sum(cells.reshape(2, 8, 512, 128).astype(F32), axis=1).astype(BF)
    aggregated = jnp.concatenate([sums[0], sums[1]], axis=1)

    joined = jnp.concatenate([features, aggregated], axis=1)
    pre_one = jnp.dot(joined, w_in, preferred_element_type=F32)
    act_one = jax.nn.silu(pre_one).astype(BF)
    pre_two = jnp.dot(act_one, w_mid, preferred_element_type=F32)
    act_two = jax.nn.silu(pre_two).astype(BF)
    updated = (
        features.astype(F32) + jnp.dot(act_two, w_out, preferred_element_type=F32)
    ).astype(BF)
    grad_pre_two = (
        jnp.dot(cotangent, w_out.T, preferred_element_type=F32) * silu_grad(pre_two)
    ).astype(BF)
    grad_pre_one = (
        jnp.dot(grad_pre_two, w_mid.T, preferred_element_type=F32) * silu_grad(pre_one)
    ).astype(BF)
    grad_joined = jnp.dot(grad_pre_one, w_in.T, preferred_element_type=F32)
    direct = cotangent.astype(F32) + grad_joined[:, :256]
    grad_agg = grad_joined[:, 256:].astype(BF)

    pieces = gather_direct(halves(grad_agg, core), "x", "yl")
    operands = (joined, act_one, cotangent, grad_pre_one, grad_pre_two, act_two)
    grad_in, grad_mid, grad_out = sum_grads(core, operands)
    back = cell_products(True, bwd_off, count, place, blk_own, blk_other, pieces)
    mine, yours = node_sum(scatter_steps(back, "z", "yh"))
    got = lax.ppermute(yours, "core", swap).astype(F32)
    first = core == 0
    relaid = jnp.concatenate(
        [jnp.where(first, mine, got), jnp.where(first, got, mine)], axis=1
    )
    grad_nodes = (direct + relaid).astype(BF)
    return updated, grad_nodes, grad_in, grad_mid, grad_out


def solution(mesh):
    fine = Mesh(mesh.devices.reshape(4, 2, 2, 2, 4), ROW + COL)
    nodes = P(ROW + COL, None)
    placed = (
        nodes,
        P(ROW, COL, None, None, None),
        P(ROW, COL, None),
        P(ROW, COL, None),
        P(ROW, COL),
        P(),
        P(),
        P(),
        nodes,
    )

    return jax.shard_map(
        shards,
        mesh=fine,
        in_specs=placed,
        out_specs=(nodes, nodes, P(), P(), P()),
        check_vma=False,
    )
```

```python
import functools

import jax
import jax.numpy as jnp
from jax import lax
from jax.experimental import pallas as pl
from jax.experimental.pallas import tpu as pltpu
from jax.sharding import Mesh, PartitionSpec as P


BF = jnp.bfloat16
F32 = jnp.float32
ROW = ("z", "yh", "core")
COL = ("yl", "x")
SLOTS = 192
SIDE = 64
CHUNK = 32
UNROLL = 32
CELL_VMEM = 28 << 20


def silu_grad(value):
    sig = jax.nn.sigmoid(value)
    return sig * (1.0 + value * (1.0 - sig))


def cells_kernel(transposed, spots, off_ref, cnt_ref, place_ref, blk0, blk1, *rest):
    pieces = rest[: len(spots)]
    out_refs = rest[len(spots) : -7]
    src, held, acc, sent, blk_sem, src_sem, out_sem = rest[-7:]
    n_chunks = SLOTS // CHUNK
    blocks = (blk0, blk1)

    def copy_of(j, ch):
        at = pl.multiple_of(ch * CHUNK, CHUNK)
        return pltpu.make_async_copy(
            blocks[j].at[pl.ds(at, CHUNK)],
            held.at[j, pl.ds(at, CHUNK)],
            blk_sem.at[j * n_chunks + ch],
        )

    moves = [
        pltpu.make_async_copy(piece, src.at[pl.ds(spot, piece.shape[0])], src_sem.at[p])
        for p, (spot, piece) in enumerate(zip(spots, pieces))
    ]
    for move in moves:
        move.start()
    used = [lax.div(cnt_ref[j] + (CHUNK - 1), CHUNK) for j in range(2)]
    for j in range(2):

        @pl.loop(0, used[j])
        def _(ch):
            copy_of(j, ch).start()

    acc[...] = jnp.zeros_like(acc)
    for move in moves:
        move.wait()
    dims = (((0,), (0,)), ((), ())) if transposed else (((1,), (0,)), ((), ()))
    for j in range(2):
        count = cnt_ref[j]

        @pl.loop(0, used[j])
        def _(ch):
            copy_of(j, ch).wait()
            left = jnp.minimum(count - ch * CHUNK, CHUNK)

            @pl.loop(0, lax.div(left + (UNROLL - 1), UNROLL))
            def _(step):
                base = ch * CHUNK + step * UNROLL
                for u in range(UNROLL):
                    slot = base + u
                    take = pl.multiple_of(off_ref[j * SLOTS + slot], SIDE)
                    put = pl.multiple_of(off_ref[(2 + j) * SLOTS + slot], SIDE)
                    term = lax.dot_general(
                        held[j, slot],
                        src[pl.ds(take, SIDE), :],
                        dims,
                        preferred_element_type=F32,
                    )
                    acc[pl.ds(put, SIDE), :] += term

    if len(out_refs) == 1:
        out_refs[0][...] = acc[: 16 * 512, :].astype(BF).reshape(out_refs[0].shape)
    else:
        moves = []
        for p, out_ref in enumerate(out_refs):
            for h in range(2):
                at = pl.multiple_of(place_ref[2 * p + h], 512)
                sent[p, h * 512 : (h + 1) * 512, :] = acc[pl.ds(at, 512), :].astype(BF)
            moves.append(pltpu.make_async_copy(sent.at[p], out_ref, out_sem.at[p]))
            moves[-1].start()
        for move in moves:
            move.wait()


def in_hbm(value):
    return pltpu.with_memory_space_constraint(value, pltpu.HBM)


def cell_products(transposed, offsets, counts, place, blk_own, blk_other, pieces):
    spots = [spot for spot, _ in pieces]
    any_spec = pl.BlockSpec(memory_space=pl.ANY)
    hbm = pl.BlockSpec(memory_space=pltpu.HBM)
    smem = pl.BlockSpec(memory_space=pltpu.SMEM)
    n_chunks = SLOTS // CHUNK
    return pl.pallas_call(
        functools.partial(cells_kernel, transposed, spots),
        out_shape=(pltpu.HBM((1024, 128), BF),) * 8
        if transposed
        else jax.ShapeDtypeStruct((16, 512, 128), BF),
        in_specs=[smem] * 3 + [hbm] * 2 + [any_spec] * len(pieces),
        out_specs=(hbm,) * 8
        if transposed
        else pl.BlockSpec(memory_space=pltpu.VMEM),
        scratch_shapes=[
            pltpu.VMEM((8192, 128), BF),
            pltpu.VMEM((2, SLOTS, SIDE, SIDE), BF),
            pltpu.VMEM((8192 + SIDE, 128), F32),
            pltpu.VMEM((8, 1024, 128) if transposed else (8, 16, 128), BF),
            pltpu.SemaphoreType.DMA((2 * n_chunks,)),
            pltpu.SemaphoreType.DMA((len(pieces),)),
            pltpu.SemaphoreType.DMA((8,)),
        ],
        compiler_params=pltpu.CompilerParams(vmem_limit_bytes=CELL_VMEM),
        cost_estimate=pl.CostEstimate(
            flops=2 * 2 * SLOTS * SIDE * SIDE * 128, bytes_accessed=10 << 20, transcendentals=0
        ),
        name="cells_back" if transposed else "cells_forward",
    )(offsets, counts, place, in_hbm(blk_own), in_hbm(blk_other), *(piece for _, piece in pieces))


def grads_kernel(half_ref, joined, act_one, cot, gp_one, gp_two, act_two, sum_ref):
    at = pl.multiple_of(half_ref[0] * 512, 512)
    sides = ((joined, gp_one, 0, 512), (act_one, gp_two, 512, 1024), (cot, act_two, 1536, 256))
    for left, right, row, size in sides:
        for part in range(0, size, 256):
            sum_ref[row + part : row + part + 256, :] = lax.dot_general(
                left[:, part : part + 256],
                right[:, pl.ds(at, 512)],
                (((0,), (0,)), ((), ())),
                preferred_element_type=F32,
            ).astype(BF)


def local_grads(half, *operands):
    vm = pl.BlockSpec(memory_space=pltpu.VMEM)
    return pl.pallas_call(
        grads_kernel,
        out_shape=jax.ShapeDtypeStruct((1792, 512), BF),
        in_specs=[pl.BlockSpec(memory_space=pltpu.SMEM)] + [vm] * 6,
        out_specs=vm,
        compiler_params=pltpu.CompilerParams(vmem_limit_bytes=16 << 20),
        cost_estimate=pl.CostEstimate(
            flops=512 * 1792 * 1024, bytes_accessed=8 << 20, transcendentals=0
        ),
    )(half.reshape(1), *operands)


def chip_kernel(own, got, out_ref, held, sems):
    moves = []
    for row in range(16):
        rows = slice(row * 112, (row + 1) * 112)
        for lane in range(4):
            lanes = slice(lane * 128, (lane + 1) * 128)
            held[row * 4 + lane] = (own[rows, lanes].astype(F32) + got[rows, lanes].astype(F32)).astype(
                BF
            )
        if row % 4 == 3:
            part = slice((row - 3) * 4, (row + 1) * 4)
            moves.append(pltpu.make_async_copy(held.at[part], out_ref.at[part], sems.at[row // 4]))
            moves[-1].start()
    for move in moves:
        move.wait()


def chip_sum(own, got):
    vm = pl.BlockSpec(memory_space=pltpu.VMEM)
    return pl.pallas_call(
        chip_kernel,
        out_shape=pltpu.HBM((64, 112, 128), BF),
        in_specs=[vm, vm],
        out_specs=pl.BlockSpec(memory_space=pltpu.HBM),
        scratch_shapes=[pltpu.VMEM((64, 112, 128), BF), pltpu.SemaphoreType.DMA((4,))],
        cost_estimate=pl.CostEstimate(flops=1 << 20, bytes_accessed=6 << 20, transcendentals=0),
        compiler_params=pltpu.CompilerParams(vmem_limit_bytes=12 << 20),
        name="chip_sum",
    )(own, got)


def chunk_kernel(parts, out_ref, taken, held, in_sem, out_sem):
    reads = [
        pltpu.make_async_copy(parts.at[8 * k : 8 * k + 8], taken.at[k], in_sem.at[k])
        for k in range(8)
    ]
    for read in reads:
        read.start()
    total = None
    for k, read in enumerate(reads):
        read.wait()
        part = jnp.sum(taken[k].astype(F32), axis=0)
        total = part if total is None else total + part
    total = total.astype(BF)
    for k in range(8):
        held[k] = total
    writes = [
        pltpu.make_async_copy(held, out_ref.at[8 * k : 8 * k + 8], out_sem.at[k])
        for k in range(8)
    ]
    for write in writes:
        write.start()
    for write in writes:
        write.wait()


def chunk_sum(parts):
    return pl.pallas_call(
        chunk_kernel,
        out_shape=pltpu.HBM((64, 112, 128), BF),
        in_specs=[pl.BlockSpec(memory_space=pl.ANY)],
        out_specs=pl.BlockSpec(memory_space=pltpu.HBM),
        scratch_shapes=[
            pltpu.VMEM((8, 8, 112, 128), BF),
            pltpu.VMEM((8, 112, 128), BF),
            pltpu.SemaphoreType.DMA((8,)),
            pltpu.SemaphoreType.DMA((8,)),
        ],
        cost_estimate=pl.CostEstimate(flops=1 << 20, bytes_accessed=3 << 20, transcendentals=0),
        compiler_params=pltpu.CompilerParams(vmem_limit_bytes=12 << 20),
        name="chunk_sum",
    )(parts)


def ring_shift(value, axis, k):
    return lax.ppermute(value, axis, [(i, (i + k) % 4) for i in range(4)])


def flip(value, axis):
    return lax.ppermute(value, axis, [(0, 1), (1, 0)])


def gather_steps(value, ring, pair):
    over = flip(value, pair)
    below = ring_shift(value, ring, 1)
    above = ring_shift(value, ring, 3)
    low = ring_shift(above[:512], ring, 3)
    high = ring_shift(below[512:], ring, 1)
    over_below = ring_shift(over, ring, 1)
    over_above = ring_shift(over, ring, 3)
    over_low = flip(low, pair)
    over_high = flip(high, pair)
    return [
        (0, value),
        (1024, over),
        (2048, below),
        (3072, over_below),
        (4096, low),
        (4608, high),
        (5120, over_low),
        (5632, over_high),
        (6144, above),
        (7168, over_above),
    ]


def gather_direct(value, ring, pair):
    got = [value] * 8
    got[1] = flip(value, pair)
    for small in range(2):
        for big in (2, 1, 3):
            p = 2 * big + small
            got[p] = ring_shift(got[small], ring, big)
    return [(1024 * p, block) for p, block in enumerate(got)]


def taken_sum(parts, taken, sems):
    reads = [pltpu.make_async_copy(part, taken.at[k], sems.at[k]) for k, part in enumerate(parts)]
    for read in reads:
        read.start()
    total = None
    for k, read in enumerate(reads):
        read.wait()
        part = taken[k].astype(F32)
        total = part if total is None else total + part
    return total


def pair_kernel(*refs):
    refs[-3][...] = taken_sum(refs[:-3], refs[-2], refs[-1]).astype(BF)


def sum_scratch(parts):
    return [
        pltpu.VMEM((len(parts), 1024, 128), BF),
        pltpu.SemaphoreType.DMA((len(parts),)),
    ]


def pair_sum(parts):
    return pl.pallas_call(
        pair_kernel,
        out_shape=jax.ShapeDtypeStruct((1024, 128), BF),
        in_specs=[pl.BlockSpec(memory_space=pl.ANY)] * len(parts),
        out_specs=pl.BlockSpec(memory_space=pltpu.VMEM),
        scratch_shapes=sum_scratch(parts),
        cost_estimate=pl.CostEstimate(flops=1 << 19, bytes_accessed=5 << 18, transcendentals=0),
        compiler_params=pltpu.CompilerParams(vmem_limit_bytes=6 << 20),
    )(in_hbm(parts[0]), *parts[1:])


def scatter_steps(pieces, ring, pair):
    cross = flip(pieces[5], pair)
    far, near = [pieces[1]], [pieces[0]]
    for small, got in ((1, far), (0, near)):
        for big in (1, 3):
            p = 2 * big + small
            got.append(ring_shift(pieces[p], ring, big))
    cross = pair_sum([pieces[4], cross])
    near.append(ring_shift(cross, ring, 2))
    far = pair_sum(far)
    return near + [flip(far, pair)]


def node_kernel(*refs):
    mine_ref, yours_ref = refs[-4:-2]
    total = taken_sum(refs[:-4], refs[-2], refs[-1])
    mine_ref[...] = total[:512]
    yours_ref[...] = total[512:].astype(BF)


def node_sum(parts):
    vm = pl.BlockSpec(memory_space=pltpu.VMEM)
    return pl.pallas_call(
        node_kernel,
        out_shape=(
            jax.ShapeDtypeStruct((512, 128), F32),
            jax.ShapeDtypeStruct((512, 128), BF),
        ),
        in_specs=[pl.BlockSpec(memory_space=pl.ANY)] * len(parts),
        out_specs=(vm, vm),
        scratch_shapes=sum_scratch(parts),
        cost_estimate=pl.CostEstimate(flops=1 << 20, bytes_accessed=3 << 20, transcendentals=0),
        compiler_params=pltpu.CompilerParams(vmem_limit_bytes=8 << 20),
        name="node_sum",
    )(in_hbm(parts[0]), *parts[1:])


def halves(value, core):
    left, right = value[:, :128], value[:, 128:]
    first = core == 0
    mine = jnp.where(first, left, right)
    yours = jnp.where(first, right, left)
    got = flip(yours, "core")
    return jnp.concatenate([mine, got], axis=0)


def finish_kernel(half_ref, blocks_ref, *rest):
    outs, taken, total, turned, sems, in_sem = rest[-8:-5], *rest[-5:]
    reads = [
        pltpu.make_async_copy(blocks_ref.at[16 * k : 16 * k + 16], taken.at[k], in_sem.at[k])
        for k in range(4)
    ]
    for read in reads:
        read.start()
    lane = pl.multiple_of(half_ref[0] * 512, 512)
    lanes = pl.ds(lane, 512)
    moves = (
        pltpu.make_async_copy(total.at[:512], outs[0].at[:, lanes], sems.at[0]),
        pltpu.make_async_copy(total.at[512:1536], outs[1].at[:, lanes], sems.at[1]),
        pltpu.make_async_copy(turned, outs[2].at[lanes, :], sems.at[2]),
    )
    for row in range(16):
        if row % 4 == 0:
            reads[row // 4].wait()
        for col in range(4):
            total[row * 112 : (row + 1) * 112, col * 128 : (col + 1) * 128] = taken[
                row // 4, (row % 4) * 4 + col
            ].astype(F32) * (1.0 / 256.0)
        if row == 4:
            moves[0].start()
        if row == 13:
            moves[1].start()
    turned[...] = total[1536:, :].T
    moves[2].start()
    for move in moves:
        move.wait()


def finish_grads(half, blocks, outs):
    any_spec = pl.BlockSpec(memory_space=pl.ANY)
    return pl.pallas_call(
        finish_kernel,
        out_shape=(
            jax.ShapeDtypeStruct((512, 1024), F32),
            jax.ShapeDtypeStruct((1024, 1024), F32),
            jax.ShapeDtypeStruct((1024, 256), F32),
        ),
        in_specs=[pl.BlockSpec(memory_space=pltpu.SMEM)] + [any_spec] * (1 + len(outs)),
        out_specs=(any_spec,) * 3,
        scratch_shapes=[
            pltpu.VMEM((4, 16, 112, 128), BF),
            pltpu.VMEM((1792, 512), F32),
            pltpu.VMEM((512, 256), F32),
            pltpu.SemaphoreType.DMA((3,)),
            pltpu.SemaphoreType.DMA((4,)),
        ],
        input_output_aliases={2 + k: k for k in range(len(outs))},
        compiler_params=pltpu.CompilerParams(vmem_limit_bytes=16 << 20),
        cost_estimate=pl.CostEstimate(flops=4 << 20, bytes_accessed=6 << 20, transcendentals=0),
        name="finish_grads",
    )(half.reshape(1), blocks, *outs)


def sum_grads(core, operands):
    swap = [(0, 1), (1, 0)]
    other = local_grads(1 - core, *operands)
    got = lax.ppermute(other, "core", swap)
    own = local_grads(core, *operands)
    parts = lax.all_to_all(chip_sum(own, got), ("z", "yh", "yl", "x"), 0, 0, tiled=True)
    chunk = chunk_sum(parts)
    mine = lax.all_to_all(chunk, ("z", "yh", "yl", "x"), 0, 0, tiled=True)
    yours = lax.ppermute(mine, "core", swap)
    outs = finish_grads(core, mine, ())
    return finish_grads(1 - core, yours, outs)


def shards(features, blocks, block_rows, block_cols, block_count, w_in, w_mid, w_out, cotangent):
    core = lax.axis_index("core")
    z, yh = lax.axis_index("z"), lax.axis_index("yh")
    yl, x = lax.axis_index("yl"), lax.axis_index("x")
    swap = [(0, 1), (1, 0)]
    shard = halves(features, core)
    blk_own = blocks[0, 0]
    slots, _ = lax.optimization_barrier(((block_rows, block_cols, block_count), shard))
    meta = jnp.concatenate(
        [slots[0][0, 0], slots[1][0, 0], jnp.broadcast_to(slots[2][0, 0], (128,))]
    )
    meta_other = lax.ppermute(meta, "core", swap)
    blk_other = flip(blk_own, "core")

    both = jnp.stack([meta, meta_other])
    rows, cols, count = both[:, :SLOTS], both[:, SLOTS : 2 * SLOTS], both[:, 2 * SLOTS]
    live = jnp.arange(SLOTS, dtype=jnp.int32)[None, :] < count[:, None]
    cell_core = jnp.stack([core, 1 - core])[:, None]
    spare = 16 * 512
    grp = cols >> 3
    step = (((z - (grp >> 2)) & 3) * 2) + (((grp >> 1) & 1) ^ yh)
    col_at = step * 1024 + ((grp & 1) ^ core) * 512 + (cols & 7) * SIDE
    row_to = jnp.where(live, cell_core * 4096 + rows * SIDE, spare)
    fwd_off = jnp.concatenate([col_at, row_to]).reshape(4 * SLOTS)
    own8 = rows >> 3
    step = (((x - own8) & 3) * 2) + ((own8 >> 2) ^ yl)
    row_at = step * 1024 + jnp.arange(2, dtype=jnp.int32)[:, None] * 512 + (rows & 7) * SIDE
    col_to = jnp.where(live, cols * SIDE, spare)
    bwd_off = jnp.concatenate([row_at, col_to]).reshape(4 * SLOTS)

    p = jnp.arange(16, dtype=jnp.int32)
    place = (((z + (p >> 2)) & 3) * 4 + (yh ^ ((p >> 1) & 1)) * 2 + (core ^ (p & 1))) * 512
    pieces = gather_steps(shard, "z", "yh")
    cells = cell_products(False, fwd_off, count, place, blk_own, blk_other, pieces)
    cells = lax.all_to_all(cells, ("core", "yl", "x"), 0, 0, tiled=True)
    sums = jnp.sum(cells.reshape(2, 8, 512, 128).astype(F32), axis=1).astype(BF)
    aggregated = jnp.concatenate([sums[0], sums[1]], axis=1)

    joined = jnp.concatenate([features, aggregated], axis=1)
    pre_one = jnp.dot(joined, w_in, preferred_element_type=F32)
    act_one = jax.nn.silu(pre_one).astype(BF)
    pre_two = jnp.dot(act_one, w_mid, preferred_element_type=F32)
    act_two = jax.nn.silu(pre_two).astype(BF)
    updated = (
        features.astype(F32) + jnp.dot(act_two, w_out, preferred_element_type=F32)
    ).astype(BF)
    grad_pre_two = (
        jnp.dot(cotangent, w_out.T, preferred_element_type=F32) * silu_grad(pre_two)
    ).astype(BF)
    grad_pre_one = (
        jnp.dot(grad_pre_two, w_mid.T, preferred_element_type=F32) * silu_grad(pre_one)
    ).astype(BF)
    grad_joined = jnp.dot(grad_pre_one, w_in.T, preferred_element_type=F32)
    direct = cotangent.astype(F32) + grad_joined[:, :256]
    grad_agg = grad_joined[:, 256:].astype(BF)

    pieces = gather_direct(halves(grad_agg, core), "x", "yl")
    operands = (joined, act_one, cotangent, grad_pre_one, grad_pre_two, act_two)
    grad_in, grad_mid, grad_out = sum_grads(core, operands)
    back = cell_products(True, bwd_off, count, place, blk_own, blk_other, pieces)
    mine, yours = node_sum(scatter_steps(back, "z", "yh"))
    got = lax.ppermute(yours, "core", swap).astype(F32)
    first = core == 0
    relaid = jnp.concatenate(
        [jnp.where(first, mine, got), jnp.where(first, got, mine)], axis=1
    )
    grad_nodes = (direct + relaid).astype(BF)
    return updated, grad_nodes, grad_in, grad_mid, grad_out


def solution(mesh):
    fine = Mesh(mesh.devices.reshape(4, 2, 2, 2, 4), ROW + COL)
    nodes = P(ROW + COL, None)
    placed = (
        nodes,
        P(ROW, COL, None, None, None),
        P(ROW, COL, None),
        P(ROW, COL, None),
        P(ROW, COL),
        P(),
        P(),
        P(),
        nodes,
    )

    return jax.shard_map(
        shards,
        mesh=fine,
        in_specs=placed,
        out_specs=(nodes, nodes, P(), P(), P()),
        check_vma=False,
    )
```

```python
import functools

import jax
import jax.numpy as jnp
from jax import lax
from jax.experimental import pallas as pl
from jax.experimental.pallas import tpu as pltpu
from jax.sharding import Mesh, PartitionSpec as P


BF = jnp.bfloat16
F32 = jnp.float32
ROW = ("z", "yh", "core")
COL = ("yl", "x")
SLOTS = 192
SIDE = 64
CHUNK = 32
UNROLL = 32
CELL_VMEM = 28 << 20


def silu_grad(value):
    sig = jax.nn.sigmoid(value)
    return sig * (1.0 + value * (1.0 - sig))


def cells_kernel(transposed, spots, off_ref, cnt_ref, place_ref, blk0, blk1, *rest):
    pieces = rest[: len(spots)]
    out_refs = rest[len(spots) : -7]
    src, held, acc, sent, blk_sem, src_sem, out_sem = rest[-7:]
    n_chunks = SLOTS // CHUNK
    blocks = (blk0, blk1)

    def copy_of(j, ch):
        at = pl.multiple_of(ch * CHUNK, CHUNK)
        return pltpu.make_async_copy(
            blocks[j].at[pl.ds(at, CHUNK)],
            held.at[j, pl.ds(at, CHUNK)],
            blk_sem.at[j * n_chunks + ch],
        )

    moves = [
        pltpu.make_async_copy(piece, src.at[pl.ds(spot, piece.shape[0])], src_sem.at[p])
        for p, (spot, piece) in enumerate(zip(spots, pieces))
    ]
    for move in moves:
        move.start()
    used = [lax.div(cnt_ref[j] + (CHUNK - 1), CHUNK) for j in range(2)]
    for j in range(2):

        @pl.loop(0, used[j])
        def _(ch):
            copy_of(j, ch).start()

    acc[...] = jnp.zeros_like(acc)
    for move in moves:
        move.wait()
    dims = (((0,), (0,)), ((), ())) if transposed else (((1,), (0,)), ((), ()))
    for j in range(2):
        count = cnt_ref[j]

        @pl.loop(0, used[j])
        def _(ch):
            copy_of(j, ch).wait()
            left = jnp.minimum(count - ch * CHUNK, CHUNK)

            @pl.loop(0, lax.div(left + (UNROLL - 1), UNROLL))
            def _(step):
                base = ch * CHUNK + step * UNROLL
                for u in range(UNROLL):
                    slot = base + u
                    take = pl.multiple_of(off_ref[j * SLOTS + slot], SIDE)
                    put = pl.multiple_of(off_ref[(2 + j) * SLOTS + slot], SIDE)
                    term = lax.dot_general(
                        held[j, slot],
                        src[pl.ds(take, SIDE), :],
                        dims,
                        preferred_element_type=F32,
                    )
                    acc[pl.ds(put, SIDE), :] += term

    if len(out_refs) == 1:
        out_refs[0][...] = acc[: 16 * 512, :].astype(BF).reshape(out_refs[0].shape)
    else:
        moves = []
        for p, out_ref in enumerate(out_refs):
            for h in range(2):
                at = pl.multiple_of(place_ref[2 * p + h], 512)
                sent[p, h * 512 : (h + 1) * 512, :] = acc[pl.ds(at, 512), :].astype(BF)
            moves.append(pltpu.make_async_copy(sent.at[p], out_ref, out_sem.at[p]))
            moves[-1].start()
        for move in moves:
            move.wait()


def in_hbm(value):
    return pltpu.with_memory_space_constraint(value, pltpu.HBM)


def cell_products(transposed, offsets, counts, place, blk_own, blk_other, pieces):
    spots = [spot for spot, _ in pieces]
    any_spec = pl.BlockSpec(memory_space=pl.ANY)
    hbm = pl.BlockSpec(memory_space=pltpu.HBM)
    smem = pl.BlockSpec(memory_space=pltpu.SMEM)
    n_chunks = SLOTS // CHUNK
    return pl.pallas_call(
        functools.partial(cells_kernel, transposed, spots),
        out_shape=(pltpu.HBM((1024, 128), BF),) * 8
        if transposed
        else jax.ShapeDtypeStruct((16, 512, 128), BF),
        in_specs=[smem] * 3 + [hbm] * 2 + [any_spec] * len(pieces),
        out_specs=(hbm,) * 8
        if transposed
        else pl.BlockSpec(memory_space=pltpu.VMEM),
        scratch_shapes=[
            pltpu.VMEM((8192, 128), BF),
            pltpu.VMEM((2, SLOTS, SIDE, SIDE), BF),
            pltpu.VMEM((8192 + SIDE, 128), F32),
            pltpu.VMEM((8, 1024, 128) if transposed else (8, 16, 128), BF),
            pltpu.SemaphoreType.DMA((2 * n_chunks,)),
            pltpu.SemaphoreType.DMA((len(pieces),)),
            pltpu.SemaphoreType.DMA((8,)),
        ],
        compiler_params=pltpu.CompilerParams(vmem_limit_bytes=CELL_VMEM),
        cost_estimate=pl.CostEstimate(
            flops=2 * 2 * SLOTS * SIDE * SIDE * 128, bytes_accessed=10 << 20, transcendentals=0
        ),
        name="cells_back" if transposed else "cells_forward",
    )(offsets, counts, place, in_hbm(blk_own), in_hbm(blk_other), *(piece for _, piece in pieces))


def grads_kernel(half_ref, joined, act_one, cot, gp_one, gp_two, act_two, sum_ref):
    at = pl.multiple_of(half_ref[0] * 512, 512)
    sides = ((joined, gp_one, 0, 512), (act_one, gp_two, 512, 1024), (cot, act_two, 1536, 256))
    for left, right, row, size in sides:
        for part in range(0, size, 256):
            sum_ref[row + part : row + part + 256, :] = lax.dot_general(
                left[:, part : part + 256],
                right[:, pl.ds(at, 512)],
                (((0,), (0,)), ((), ())),
                preferred_element_type=F32,
            ).astype(BF)


def local_grads(half, *operands):
    vm = pl.BlockSpec(memory_space=pltpu.VMEM)
    return pl.pallas_call(
        grads_kernel,
        out_shape=jax.ShapeDtypeStruct((1792, 512), BF),
        in_specs=[pl.BlockSpec(memory_space=pltpu.SMEM)] + [vm] * 6,
        out_specs=vm,
        compiler_params=pltpu.CompilerParams(vmem_limit_bytes=16 << 20),
        cost_estimate=pl.CostEstimate(
            flops=512 * 1792 * 1024, bytes_accessed=8 << 20, transcendentals=0
        ),
    )(half.reshape(1), *operands)


def chip_kernel(own, got, out_ref, held, sems):
    moves = []
    for row in range(16):
        rows = slice(row * 112, (row + 1) * 112)
        for lane in range(4):
            lanes = slice(lane * 128, (lane + 1) * 128)
            held[row * 4 + lane] = (own[rows, lanes].astype(F32) + got[rows, lanes].astype(F32)).astype(
                BF
            )
        if row % 4 == 3:
            part = slice((row - 3) * 4, (row + 1) * 4)
            moves.append(pltpu.make_async_copy(held.at[part], out_ref.at[part], sems.at[row // 4]))
            moves[-1].start()
    for move in moves:
        move.wait()


def chip_sum(own, got):
    vm = pl.BlockSpec(memory_space=pltpu.VMEM)
    return pl.pallas_call(
        chip_kernel,
        out_shape=pltpu.HBM((64, 112, 128), BF),
        in_specs=[vm, vm],
        out_specs=pl.BlockSpec(memory_space=pltpu.HBM),
        scratch_shapes=[pltpu.VMEM((64, 112, 128), BF), pltpu.SemaphoreType.DMA((4,))],
        cost_estimate=pl.CostEstimate(flops=1 << 20, bytes_accessed=6 << 20, transcendentals=0),
        compiler_params=pltpu.CompilerParams(vmem_limit_bytes=12 << 20),
        name="chip_sum",
    )(own, got)


def chunk_kernel(parts, out_ref, taken, held, in_sem, out_sem):
    reads = [
        pltpu.make_async_copy(parts.at[8 * k : 8 * k + 8], taken.at[k], in_sem.at[k])
        for k in range(8)
    ]
    for read in reads:
        read.start()
    total = None
    for k, read in enumerate(reads):
        read.wait()
        part = jnp.sum(taken[k].astype(F32), axis=0)
        total = part if total is None else total + part
    total = total.astype(BF)
    for k in range(8):
        held[k] = total
    writes = [
        pltpu.make_async_copy(held, out_ref.at[8 * k : 8 * k + 8], out_sem.at[k])
        for k in range(8)
    ]
    for write in writes:
        write.start()
    for write in writes:
        write.wait()


def chunk_sum(parts):
    return pl.pallas_call(
        chunk_kernel,
        out_shape=pltpu.HBM((64, 112, 128), BF),
        in_specs=[pl.BlockSpec(memory_space=pl.ANY)],
        out_specs=pl.BlockSpec(memory_space=pltpu.HBM),
        scratch_shapes=[
            pltpu.VMEM((8, 8, 112, 128), BF),
            pltpu.VMEM((8, 112, 128), BF),
            pltpu.SemaphoreType.DMA((8,)),
            pltpu.SemaphoreType.DMA((8,)),
        ],
        cost_estimate=pl.CostEstimate(flops=1 << 20, bytes_accessed=3 << 20, transcendentals=0),
        compiler_params=pltpu.CompilerParams(vmem_limit_bytes=12 << 20),
        name="chunk_sum",
    )(parts)


def ring_shift(value, axis, k):
    return lax.ppermute(value, axis, [(i, (i + k) % 4) for i in range(4)])


def flip(value, axis):
    return lax.ppermute(value, axis, [(0, 1), (1, 0)])


def gather_steps(value, ring, pair):
    over = flip(value, pair)
    below = ring_shift(value, ring, 1)
    above = ring_shift(value, ring, 3)
    low = ring_shift(above[:512], ring, 3)
    high = ring_shift(below[512:], ring, 1)
    over_below = ring_shift(over, ring, 1)
    over_above = ring_shift(over, ring, 3)
    over_low = flip(low, pair)
    over_high = flip(high, pair)
    return [
        (0, value),
        (1024, over),
        (2048, below),
        (3072, over_below),
        (4096, low),
        (4608, high),
        (5120, over_low),
        (5632, over_high),
        (6144, above),
        (7168, over_above),
    ]


def gather_direct(value, ring, pair):
    got = [value] * 8
    got[1] = flip(value, pair)
    for small in range(2):
        for big in (2, 1, 3):
            p = 2 * big + small
            got[p] = ring_shift(got[small], ring, big)
    return [(1024 * p, block) for p, block in enumerate(got)]


def taken_sum(parts, taken, sems):
    reads = [pltpu.make_async_copy(part, taken.at[k], sems.at[k]) for k, part in enumerate(parts)]
    for read in reads:
        read.start()
    total = None
    for k, read in enumerate(reads):
        read.wait()
        part = taken[k].astype(F32)
        total = part if total is None else total + part
    return total


def pair_kernel(*refs):
    refs[-3][...] = taken_sum(refs[:-3], refs[-2], refs[-1]).astype(BF)


def sum_scratch(parts):
    return [
        pltpu.VMEM((len(parts), 1024, 128), BF),
        pltpu.SemaphoreType.DMA((len(parts),)),
    ]


def pair_sum(parts):
    return pl.pallas_call(
        pair_kernel,
        out_shape=jax.ShapeDtypeStruct((1024, 128), BF),
        in_specs=[pl.BlockSpec(memory_space=pl.ANY)] * len(parts),
        out_specs=pl.BlockSpec(memory_space=pltpu.VMEM),
        scratch_shapes=sum_scratch(parts),
        cost_estimate=pl.CostEstimate(flops=1 << 19, bytes_accessed=5 << 18, transcendentals=0),
        compiler_params=pltpu.CompilerParams(vmem_limit_bytes=6 << 20),
    )(in_hbm(parts[0]), *parts[1:])


def scatter_steps(pieces, ring, pair):
    cross = flip(pieces[5], pair)
    far, near = [pieces[1]], [pieces[0]]
    for small, got in ((1, far), (0, near)):
        for big in (1, 3):
            p = 2 * big + small
            got.append(ring_shift(pieces[p], ring, big))
    cross = pair_sum([pieces[4], cross])
    near.append(ring_shift(cross, ring, 2))
    far = pair_sum(far)
    return near + [flip(far, pair)]


def node_kernel(*refs):
    mine_ref, yours_ref = refs[-4:-2]
    total = taken_sum(refs[:-4], refs[-2], refs[-1])
    mine_ref[...] = total[:512]
    yours_ref[...] = total[512:].astype(BF)


def node_sum(parts):
    vm = pl.BlockSpec(memory_space=pltpu.VMEM)
    return pl.pallas_call(
        node_kernel,
        out_shape=(
            jax.ShapeDtypeStruct((512, 128), F32),
            jax.ShapeDtypeStruct((512, 128), BF),
        ),
        in_specs=[pl.BlockSpec(memory_space=pl.ANY)] * len(parts),
        out_specs=(vm, vm),
        scratch_shapes=sum_scratch(parts),
        cost_estimate=pl.CostEstimate(flops=1 << 20, bytes_accessed=3 << 20, transcendentals=0),
        compiler_params=pltpu.CompilerParams(vmem_limit_bytes=8 << 20),
        name="node_sum",
    )(in_hbm(parts[0]), *parts[1:])


def halves(value, core):
    left, right = value[:, :128], value[:, 128:]
    first = core == 0
    mine = jnp.where(first, left, right)
    yours = jnp.where(first, right, left)
    got = flip(yours, "core")
    return jnp.concatenate([mine, got], axis=0)


def finish_kernel(near, half_ref, blocks_ref, *rest):
    outs, taken, total, turned, sems, in_sem = rest[-8:-5], *rest[-5:]
    reads = [] if near else [
        pltpu.make_async_copy(blocks_ref.at[16 * k : 16 * k + 16], taken.at[k], in_sem.at[k])
        for k in range(4)
    ]
    for read in reads:
        read.start()
    lane = pl.multiple_of(half_ref[0] * 512, 512)
    lanes = pl.ds(lane, 512)
    moves = (
        pltpu.make_async_copy(total.at[:512], outs[0].at[:, lanes], sems.at[0]),
        pltpu.make_async_copy(total.at[512:1536], outs[1].at[:, lanes], sems.at[1]),
        pltpu.make_async_copy(turned, outs[2].at[lanes, :], sems.at[2]),
    )
    for row in range(16):
        if row % 4 == 0 and not near:
            reads[row // 4].wait()
        for col in range(4):
            block = (
                blocks_ref[row * 4 + col] if near else taken[row // 4, (row % 4) * 4 + col]
            )
            total[row * 112 : (row + 1) * 112, col * 128 : (col + 1) * 128] = block.astype(
                F32
            ) * (1.0 / 256.0)
        if row == 4:
            moves[0].start()
        if row == 13:
            moves[1].start()
    turned[...] = total[1536:, :].T
    moves[2].start()
    for move in moves:
        move.wait()


def finish_grads(half, blocks, outs, near):
    any_spec = pl.BlockSpec(memory_space=pl.ANY)
    own_spec = pl.BlockSpec(memory_space=pltpu.VMEM) if near else any_spec
    return pl.pallas_call(
        functools.partial(finish_kernel, near),
        out_shape=(
            jax.ShapeDtypeStruct((512, 1024), F32),
            jax.ShapeDtypeStruct((1024, 1024), F32),
            jax.ShapeDtypeStruct((1024, 256), F32),
        ),
        in_specs=[pl.BlockSpec(memory_space=pltpu.SMEM), own_spec] + [any_spec] * len(outs),
        out_specs=(any_spec,) * 3,
        scratch_shapes=[
            pltpu.VMEM((1, 16, 16, 128) if near else (4, 16, 112, 128), BF),
            pltpu.VMEM((1792, 512), F32),
            pltpu.VMEM((512, 256), F32),
            pltpu.SemaphoreType.DMA((3,)),
            pltpu.SemaphoreType.DMA((4,)),
        ],
        input_output_aliases={2 + k: k for k in range(len(outs))},
        compiler_params=pltpu.CompilerParams(vmem_limit_bytes=16 << 20),
        cost_estimate=pl.CostEstimate(flops=4 << 20, bytes_accessed=6 << 20, transcendentals=0),
        name="finish_grads",
    )(half.reshape(1), blocks, *outs)


def sum_grads(core, operands):
    swap = [(0, 1), (1, 0)]
    other = local_grads(1 - core, *operands)
    got = lax.ppermute(other, "core", swap)
    own = local_grads(core, *operands)
    parts = lax.all_to_all(chip_sum(own, got), ("z", "yh", "yl", "x"), 0, 0, tiled=True)
    chunk = chunk_sum(parts)
    mine = lax.all_to_all(chunk, ("z", "yh", "yl", "x"), 0, 0, tiled=True)
    yours = lax.ppermute(mine, "core", swap)
    outs = finish_grads(core, mine, (), False)
    return finish_grads(1 - core, yours, outs, True)


def shards(features, blocks, block_rows, block_cols, block_count, w_in, w_mid, w_out, cotangent):
    core = lax.axis_index("core")
    z, yh = lax.axis_index("z"), lax.axis_index("yh")
    yl, x = lax.axis_index("yl"), lax.axis_index("x")
    swap = [(0, 1), (1, 0)]
    shard = halves(features, core)
    blk_own = blocks[0, 0]
    slots, _ = lax.optimization_barrier(((block_rows, block_cols, block_count), shard))
    meta = jnp.concatenate(
        [slots[0][0, 0], slots[1][0, 0], jnp.broadcast_to(slots[2][0, 0], (128,))]
    )
    meta_other = lax.ppermute(meta, "core", swap)
    blk_other = flip(blk_own, "core")

    both = jnp.stack([meta, meta_other])
    rows, cols, count = both[:, :SLOTS], both[:, SLOTS : 2 * SLOTS], both[:, 2 * SLOTS]
    live = jnp.arange(SLOTS, dtype=jnp.int32)[None, :] < count[:, None]
    cell_core = jnp.stack([core, 1 - core])[:, None]
    spare = 16 * 512
    grp = cols >> 3
    step = (((z - (grp >> 2)) & 3) * 2) + (((grp >> 1) & 1) ^ yh)
    col_at = step * 1024 + ((grp & 1) ^ core) * 512 + (cols & 7) * SIDE
    row_to = jnp.where(live, cell_core * 4096 + rows * SIDE, spare)
    fwd_off = jnp.concatenate([col_at, row_to]).reshape(4 * SLOTS)
    own8 = rows >> 3
    step = (((x - own8) & 3) * 2) + ((own8 >> 2) ^ yl)
    row_at = step * 1024 + jnp.arange(2, dtype=jnp.int32)[:, None] * 512 + (rows & 7) * SIDE
    col_to = jnp.where(live, cols * SIDE, spare)
    bwd_off = jnp.concatenate([row_at, col_to]).reshape(4 * SLOTS)

    p = jnp.arange(16, dtype=jnp.int32)
    place = (((z + (p >> 2)) & 3) * 4 + (yh ^ ((p >> 1) & 1)) * 2 + (core ^ (p & 1))) * 512
    pieces = gather_steps(shard, "z", "yh")
    cells = cell_products(False, fwd_off, count, place, blk_own, blk_other, pieces)
    cells = lax.all_to_all(cells, ("core", "yl", "x"), 0, 0, tiled=True)
    sums = jnp.sum(cells.reshape(2, 8, 512, 128).astype(F32), axis=1).astype(BF)
    aggregated = jnp.concatenate([sums[0], sums[1]], axis=1)

    joined = jnp.concatenate([features, aggregated], axis=1)
    pre_one = jnp.dot(joined, w_in, preferred_element_type=F32)
    act_one = jax.nn.silu(pre_one).astype(BF)
    pre_two = jnp.dot(act_one, w_mid, preferred_element_type=F32)
    act_two = jax.nn.silu(pre_two).astype(BF)
    updated = (
        features.astype(F32) + jnp.dot(act_two, w_out, preferred_element_type=F32)
    ).astype(BF)
    grad_pre_two = (
        jnp.dot(cotangent, w_out.T, preferred_element_type=F32) * silu_grad(pre_two)
    ).astype(BF)
    grad_pre_one = (
        jnp.dot(grad_pre_two, w_mid.T, preferred_element_type=F32) * silu_grad(pre_one)
    ).astype(BF)
    grad_joined = jnp.dot(grad_pre_one, w_in.T, preferred_element_type=F32)
    direct = cotangent.astype(F32) + grad_joined[:, :256]
    grad_agg = grad_joined[:, 256:].astype(BF)

    pieces = gather_direct(halves(grad_agg, core), "x", "yl")
    operands = (joined, act_one, cotangent, grad_pre_one, grad_pre_two, act_two)
    grad_in, grad_mid, grad_out = sum_grads(core, operands)
    back = cell_products(True, bwd_off, count, place, blk_own, blk_other, pieces)
    mine, yours = node_sum(scatter_steps(back, "z", "yh"))
    got = lax.ppermute(yours, "core", swap).astype(F32)
    first = core == 0
    relaid = jnp.concatenate(
        [jnp.where(first, mine, got), jnp.where(first, got, mine)], axis=1
    )
    grad_nodes = (direct + relaid).astype(BF)
    return updated, grad_nodes, grad_in, grad_mid, grad_out


def solution(mesh):
    fine = Mesh(mesh.devices.reshape(4, 2, 2, 2, 4), ROW + COL)
    nodes = P(ROW + COL, None)
    placed = (
        nodes,
        P(ROW, COL, None, None, None),
        P(ROW, COL, None),
        P(ROW, COL, None),
        P(ROW, COL),
        P(),
        P(),
        P(),
        nodes,
    )

    return jax.shard_map(
        shards,
        mesh=fine,
        in_specs=placed,
        out_specs=(nodes, nodes, P(), P(), P()),
        check_vma=False,
    )
```
